256 devices in a mesh: seq: 32 (over z_hi, x, core), uly: 8 (over y, z_lo).
Axes of the slice: x: 4, y: 4, z: 8 (z_hi: 4, z_lo: 2; z = z_hi * 2 + z_lo), core: 2. Of those that a mesh axis runs over, the one named last changes fastest.
Arguments:
- normed: bfloat16 [32768, 5376], P('seq', 'uly'), may hold values from -6 to 6
- q_raw: bfloat16 [32768, 2048], P('seq', 'uly'), may hold values from -6 to 6
- key_weight: bfloat16 [5376, 1024], P('uly', 'seq'), may hold values from -0.078125 to 0.078125
- value_weight: bfloat16 [5376, 1024], P('uly', 'seq'), may hold values from -0.078125 to 0.078125
- q_gain: float32 [128], replicated, may hold values from 0.1 to 1.9
- k_gain: float32 [128], replicated, may hold values from 0.1 to 1.9
- segment_ids: int32 [32768], replicated, may hold values from 0 to 1, as said below
- grad_out: bfloat16 [32768, 2048], P('seq', 'uly'), may hold values from -6 to 6
Outputs:
- attention: bfloat16 [32768, 2048], P('seq', 'uly')
- grad_normed: bfloat16 [32768, 5376], P('seq', 'uly')
- grad_q: bfloat16 [32768, 2048], P('seq', 'uly')
- grad_key_weight: float32 [5376, 1024], P('uly', 'seq')
- grad_value_weight: float32 [5376, 1024], P('uly', 'seq')
The draws below stay inside these ranges and needn't reach their ends.
Inputs may be any that keep to these rules, and one draw needn't show every extreme that they name: `segment_ids`: 0 up to one position and 1 from it on; that position lies between 8192 and 24576.
All inputs are finite; a program needn't handle non-finite values.
Results may differ from the reference program's by a relative error of at most 0.025.
Values may be sent and summed in bfloat16 or wider, within the bound.
A program may use at most 128 MiB of HBM per device.

```python
import jax
import jax.numpy as jnp
from jax import lax

D = 5376
HD = 128
HK = 8
WINDOW = 1024
HQ = 16
SPAN = 1024
TOKENS = 32768
N_SEQ = 32
N_ULY = 8


def draw_segment_ids(key, part):
    boundary = jax.random.randint(key, (), TOKENS // 4, 3 * TOKENS // 4 + 1)
    return (jnp.arange(TOKENS) >= boundary).astype(jnp.int32)


def block_levels(stream_key, extent, cuts, low, high):
    level = 1.0
    for dim, shards_of in cuts:
        heights = jax.random.uniform(jax.random.fold_in(jax.random.fold_in(stream_key, 6), dim), (shards_of,), jnp.float32, low / len(cuts), high / len(cuts))
        level = level * jnp.repeat(jnp.exp(heights), extent[dim] // shards_of).reshape((-1,) + (1,) * (len(extent) - 1 - dim))
    return level


def gaussian(own_key, extent, scale, most, split=(), kind=jnp.bfloat16):
    level = block_levels(own_key, extent, split, -0.22, 0.18) if split else 1.0
    result = jax.random.normal(own_key, extent, jnp.float32) * scale * level
    return jnp.minimum(jnp.maximum(result, -most), most).astype(kind)


def setup_inputs(seed: int = 0) -> dict:
    key_of = jax.random.split(jax.random.key(seed), 9)
    return {
        "normed": gaussian(key_of[0], (TOKENS, D), 1.0, 6.0, ((0, 32), (1, 8))),
        "q_raw": gaussian(key_of[1], (TOKENS, HQ * HD), 1.0, 6.0, ((0, 32), (1, 8))),
        "key_weight": gaussian(key_of[2], (D, HK * HD), D ** -0.5, 0.078125, ((0, 8), (1, 32))),
        "value_weight": gaussian(key_of[3], (D, HK * HD), D ** -0.5, 0.078125, ((0, 8), (1, 32))),
        "q_gain": jnp.clip(1.0 + 0.18 * jax.random.normal(key_of[4], (HD,), jnp.float32), 0.1, 1.9),
        "k_gain": jnp.clip(1.0 + 0.18 * jax.random.normal(key_of[5], (HD,), jnp.float32), 0.1, 1.9),
        "segment_ids": draw_segment_ids(jax.random.fold_in(key_of[8], 71), 0),
        "grad_out": gaussian(key_of[7], (TOKENS, HQ * HD), 1.0, 6.0, ((0, 32), (1, 8))),
    }


epsilon = 1e-06
query_scale = 168.0 ** (-0.5)

def normalize(raw_vals, gain, factor):
    mean_sq = lax.optimization_barrier(jnp.mean(raw_vals * raw_vals, axis=-1, keepdims=True))
    return raw_vals * lax.rsqrt(mean_sq + epsilon) * gain * factor

def attend_block(queries, key_block, value_block, grad_block, query_pos, key_pos, query_seg, key_seg):
    query_f = queries.astype(jnp.float32)
    key_f = key_block.astype(jnp.float32)
    value_f = value_block.astype(jnp.float32)
    grad_f = grad_block.astype(jnp.float32)
    scores = jnp.einsum('bhge,lhe->hgbl', query_f, key_f)
    allowed = (key_pos[None, :] <= query_pos[:, None]) & (key_pos[None, :] > query_pos[:, None] - WINDOW) & (key_seg[None, :] == query_seg[:, None])
    exp_scores = jnp.where(allowed[None, None], jnp.exp(scores), 0.0)
    probs = exp_scores / lax.optimization_barrier(jnp.sum(exp_scores, axis=-1, keepdims=True))
    weights = probs.astype(jnp.bfloat16)
    weight_f = weights.astype(jnp.float32)
    attended = jnp.einsum('hgbl,lhe->bhge', weight_f, value_f).astype(jnp.bfloat16)
    dprob = jnp.einsum('bhge,lhe->hgbl', grad_f, value_f)
    delta_row = lax.optimization_barrier(jnp.sum(probs * dprob, axis=-1, keepdims=True))
    dscore = (probs * (dprob - delta_row)).astype(jnp.bfloat16)
    dscore_f = dscore.astype(jnp.float32)
    dquery = jnp.einsum('hgbl,lhe->bhge', dscore_f, key_f)
    dkey = jnp.einsum('hgbl,bhge->lhe', dscore_f, query_f)
    dvalue = jnp.einsum('hgbl,bhge->lhe', weight_f, grad_f)
    return (attended, dquery, dkey, dvalue)

def reference(normed, q_raw, key_weight, value_weight, q_gain, k_gain, segment_ids, grad_out):
    feature_rows = D // N_ULY
    key_raw = jnp.zeros((TOKENS, HK * HD), jnp.float32)
    value_raw = jnp.zeros((TOKENS, HK * HD), jnp.float32)
    for slot_index in range(N_ULY):
        lower = slot_index * feature_rows
        rows_in = normed[:, lower:lower + feature_rows]
        key_term = jnp.dot(rows_in, key_weight[lower:lower + feature_rows], preferred_element_type=jnp.float32).astype(jnp.bfloat16)
        value_term = jnp.dot(rows_in, value_weight[lower:lower + feature_rows], preferred_element_type=jnp.float32).astype(jnp.bfloat16)
        key_term, value_term = lax.optimization_barrier((key_term, value_term))
        key_raw = key_raw + key_term.astype(jnp.float32)
        value_raw = value_raw + value_term.astype(jnp.float32)
    query_in = q_raw.astype(jnp.float32).reshape(TOKENS, HK, 2, HD)
    queries = normalize(query_in, q_gain, query_scale).astype(jnp.bfloat16)
    key_in = key_raw.reshape(TOKENS, HK, HD)
    keys_bf = normalize(key_in, k_gain, 1.0).astype(jnp.bfloat16)
    values_bf = value_raw.reshape(TOKENS, HK, HD).astype(jnp.bfloat16)
    grad_heads = grad_out.reshape(TOKENS, HK, 2, HD)
    block_rows = min(512, TOKENS)
    count_blocks = TOKENS // block_rows
    span_rows = block_rows + WINDOW
    key_pad = jnp.concatenate([jnp.zeros((WINDOW, HK, HD), jnp.bfloat16), keys_bf], axis=0)
    value_pad = jnp.concatenate([jnp.zeros((WINDOW, HK, HD), jnp.bfloat16), values_bf], axis=0)
    seg_ids = segment_ids.astype(jnp.int32)
    seg_pad = jnp.concatenate([jnp.full((WINDOW,), -1, jnp.int32), seg_ids])

    def step(carry, block_index):
        key_acc, value_acc = carry
        begin_row = (block_index * block_rows).astype(jnp.int32)
        query_pos = begin_row + jnp.arange(block_rows, dtype=jnp.int32)
        key_pos = begin_row - WINDOW + jnp.arange(span_rows, dtype=jnp.int32)
        attended, dquery, dkey, dvalue = attend_block(lax.dynamic_slice_in_dim(queries, begin_row, block_rows, 0), lax.dynamic_slice_in_dim(key_pad, begin_row, span_rows, 0), lax.dynamic_slice_in_dim(value_pad, begin_row, span_rows, 0), lax.dynamic_slice_in_dim(grad_heads, begin_row, block_rows, 0), query_pos, key_pos, lax.dynamic_slice_in_dim(seg_ids, begin_row, block_rows, 0), lax.dynamic_slice_in_dim(seg_pad, begin_row, span_rows, 0))
        key_acc = lax.dynamic_update_slice_in_dim(key_acc, lax.dynamic_slice_in_dim(key_acc, begin_row, span_rows, 0) + dkey, begin_row, 0)
        value_acc = lax.dynamic_update_slice_in_dim(value_acc, lax.dynamic_slice_in_dim(value_acc, begin_row, span_rows, 0) + dvalue, begin_row, 0)
        return ((key_acc, value_acc), (attended, dquery))
    zero_acc = jnp.zeros((TOKENS + WINDOW, HK, HD), jnp.float32)
    (key_acc, value_acc), (attended, dquery) = lax.scan(step, (zero_acc, zero_acc), jnp.arange(count_blocks, dtype=jnp.int32))
    attention = attended.reshape(TOKENS, HQ * HD)
    _, pull_query = jax.vjp(lambda raw_vals: normalize(raw_vals, q_gain, query_scale), query_in)
    grad_q = pull_query(dquery.reshape(TOKENS, HK, 2, HD))[0].astype(jnp.bfloat16).reshape(TOKENS, HQ * HD)
    _, pull_key = jax.vjp(lambda raw_vals: normalize(raw_vals, k_gain, 1.0), key_in)
    key_grad = pull_key(key_acc[WINDOW:])[0].astype(jnp.bfloat16).reshape(TOKENS, HK * HD)
    value_grad = value_acc[WINDOW:].astype(jnp.bfloat16).reshape(TOKENS, HK * HD)
    grad_normed = (jnp.dot(key_grad, key_weight.T, preferred_element_type=jnp.float32) + jnp.dot(value_grad, value_weight.T, preferred_element_type=jnp.float32)).astype(jnp.bfloat16)

    def weight_step(carry, seq_block):
        begin_row = (seq_block * SPAN).astype(jnp.int32)
        rows_in = lax.dynamic_slice_in_dim(normed, begin_row, SPAN, 0)
        key_term = jnp.dot(rows_in.T, lax.dynamic_slice_in_dim(key_grad, begin_row, SPAN, 0), preferred_element_type=jnp.float32).astype(jnp.bfloat16)
        value_term = jnp.dot(rows_in.T, lax.dynamic_slice_in_dim(value_grad, begin_row, SPAN, 0), preferred_element_type=jnp.float32).astype(jnp.bfloat16)
        key_term, value_term = lax.optimization_barrier((key_term, value_term))
        return ((carry[0] + key_term.astype(jnp.float32), carry[1] + value_term.astype(jnp.float32)), None)
    weight_zero = jnp.zeros((D, HK * HD), jnp.float32)
    (grad_key_weight, grad_value_weight), _ = lax.scan(weight_step, (weight_zero, weight_zero), jnp.arange(N_SEQ, dtype=jnp.int32))
    return (attention, grad_normed, grad_q, grad_key_weight, grad_value_weight)
```

```python
import jax
import jax.numpy as jnp
from jax import lax
from jax.sharding import PartitionSpec as P

HD = 128
WINDOW = 1024


epsilon = 1e-06
query_scale = 168.0 ** (-0.5)


def from_behind(array, axis, by):
    devices = lax.axis_size(axis)
    pairs = [(i, i + by) for i in range(devices) if 0 <= i + by < devices]
    return lax.ppermute(array, axis, pairs)


def normalize(raw_vals, gain, factor):
    mean_sq = jnp.mean(raw_vals * raw_vals, axis=-1, keepdims=True)
    return raw_vals * lax.rsqrt(mean_sq + epsilon) * gain * factor


def exchange(blocks, axis):
    return lax.all_to_all(blocks, axis, 0, 0)


def gather_all(block, axis):
    count = lax.axis_size(axis)
    return exchange(jnp.broadcast_to(block[None], (count,) + block.shape), axis)


def attend_block(
    queries, key_block, value_block, grad_block, query_pos, key_pos, query_seg, key_seg
):
    scores = jnp.einsum("bhge,lhe->hgbl", queries, key_block, preferred_element_type=jnp.float32)
    allowed = (
        (key_pos[None, :] <= query_pos[:, None])
        & (key_pos[None, :] > query_pos[:, None] - WINDOW)
        & (key_seg[None, :] == query_seg[:, None])
    )
    exp_scores = jnp.where(allowed[None, None], jnp.exp(scores), 0.0)
    probs = exp_scores / jnp.sum(exp_scores, axis=-1, keepdims=True)
    weights = probs.astype(jnp.bfloat16)
    attended = jnp.einsum(
        "hgbl,lhe->bhge", weights, value_block, preferred_element_type=jnp.float32
    ).astype(jnp.bfloat16)
    dprob = jnp.einsum(
        "bhge,lhe->hgbl", grad_block, value_block, preferred_element_type=jnp.float32
    )
    delta_row = jnp.sum(probs * dprob, axis=-1, keepdims=True)
    dscore = (probs * (dprob - delta_row)).astype(jnp.bfloat16)
    dquery = jnp.einsum("hgbl,lhe->bhge", dscore, key_block, preferred_element_type=jnp.float32)
    dkey = jnp.einsum("hgbl,bhge->lhe", dscore, queries, preferred_element_type=jnp.float32)
    dvalue = jnp.einsum("hgbl,bhge->lhe", weights, grad_block, preferred_element_type=jnp.float32)
    return (attended, dquery, dkey, dvalue)


def body(normed, q_raw, key_weight, value_weight, q_gain, k_gain, segment_ids, grad_out):
    rows_here = normed.shape[0]
    feats = normed.shape[1]
    heads_here = q_raw.shape[1] // (2 * HD)
    n_seq = lax.axis_size("seq")
    n_uly = lax.axis_size("uly")
    col_block = key_weight.shape[1]
    seq_index = lax.axis_index("seq")
    base_row = seq_index * rows_here
    pair_local = jnp.stack([key_weight, value_weight], axis=1)
    gathered = gather_all(pair_local, "seq")
    weight_all = gathered.transpose(1, 2, 0, 3).reshape(feats, 2, n_uly, heads_here * HD)
    terms = jnp.einsum(
        "tf,fkhc->htkc", normed, weight_all, preferred_element_type=jnp.float32
    ).astype(jnp.bfloat16)
    received = exchange(terms, "uly")
    raw_pair = jnp.sum(received.astype(jnp.float32), axis=0)
    key_raw = raw_pair[:, 0]
    value_raw = raw_pair[:, 1]
    key_in = key_raw.reshape(rows_here, heads_here, HD)
    keys_bf = normalize(key_in, k_gain, 1.0).astype(jnp.bfloat16)
    values_bf = value_raw.reshape(rows_here, heads_here, HD).astype(jnp.bfloat16)
    query_in = q_raw.astype(jnp.float32).reshape(rows_here, heads_here, 2, HD)
    queries = normalize(query_in, q_gain, query_scale).astype(jnp.bfloat16)
    grad_heads = grad_out.reshape(rows_here, heads_here, 2, HD)
    stacked = jnp.stack([keys_bf, values_bf])
    pieces = []
    distance = 1
    pieces.append(from_behind(stacked, "seq", distance))
    pieces.append(stacked)
    extended = jnp.concatenate(pieces, axis=1)
    block_rows = min(512, rows_here)
    span_rows = block_rows + WINDOW
    count_blocks = rows_here // block_rows
    seg_pad = jnp.concatenate([jnp.full((WINDOW,), -1, jnp.int32), segment_ids])
    query_seg_all = lax.dynamic_slice_in_dim(segment_ids, base_row, rows_here, 0)
    key_seg_all = lax.dynamic_slice_in_dim(seg_pad, base_row, WINDOW + rows_here, 0)

    def step(grad_acc, block_index):
        begin_row = block_index * block_rows
        query_pos = base_row + begin_row + jnp.arange(block_rows, dtype=jnp.int32)
        key_pos = base_row + begin_row - WINDOW + jnp.arange(span_rows, dtype=jnp.int32)
        key_block = lax.dynamic_slice_in_dim(extended, begin_row, span_rows, 1)
        attended, dquery, dkey, dvalue = attend_block(
            lax.dynamic_slice_in_dim(queries, begin_row, block_rows, 0),
            key_block[0],
            key_block[1],
            lax.dynamic_slice_in_dim(grad_heads, begin_row, block_rows, 0),
            query_pos,
            key_pos,
            lax.dynamic_slice_in_dim(query_seg_all, begin_row, block_rows, 0),
            lax.dynamic_slice_in_dim(key_seg_all, begin_row, span_rows, 0),
        )
        update = jnp.stack([dkey, dvalue])
        grad_acc = lax.dynamic_update_slice_in_dim(
            grad_acc,
            lax.dynamic_slice_in_dim(grad_acc, begin_row, span_rows, 1) + update,
            begin_row,
            1,
        )
        return (grad_acc, (attended, dquery))

    zero_acc = jnp.zeros((2, WINDOW + rows_here, heads_here, HD), jnp.float32)
    grad_acc, (attended, dquery) = lax.scan(
        step, zero_acc, jnp.arange(count_blocks, dtype=jnp.int32)
    )
    attention = attended.reshape(rows_here, 2 * heads_here * HD)
    dquery = dquery.reshape(rows_here, heads_here, 2, HD)
    own_grads = grad_acc[:, WINDOW:]
    offset_row = 0
    distance = 1
    first_row = max(0, distance * rows_here - WINDOW)
    piece_rows = rows_here - first_row
    outgoing = grad_acc[:, offset_row : offset_row + piece_rows]
    returned = from_behind(outgoing.astype(jnp.bfloat16), "seq", -distance).astype(outgoing.dtype)
    own_grads = own_grads.at[:, first_row:].add(returned)
    _, pull_query = jax.vjp(lambda raw_vals: normalize(raw_vals, q_gain, query_scale), query_in)
    grad_q = pull_query(dquery)[0].astype(jnp.bfloat16).reshape(rows_here, 2 * heads_here * HD)
    _, pull_key = jax.vjp(lambda raw_vals: normalize(raw_vals, k_gain, 1.0), key_in)
    key_grad = pull_key(own_grads[0])[0].astype(jnp.bfloat16).reshape(rows_here, heads_here * HD)
    value_grad = own_grads[1].astype(jnp.bfloat16).reshape(rows_here, heads_here * HD)
    grads_all = gather_all(jnp.stack([key_grad, value_grad], axis=1), "uly")
    grad_normed = jnp.einsum(
        "htkc,fkhc->tf", grads_all, weight_all, preferred_element_type=jnp.float32
    ).astype(jnp.bfloat16)
    weight_part = jnp.einsum(
        "tf,htkc->fkhc", normed, grads_all, preferred_element_type=jnp.float32
    ).astype(jnp.bfloat16)
    to_owner = weight_part.reshape(feats, 2, n_seq, col_block).transpose(2, 0, 1, 3)
    summed = jnp.sum(exchange(to_owner, "seq").astype(jnp.float32), axis=0)
    grad_key_weight = summed[:, 0]
    grad_value_weight = summed[:, 1]
    return (attention, grad_normed, grad_q, grad_key_weight, grad_value_weight)


def solution(mesh):
    return jax.shard_map(
        body,
        mesh=mesh,
        in_specs=(
            P("seq", "uly"),
            P("seq", "uly"),
            P("uly", "seq"),
            P("uly", "seq"),
            P(),
            P(),
            P(),
            P("seq", "uly"),
        ),
        out_specs=(
            P("seq", "uly"),
            P("seq", "uly"),
            P("seq", "uly"),
            P("uly", "seq"),
            P("uly", "seq"),
        ),
        check_vma=False,
    )
```

```python
import jax
import jax.numpy as jnp
from jax import lax
from jax.sharding import PartitionSpec as P

HD = 128
WINDOW = 1024


epsilon = 1e-06
query_scale = 168.0 ** (-0.5)


def from_behind(array, axis, by):
    devices = lax.axis_size(axis)
    pairs = [(i, i + by) for i in range(devices) if 0 <= i + by < devices]
    return lax.ppermute(array, axis, pairs)


def normalize(raw_vals, gain, factor):
    mean_sq = jnp.mean(raw_vals * raw_vals, axis=-1, keepdims=True)
    return raw_vals * lax.rsqrt(mean_sq + epsilon) * gain * factor


def exchange(blocks, axis):
    return lax.all_to_all(blocks, axis, 0, 0)


def gather_all(block, axis):
    count = lax.axis_size(axis)
    return exchange(jnp.broadcast_to(block[None], (count,) + block.shape), axis)


SEQ = ("chip", "core")
SWAP = [(0, 1), (1, 0)]


def gather_seq(block):
    mine = gather_all(block, "chip")
    other = lax.ppermute(mine, "core", SWAP)
    first = lax.axis_index("core") == 0
    pair = jnp.where(first, jnp.stack([mine, other], 1), jnp.stack([other, mine], 1))
    return pair.reshape((-1,) + block.shape)


def reduce_seq(blocks):
    chips = blocks.shape[0] // 2
    split = blocks.reshape((chips, 2) + blocks.shape[1:])
    core = lax.axis_index("core")
    keep = jnp.take(split, core, axis=1)
    send = jnp.take(split, 1 - core, axis=1)
    pair = (keep.astype(jnp.float32) + lax.ppermute(send, "core", SWAP).astype(jnp.float32))
    return jnp.sum(exchange(pair.astype(jnp.bfloat16), "chip").astype(jnp.float32), axis=0)


def attend_block(
    queries, key_block, value_block, grad_block, query_pos, key_pos, query_seg, key_seg
):
    scores = jnp.einsum("bhge,lhe->hgbl", queries, key_block, preferred_element_type=jnp.float32)
    allowed = (
        (key_pos[None, :] <= query_pos[:, None])
        & (key_pos[None, :] > query_pos[:, None] - WINDOW)
        & (key_seg[None, :] == query_seg[:, None])
    )
    exp_scores = jnp.where(allowed[None, None], jnp.exp(scores), 0.0)
    probs = exp_scores / jnp.sum(exp_scores, axis=-1, keepdims=True)
    weights = probs.astype(jnp.bfloat16)
    attended = jnp.einsum(
        "hgbl,lhe->bhge", weights, value_block, preferred_element_type=jnp.float32
    ).astype(jnp.bfloat16)
    dprob = jnp.einsum(
        "bhge,lhe->hgbl", grad_block, value_block, preferred_element_type=jnp.float32
    )
    delta_row = jnp.sum(probs * dprob, axis=-1, keepdims=True)
    dscore = (probs * (dprob - delta_row)).astype(jnp.bfloat16)
    dquery = jnp.einsum("hgbl,lhe->bhge", dscore, key_block, preferred_element_type=jnp.float32)
    dkey = jnp.einsum("hgbl,bhge->lhe", dscore, queries, preferred_element_type=jnp.float32)
    dvalue = jnp.einsum("hgbl,bhge->lhe", weights, grad_block, preferred_element_type=jnp.float32)
    return (attended, dquery, dkey, dvalue)


def body(normed, q_raw, key_weight, value_weight, q_gain, k_gain, segment_ids, grad_out):
    rows_here = normed.shape[0]
    feats = normed.shape[1]
    heads_here = q_raw.shape[1] // (2 * HD)
    n_seq = lax.axis_size(SEQ)
    n_uly = lax.axis_size("uly")
    col_block = key_weight.shape[1]
    seq_index = lax.axis_index(SEQ)
    base_row = seq_index * rows_here
    pair_local = jnp.stack([key_weight, value_weight], axis=1)
    gathered = gather_seq(pair_local)
    weight_all = gathered.transpose(1, 2, 0, 3).reshape(feats, 2, n_uly, heads_here * HD)
    terms = jnp.einsum(
        "tf,fkhc->htkc", normed, weight_all, preferred_element_type=jnp.float32
    ).astype(jnp.bfloat16)
    received = exchange(terms, "uly")
    raw_pair = jnp.sum(received.astype(jnp.float32), axis=0)
    key_raw = raw_pair[:, 0]
    value_raw = raw_pair[:, 1]
    key_in = key_raw.reshape(rows_here, heads_here, HD)
    keys_bf = normalize(key_in, k_gain, 1.0).astype(jnp.bfloat16)
    values_bf = value_raw.reshape(rows_here, heads_here, HD).astype(jnp.bfloat16)
    query_in = q_raw.astype(jnp.float32).reshape(rows_here, heads_here, 2, HD)
    queries = normalize(query_in, q_gain, query_scale).astype(jnp.bfloat16)
    grad_heads = grad_out.reshape(rows_here, heads_here, 2, HD)
    stacked = jnp.stack([keys_bf, values_bf])
    pieces = []
    distance = 1
    pieces.append(from_behind(stacked, SEQ, distance))
    pieces.append(stacked)
    extended = jnp.concatenate(pieces, axis=1)
    block_rows = min(512, rows_here)
    span_rows = block_rows + WINDOW
    count_blocks = rows_here // block_rows
    seg_pad = jnp.concatenate([jnp.full((WINDOW,), -1, jnp.int32), segment_ids])
    query_seg_all = lax.dynamic_slice_in_dim(segment_ids, base_row, rows_here, 0)
    key_seg_all = lax.dynamic_slice_in_dim(seg_pad, base_row, WINDOW + rows_here, 0)

    def step(grad_acc, block_index):
        begin_row = block_index * block_rows
        query_pos = base_row + begin_row + jnp.arange(block_rows, dtype=jnp.int32)
        key_pos = base_row + begin_row - WINDOW + jnp.arange(span_rows, dtype=jnp.int32)
        key_block = lax.dynamic_slice_in_dim(extended, begin_row, span_rows, 1)
        attended, dquery, dkey, dvalue = attend_block(
            lax.dynamic_slice_in_dim(queries, begin_row, block_rows, 0),
            key_block[0],
            key_block[1],
            lax.dynamic_slice_in_dim(grad_heads, begin_row, block_rows, 0),
            query_pos,
            key_pos,
            lax.dynamic_slice_in_dim(query_seg_all, begin_row, block_rows, 0),
            lax.dynamic_slice_in_dim(key_seg_all, begin_row, span_rows, 0),
        )
        update = jnp.stack([dkey, dvalue])
        grad_acc = lax.dynamic_update_slice_in_dim(
            grad_acc,
            lax.dynamic_slice_in_dim(grad_acc, begin_row, span_rows, 1) + update,
            begin_row,
            1,
        )
        return (grad_acc, (attended, dquery))

    zero_acc = jnp.zeros((2, WINDOW + rows_here, heads_here, HD), jnp.float32)
    grad_acc, (attended, dquery) = lax.scan(
        step, zero_acc, jnp.arange(count_blocks, dtype=jnp.int32)
    )
    attention = attended.reshape(rows_here, 2 * heads_here * HD)
    dquery = dquery.reshape(rows_here, heads_here, 2, HD)
    own_grads = grad_acc[:, WINDOW:]
    offset_row = 0
    distance = 1
    first_row = max(0, distance * rows_here - WINDOW)
    piece_rows = rows_here - first_row
    outgoing = grad_acc[:, offset_row : offset_row + piece_rows]
    returned = from_behind(outgoing.astype(jnp.bfloat16), SEQ, -distance).astype(outgoing.dtype)
    own_grads = own_grads.at[:, first_row:].add(returned)
    _, pull_query = jax.vjp(lambda raw_vals: normalize(raw_vals, q_gain, query_scale), query_in)
    grad_q = pull_query(dquery)[0].astype(jnp.bfloat16).reshape(rows_here, 2 * heads_here * HD)
    _, pull_key = jax.vjp(lambda raw_vals: normalize(raw_vals, k_gain, 1.0), key_in)
    key_grad = pull_key(own_grads[0])[0].astype(jnp.bfloat16).reshape(rows_here, heads_here * HD)
    value_grad = own_grads[1].astype(jnp.bfloat16).reshape(rows_here, heads_here * HD)
    grads_all = gather_all(jnp.stack([key_grad, value_grad], axis=1), "uly")
    grad_normed = jnp.einsum(
        "htkc,fkhc->tf", grads_all, weight_all, preferred_element_type=jnp.float32
    ).astype(jnp.bfloat16)
    weight_part = jnp.einsum(
        "tf,htkc->fkhc", normed, grads_all, preferred_element_type=jnp.float32
    ).astype(jnp.bfloat16)
    to_owner = weight_part.reshape(feats, 2, n_seq, col_block).transpose(2, 0, 1, 3)
    summed = reduce_seq(to_owner)
    grad_key_weight = summed[:, 0]
    grad_value_weight = summed[:, 1]
    return (attention, grad_normed, grad_q, grad_key_weight, grad_value_weight)


def solution(mesh):
    n_seq, n_uly = mesh.shape["seq"], mesh.shape["uly"]
    fine = jax.sharding.Mesh(mesh.devices.reshape(n_seq // 2, 2, n_uly), ("chip", "core", "uly"))
    return jax.shard_map(
        body,
        mesh=fine,
        in_specs=(
            P(SEQ, "uly"),
            P(SEQ, "uly"),
            P("uly", SEQ),
            P("uly", SEQ),
            P(),
            P(),
            P(),
            P(SEQ, "uly"),
        ),
        out_specs=(
            P(SEQ, "uly"),
            P(SEQ, "uly"),
            P(SEQ, "uly"),
            P("uly", SEQ),
            P("uly", SEQ),
        ),
        check_vma=False,
    )
```

```python
import jax
import jax.numpy as jnp
from jax import lax
from jax.experimental import pallas as pl
from jax.experimental.pallas import tpu as pltpu
from jax.sharding import PartitionSpec as P

HD = 128
WINDOW = 1024


epsilon = 1e-06
query_scale = 168.0 ** (-0.5)


def from_behind(array, axis, by):
    devices = lax.axis_size(axis)
    pairs = [(i, i + by) for i in range(devices) if 0 <= i + by < devices]
    return lax.ppermute(array, axis, pairs)


def normalize(raw_vals, gain, factor):
    mean_sq = jnp.mean(raw_vals * raw_vals, axis=-1, keepdims=True)
    return raw_vals * lax.rsqrt(mean_sq + epsilon) * gain * factor


def exchange(blocks, axis):
    return lax.all_to_all(blocks, axis, 0, 0)


def gather_all(block, axis):
    count = lax.axis_size(axis)
    return exchange(jnp.broadcast_to(block[None], (count,) + block.shape), axis)


SEQ = ("chip", "core")
SWAP = [(0, 1), (1, 0)]


def gather_seq(block):
    mine = gather_all(block, "chip")
    other = lax.ppermute(mine, "core", SWAP)
    first = lax.axis_index("core") == 0
    pair = jnp.where(first, jnp.stack([mine, other], 1), jnp.stack([other, mine], 1))
    return pair.reshape((-1,) + block.shape)


def reduce_seq(blocks):
    chips = blocks.shape[0] // 2
    split = blocks.reshape((chips, 2) + blocks.shape[1:])
    core = lax.axis_index("core")
    keep = jnp.take(split, core, axis=1)
    send = jnp.take(split, 1 - core, axis=1)
    pair = (keep.astype(jnp.float32) + lax.ppermute(send, "core", SWAP).astype(jnp.float32))
    return jnp.sum(exchange(pair.astype(jnp.bfloat16), "chip").astype(jnp.float32), axis=0)


def attend_block(
    queries, key_block, value_block, grad_block, query_pos, key_pos, query_seg, key_seg
):
    scores = jnp.einsum("bhge,lhe->hgbl", queries, key_block, preferred_element_type=jnp.float32)
    allowed = (
        (key_pos[None, :] <= query_pos[:, None])
        & (key_pos[None, :] > query_pos[:, None] - WINDOW)
        & (key_seg[None, :] == query_seg[:, None])
    )
    exp_scores = jnp.where(allowed[None, None], jnp.exp(scores), 0.0)
    probs = exp_scores / jnp.sum(exp_scores, axis=-1, keepdims=True)
    weights = probs.astype(jnp.bfloat16)
    attended = jnp.einsum(
        "hgbl,lhe->bhge", weights, value_block, preferred_element_type=jnp.float32
    ).astype(jnp.bfloat16)
    dprob = jnp.einsum(
        "bhge,lhe->hgbl", grad_block, value_block, preferred_element_type=jnp.float32
    )
    delta_row = jnp.sum(probs * dprob, axis=-1, keepdims=True)
    dscore = (probs * (dprob - delta_row)).astype(jnp.bfloat16)
    dquery = jnp.einsum("hgbl,lhe->bhge", dscore, key_block, preferred_element_type=jnp.float32)
    dkey = jnp.einsum("hgbl,bhge->lhe", dscore, queries, preferred_element_type=jnp.float32)
    dvalue = jnp.einsum("hgbl,bhge->lhe", weights, grad_block, preferred_element_type=jnp.float32)
    return (attended, dquery, dkey, dvalue)


def attention_kernel(q_ref, do_ref, k_ref, v_ref, qseg_ref, kseg_ref, out_ref, dq_ref, dkv_ref):
    rows = q_ref.shape[0]
    block = 256
    span = block + WINDOW
    dkv_ref[...] = jnp.zeros(dkv_ref.shape, jnp.float32)
    nt = (((1,), (1,)), ((), ()))
    tn = (((0,), (0,)), ((), ()))
    for b in range(rows // block):
        r0 = b * block
        k = k_ref[pl.ds(r0, span), :]
        v = v_ref[pl.ds(r0, span), :]
        row = lax.broadcasted_iota(jnp.int32, (block, span), 0)
        col = lax.broadcasted_iota(jnp.int32, (block, span), 1)
        allowed = (col <= row + WINDOW) & (col > row)
        allowed = allowed & (qseg_ref[pl.ds(r0, block), :] == kseg_ref[:, pl.ds(r0, span)])
        dk_acc = jnp.zeros((span, HD), jnp.float32)
        dv_acc = jnp.zeros((span, HD), jnp.float32)
        for g in range(2):
            q = q_ref[pl.ds(r0, block), pl.ds(g * HD, HD)]
            do = do_ref[pl.ds(r0, block), pl.ds(g * HD, HD)]
            scores = lax.dot_general(q, k, nt, preferred_element_type=jnp.float32)
            exp_scores = jnp.where(allowed, jnp.exp(scores), 0.0)
            probs = exp_scores / jnp.sum(exp_scores, axis=1, keepdims=True)
            weights = probs.astype(jnp.bfloat16)
            out_ref[pl.ds(r0, block), pl.ds(g * HD, HD)] = jnp.dot(
                weights, v, preferred_element_type=jnp.float32
            ).astype(out_ref.dtype)
            dprob = lax.dot_general(do, v, nt, preferred_element_type=jnp.float32)
            delta_row = jnp.sum(probs * dprob, axis=1, keepdims=True)
            dscore = (probs * (dprob - delta_row)).astype(jnp.bfloat16)
            dq_ref[pl.ds(r0, block), pl.ds(g * HD, HD)] = jnp.dot(
                dscore, k, preferred_element_type=jnp.float32
            )
            dk_acc = dk_acc + lax.dot_general(dscore, q, tn, preferred_element_type=jnp.float32)
            dv_acc = dv_acc + lax.dot_general(weights, do, tn, preferred_element_type=jnp.float32)
        dkv_ref[0, pl.ds(r0, span), :] += dk_acc
        dkv_ref[1, pl.ds(r0, span), :] += dv_acc


def attend(queries, grad_out, keys, values, query_seg, key_seg):
    rows = queries.shape[0]
    spec = pl.BlockSpec(memory_space=pltpu.VMEM)
    return pl.pallas_call(
        attention_kernel,
        out_shape=(
            jax.ShapeDtypeStruct((rows, 2 * HD), jnp.bfloat16),
            jax.ShapeDtypeStruct((rows, 2 * HD), jnp.float32),
            jax.ShapeDtypeStruct((2, keys.shape[0], HD), jnp.float32),
        ),
        in_specs=[spec] * 6,
        out_specs=(spec, spec, spec),
        cost_estimate=pl.CostEstimate(
            flops=12 * rows * (rows + WINDOW) * HD * 2, transcendentals=2 * rows * (rows + WINDOW),
            bytes_accessed=16 * rows * HD * 4,
        ),
    )(queries, grad_out, keys, values, query_seg, key_seg)


def body(normed, q_raw, key_weight, value_weight, q_gain, k_gain, segment_ids, grad_out):
    rows_here = normed.shape[0]
    feats = normed.shape[1]
    heads_here = q_raw.shape[1] // (2 * HD)
    n_seq = lax.axis_size(SEQ)
    n_uly = lax.axis_size("uly")
    col_block = key_weight.shape[1]
    seq_index = lax.axis_index(SEQ)
    base_row = seq_index * rows_here
    pair_local = jnp.stack([key_weight, value_weight], axis=1)
    gathered = gather_seq(pair_local)
    weight_all = gathered.transpose(1, 2, 0, 3).reshape(feats, 2, n_uly, heads_here * HD)
    terms = jnp.einsum(
        "tf,fkhc->htkc", normed, weight_all, preferred_element_type=jnp.float32
    ).astype(jnp.bfloat16)
    received = exchange(terms, "uly")
    raw_pair = jnp.sum(received.astype(jnp.float32), axis=0)
    key_raw = raw_pair[:, 0]
    value_raw = raw_pair[:, 1]
    key_in = key_raw.reshape(rows_here, heads_here, HD)
    keys_bf = normalize(key_in, k_gain, 1.0).astype(jnp.bfloat16)
    values_bf = value_raw.reshape(rows_here, heads_here, HD).astype(jnp.bfloat16)
    query_in = q_raw.astype(jnp.float32).reshape(rows_here, heads_here, 2, HD)
    queries = normalize(query_in, q_gain, query_scale).astype(jnp.bfloat16)
    grad_heads = grad_out.reshape(rows_here, heads_here, 2, HD)
    stacked = jnp.stack([keys_bf, values_bf])
    behind = from_behind(stacked, SEQ, 1)
    extended = jnp.concatenate([behind, stacked], axis=1).reshape(2, WINDOW + rows_here, HD)
    seg_pad = jnp.concatenate([jnp.full((WINDOW,), -1, jnp.int32), segment_ids])
    query_seg = lax.dynamic_slice_in_dim(segment_ids, base_row, rows_here, 0)
    key_seg = lax.dynamic_slice_in_dim(seg_pad, base_row, WINDOW + rows_here, 0)
    attention, dquery, grad_acc = attend(
        queries.reshape(rows_here, 2 * HD),
        grad_out,
        extended[0],
        extended[1],
        query_seg.reshape(rows_here, 1),
        key_seg.reshape(1, WINDOW + rows_here),
    )
    dquery = dquery.reshape(rows_here, heads_here, 2, HD)
    grad_acc = grad_acc.reshape(2, WINDOW + rows_here, heads_here, HD)
    own_grads = grad_acc[:, WINDOW:]
    offset_row = 0
    distance = 1
    first_row = max(0, distance * rows_here - WINDOW)
    piece_rows = rows_here - first_row
    outgoing = grad_acc[:, offset_row : offset_row + piece_rows]
    returned = from_behind(outgoing.astype(jnp.bfloat16), SEQ, -distance).astype(outgoing.dtype)
    own_grads = own_grads.at[:, first_row:].add(returned)
    _, pull_query = jax.vjp(lambda raw_vals: normalize(raw_vals, q_gain, query_scale), query_in)
    grad_q = pull_query(dquery)[0].astype(jnp.bfloat16).reshape(rows_here, 2 * heads_here * HD)
    _, pull_key = jax.vjp(lambda raw_vals: normalize(raw_vals, k_gain, 1.0), key_in)
    key_grad = pull_key(own_grads[0])[0].astype(jnp.bfloat16).reshape(rows_here, heads_here * HD)
    value_grad = own_grads[1].astype(jnp.bfloat16).reshape(rows_here, heads_here * HD)
    grads_all = gather_all(jnp.stack([key_grad, value_grad], axis=1), "uly")
    grad_normed = jnp.einsum(
        "htkc,fkhc->tf", grads_all, weight_all, preferred_element_type=jnp.float32
    ).astype(jnp.bfloat16)
    weight_part = jnp.einsum(
        "tf,htkc->fkhc", normed, grads_all, preferred_element_type=jnp.float32
    ).astype(jnp.bfloat16)
    to_owner = weight_part.reshape(feats, 2, n_seq, col_block).transpose(2, 0, 1, 3)
    summed = reduce_seq(to_owner)
    grad_key_weight = summed[:, 0]
    grad_value_weight = summed[:, 1]
    return (attention, grad_normed, grad_q, grad_key_weight, grad_value_weight)


def solution(mesh):
    n_seq, n_uly = mesh.shape["seq"], mesh.shape["uly"]
    fine = jax.sharding.Mesh(mesh.devices.reshape(n_seq // 2, 2, n_uly), ("chip", "core", "uly"))
    return jax.shard_map(
        body,
        mesh=fine,
        in_specs=(
            P(SEQ, "uly"),
            P(SEQ, "uly"),
            P("uly", SEQ),
            P("uly", SEQ),
            P(),
            P(),
            P(),
            P(SEQ, "uly"),
        ),
        out_specs=(
            P(SEQ, "uly"),
            P(SEQ, "uly"),
            P(SEQ, "uly"),
            P("uly", SEQ),
            P("uly", SEQ),
        ),
        check_vma=False,
    )
```

```python
import functools

import jax
import jax.numpy as jnp
from jax import lax
from jax.experimental import pallas as pl
from jax.experimental.pallas import tpu as pltpu
from jax.sharding import PartitionSpec as P

HD = 128
WINDOW = 1024


epsilon = 1e-06
query_scale = 168.0 ** (-0.5)


def from_behind(array, axis, by):
    devices = lax.axis_size(axis)
    pairs = [(i, i + by) for i in range(devices) if 0 <= i + by < devices]
    return lax.ppermute(array, axis, pairs)


def normalize(raw_vals, gain, factor):
    mean_sq = jnp.mean(raw_vals * raw_vals, axis=-1, keepdims=True)
    return raw_vals * lax.rsqrt(mean_sq + epsilon) * gain * factor


def exchange(blocks, axis):
    return lax.all_to_all(blocks, axis, 0, 0)


def gather_all(block, axis):
    count = lax.axis_size(axis)
    return exchange(jnp.broadcast_to(block[None], (count,) + block.shape), axis)


SEQ = ("chip", "core")
SWAP = [(0, 1), (1, 0)]


def gather_kernel(chips, x_ref, out_ref, local_sem, send_sem, recv_sem, fwd_send, fwd_recv):
    chip = lax.axis_index("chip")
    core = lax.axis_index("core")
    uly = lax.axis_index("uly")
    other = 1 - core
    mesh_ids = pl.DeviceIdType.MESH
    barrier = pltpu.get_barrier_semaphore()
    for d in range(1, chips):
        peer = (lax.rem(chip + d, chips), core, uly)
        pl.semaphore_signal(barrier, 1, device_id=peer, device_id_type=mesh_ids)
    pl.semaphore_signal(barrier, 1, device_id=(chip, other, uly), device_id_type=mesh_ids)
    pl.semaphore_wait(barrier, chips)
    mine = chip * 2 + core
    local = pltpu.make_async_copy(x_ref, out_ref.at[mine], local_sem)
    local.start()
    sends = {}
    for d in range(1, chips):
        sends[d] = pltpu.make_async_remote_copy(
            src_ref=x_ref,
            dst_ref=out_ref.at[mine],
            send_sem=send_sem.at[d],
            recv_sem=recv_sem.at[d],
            device_id=(lax.rem(chip + d, chips), core, uly),
            device_id_type=mesh_ids,
        )
        sends[d].start()
    forwards = [
        pltpu.make_async_remote_copy(
            src_ref=x_ref,
            dst_ref=out_ref.at[mine],
            send_sem=fwd_send.at[0],
            recv_sem=fwd_recv.at[0],
            device_id=(chip, other, uly),
            device_id_type=mesh_ids,
        )
    ]
    forwards[0].start()
    for d in range(1, chips):
        sends[d].wait_recv()
        slot = lax.rem(chip + chips - d, chips) * 2 + core
        forward = pltpu.make_async_remote_copy(
            src_ref=out_ref.at[slot],
            dst_ref=out_ref.at[slot],
            send_sem=fwd_send.at[d],
            recv_sem=fwd_recv.at[d],
            device_id=(chip, other, uly),
            device_id_type=mesh_ids,
        )
        forward.start()
        forwards.append(forward)
    for d in range(1, chips):
        sends[d].wait_send()
    for forward in forwards:
        forward.wait()
    local.wait()


def gather_seq(block):
    chips = lax.axis_size("chip")
    flat = block.reshape(-1, 128)
    spec = pl.BlockSpec(memory_space=pltpu.VMEM)
    out = pl.pallas_call(
        functools.partial(gather_kernel, chips),
        out_shape=jax.ShapeDtypeStruct((2 * chips,) + flat.shape, flat.dtype),
        in_specs=[spec],
        out_specs=spec,
        scratch_shapes=[
            pltpu.SemaphoreType.DMA(()),
            pltpu.SemaphoreType.DMA((chips,)),
            pltpu.SemaphoreType.DMA((chips,)),
            pltpu.SemaphoreType.DMA((chips,)),
            pltpu.SemaphoreType.DMA((chips,)),
        ],
        compiler_params=pltpu.CompilerParams(collective_id=0, has_side_effects=True),
    )(flat)
    return out.reshape((2 * chips,) + block.shape)


def reduce_seq(blocks):
    chips = blocks.shape[0] // 2
    split = blocks.reshape((chips, 2) + blocks.shape[1:])
    core = lax.axis_index("core")
    keep = jnp.take(split, core, axis=1)
    send = jnp.take(split, 1 - core, axis=1)
    pair = (keep.astype(jnp.float32) + lax.ppermute(send, "core", SWAP).astype(jnp.float32))
    return jnp.sum(exchange(pair.astype(jnp.bfloat16), "chip").astype(jnp.float32), axis=0)


def attend_block(
    queries, key_block, value_block, grad_block, query_pos, key_pos, query_seg, key_seg
):
    scores = jnp.einsum("bhge,lhe->hgbl", queries, key_block, preferred_element_type=jnp.float32)
    allowed = (
        (key_pos[None, :] <= query_pos[:, None])
        & (key_pos[None, :] > query_pos[:, None] - WINDOW)
        & (key_seg[None, :] == query_seg[:, None])
    )
    exp_scores = jnp.where(allowed[None, None], jnp.exp(scores), 0.0)
    probs = exp_scores / jnp.sum(exp_scores, axis=-1, keepdims=True)
    weights = probs.astype(jnp.bfloat16)
    attended = jnp.einsum(
        "hgbl,lhe->bhge", weights, value_block, preferred_element_type=jnp.float32
    ).astype(jnp.bfloat16)
    dprob = jnp.einsum(
        "bhge,lhe->hgbl", grad_block, value_block, preferred_element_type=jnp.float32
    )
    delta_row = jnp.sum(probs * dprob, axis=-1, keepdims=True)
    dscore = (probs * (dprob - delta_row)).astype(jnp.bfloat16)
    dquery = jnp.einsum("hgbl,lhe->bhge", dscore, key_block, preferred_element_type=jnp.float32)
    dkey = jnp.einsum("hgbl,bhge->lhe", dscore, queries, preferred_element_type=jnp.float32)
    dvalue = jnp.einsum("hgbl,bhge->lhe", weights, grad_block, preferred_element_type=jnp.float32)
    return (attended, dquery, dkey, dvalue)


def attention_kernel(q_ref, do_ref, k_ref, v_ref, qseg_ref, kseg_ref, out_ref, dq_ref, dkv_ref):
    rows = q_ref.shape[0]
    block = 256
    span = block + WINDOW
    dkv_ref[...] = jnp.zeros(dkv_ref.shape, jnp.float32)
    nt = (((1,), (1,)), ((), ()))
    tn = (((0,), (0,)), ((), ()))
    for b in range(rows // block):
        r0 = b * block
        k = k_ref[pl.ds(r0, span), :]
        v = v_ref[pl.ds(r0, span), :]
        row = lax.broadcasted_iota(jnp.int32, (block, span), 0)
        col = lax.broadcasted_iota(jnp.int32, (block, span), 1)
        allowed = (col <= row + WINDOW) & (col > row)
        allowed = allowed & (qseg_ref[pl.ds(r0, block), :] == kseg_ref[:, pl.ds(r0, span)])
        dk_acc = jnp.zeros((span, HD), jnp.float32)
        dv_acc = jnp.zeros((span, HD), jnp.float32)
        for g in range(2):
            q = q_ref[pl.ds(r0, block), pl.ds(g * HD, HD)]
            do = do_ref[pl.ds(r0, block), pl.ds(g * HD, HD)]
            scores = lax.dot_general(q, k, nt, preferred_element_type=jnp.float32)
            exp_scores = jnp.where(allowed, jnp.exp(scores), 0.0)
            probs = exp_scores / jnp.sum(exp_scores, axis=1, keepdims=True)
            weights = probs.astype(jnp.bfloat16)
            out_ref[pl.ds(r0, block), pl.ds(g * HD, HD)] = jnp.dot(
                weights, v, preferred_element_type=jnp.float32
            ).astype(out_ref.dtype)
            dprob = lax.dot_general(do, v, nt, preferred_element_type=jnp.float32)
            delta_row = jnp.sum(probs * dprob, axis=1, keepdims=True)
            dscore = (probs * (dprob - delta_row)).astype(jnp.bfloat16)
            dq_ref[pl.ds(r0, block), pl.ds(g * HD, HD)] = jnp.dot(
                dscore, k, preferred_element_type=jnp.float32
            )
            dk_acc = dk_acc + lax.dot_general(dscore, q, tn, preferred_element_type=jnp.float32)
            dv_acc = dv_acc + lax.dot_general(weights, do, tn, preferred_element_type=jnp.float32)
        dkv_ref[0, pl.ds(r0, span), :] += dk_acc
        dkv_ref[1, pl.ds(r0, span), :] += dv_acc


def attend(queries, grad_out, keys, values, query_seg, key_seg):
    rows = queries.shape[0]
    spec = pl.BlockSpec(memory_space=pltpu.VMEM)
    return pl.pallas_call(
        attention_kernel,
        out_shape=(
            jax.ShapeDtypeStruct((rows, 2 * HD), jnp.bfloat16),
            jax.ShapeDtypeStruct((rows, 2 * HD), jnp.float32),
            jax.ShapeDtypeStruct((2, keys.shape[0], HD), jnp.float32),
        ),
        in_specs=[spec] * 6,
        out_specs=(spec, spec, spec),
        cost_estimate=pl.CostEstimate(
            flops=12 * rows * (rows + WINDOW) * HD * 2, transcendentals=2 * rows * (rows + WINDOW),
            bytes_accessed=16 * rows * HD * 4,
        ),
    )(queries, grad_out, keys, values, query_seg, key_seg)


def body(normed, q_raw, key_weight, value_weight, q_gain, k_gain, segment_ids, grad_out):
    rows_here = normed.shape[0]
    feats = normed.shape[1]
    heads_here = q_raw.shape[1] // (2 * HD)
    n_seq = lax.axis_size(SEQ)
    n_uly = lax.axis_size("uly")
    col_block = key_weight.shape[1]
    seq_index = lax.axis_index(SEQ)
    base_row = seq_index * rows_here
    pair_local = jnp.stack([key_weight, value_weight], axis=1)
    gathered = gather_seq(pair_local)
    weight_all = gathered.transpose(1, 2, 0, 3).reshape(feats, 2, n_uly, heads_here * HD)
    terms = jnp.einsum(
        "tf,fkhc->htkc", normed, weight_all, preferred_element_type=jnp.float32
    ).astype(jnp.bfloat16)
    received = exchange(terms, "uly")
    raw_pair = jnp.sum(received.astype(jnp.float32), axis=0)
    key_raw = raw_pair[:, 0]
    value_raw = raw_pair[:, 1]
    key_in = key_raw.reshape(rows_here, heads_here, HD)
    keys_bf = normalize(key_in, k_gain, 1.0).astype(jnp.bfloat16)
    values_bf = value_raw.reshape(rows_here, heads_here, HD).astype(jnp.bfloat16)
    query_in = q_raw.astype(jnp.float32).reshape(rows_here, heads_here, 2, HD)
    queries = normalize(query_in, q_gain, query_scale).astype(jnp.bfloat16)
    grad_heads = grad_out.reshape(rows_here, heads_here, 2, HD)
    stacked = jnp.stack([keys_bf, values_bf])
    behind = from_behind(stacked, SEQ, 1)
    extended = jnp.concatenate([behind, stacked], axis=1).reshape(2, WINDOW + rows_here, HD)
    seg_pad = jnp.concatenate([jnp.full((WINDOW,), -1, jnp.int32), segment_ids])
    query_seg = lax.dynamic_slice_in_dim(segment_ids, base_row, rows_here, 0)
    key_seg = lax.dynamic_slice_in_dim(seg_pad, base_row, WINDOW + rows_here, 0)
    attention, dquery, grad_acc = attend(
        queries.reshape(rows_here, 2 * HD),
        grad_out,
        extended[0],
        extended[1],
        query_seg.reshape(rows_here, 1),
        key_seg.reshape(1, WINDOW + rows_here),
    )
    dquery = dquery.reshape(rows_here, heads_here, 2, HD)
    grad_acc = grad_acc.reshape(2, WINDOW + rows_here, heads_here, HD)
    own_grads = grad_acc[:, WINDOW:]
    offset_row = 0
    distance = 1
    first_row = max(0, distance * rows_here - WINDOW)
    piece_rows = rows_here - first_row
    outgoing = grad_acc[:, offset_row : offset_row + piece_rows]
    returned = from_behind(outgoing.astype(jnp.bfloat16), SEQ, -distance).astype(outgoing.dtype)
    own_grads = own_grads.at[:, first_row:].add(returned)
    _, pull_query = jax.vjp(lambda raw_vals: normalize(raw_vals, q_gain, query_scale), query_in)
    grad_q = pull_query(dquery)[0].astype(jnp.bfloat16).reshape(rows_here, 2 * heads_here * HD)
    _, pull_key = jax.vjp(lambda raw_vals: normalize(raw_vals, k_gain, 1.0), key_in)
    key_grad = pull_key(own_grads[0])[0].astype(jnp.bfloat16).reshape(rows_here, heads_here * HD)
    value_grad = own_grads[1].astype(jnp.bfloat16).reshape(rows_here, heads_here * HD)
    grads_all = gather_all(jnp.stack([key_grad, value_grad], axis=1), "uly")
    grad_normed = jnp.einsum(
        "htkc,fkhc->tf", grads_all, weight_all, preferred_element_type=jnp.float32
    ).astype(jnp.bfloat16)
    weight_part = jnp.einsum(
        "tf,htkc->fkhc", normed, grads_all, preferred_element_type=jnp.float32
    ).astype(jnp.bfloat16)
    to_owner = weight_part.reshape(feats, 2, n_seq, col_block).transpose(2, 0, 1, 3)
    summed = reduce_seq(to_owner)
    grad_key_weight = summed[:, 0]
    grad_value_weight = summed[:, 1]
    return (attention, grad_normed, grad_q, grad_key_weight, grad_value_weight)


def solution(mesh):
    n_seq, n_uly = mesh.shape["seq"], mesh.shape["uly"]
    fine = jax.sharding.Mesh(mesh.devices.reshape(n_seq // 2, 2, n_uly), ("chip", "core", "uly"))
    return jax.shard_map(
        body,
        mesh=fine,
        in_specs=(
            P(SEQ, "uly"),
            P(SEQ, "uly"),
            P("uly", SEQ),
            P("uly", SEQ),
            P(),
            P(),
            P(),
            P(SEQ, "uly"),
        ),
        out_specs=(
            P(SEQ, "uly"),
            P(SEQ, "uly"),
            P(SEQ, "uly"),
            P("uly", SEQ),
            P("uly", SEQ),
        ),
        check_vma=False,
    )
```

```python
import functools

import jax
import jax.numpy as jnp
from jax import lax
from jax.experimental import pallas as pl
from jax.experimental.pallas import tpu as pltpu
from jax.sharding import PartitionSpec as P

HD = 128
WINDOW = 1024


epsilon = 1e-06
query_scale = 168.0 ** (-0.5)


def from_behind(array, axis, by):
    devices = lax.axis_size(axis)
    pairs = [(i, i + by) for i in range(devices) if 0 <= i + by < devices]
    return lax.ppermute(array, axis, pairs)


def normalize(raw_vals, gain, factor):
    mean_sq = jnp.mean(raw_vals * raw_vals, axis=-1, keepdims=True)
    return raw_vals * lax.rsqrt(mean_sq + epsilon) * gain * factor


def exchange(blocks, axis):
    return lax.all_to_all(blocks, axis, 0, 0)


def gather_all(block, axis):
    count = lax.axis_size(axis)
    return exchange(jnp.broadcast_to(block[None], (count,) + block.shape), axis)


SEQ = ("chip", "core")
SWAP = [(0, 1), (1, 0)]


def gather_kernel(chips, x_ref, out_ref, local_sem, send_sem, recv_sem, fwd_send, fwd_recv):
    chip = lax.axis_index("chip")
    core = lax.axis_index("core")
    uly = lax.axis_index("uly")
    other = 1 - core
    mesh_ids = pl.DeviceIdType.MESH
    barrier = pltpu.get_barrier_semaphore()
    for d in range(1, chips):
        peer = (lax.rem(chip + d, chips), core, uly)
        pl.semaphore_signal(barrier, 1, device_id=peer, device_id_type=mesh_ids)
    pl.semaphore_signal(barrier, 1, device_id=(chip, other, uly), device_id_type=mesh_ids)
    pl.semaphore_wait(barrier, chips)
    mine = chip * 2 + core
    local = pltpu.make_async_copy(x_ref, out_ref.at[:, pl.ds(mine, 1)], local_sem)
    local.start()
    sends = {}
    for d in range(1, chips):
        sends[d] = pltpu.make_async_remote_copy(
            src_ref=x_ref,
            dst_ref=out_ref.at[:, pl.ds(mine, 1)],
            send_sem=send_sem.at[d],
            recv_sem=recv_sem.at[d],
            device_id=(lax.rem(chip + d, chips), core, uly),
            device_id_type=mesh_ids,
        )
        sends[d].start()
    forwards = [
        pltpu.make_async_remote_copy(
            src_ref=x_ref,
            dst_ref=out_ref.at[:, pl.ds(mine, 1)],
            send_sem=fwd_send.at[0],
            recv_sem=fwd_recv.at[0],
            device_id=(chip, other, uly),
            device_id_type=mesh_ids,
        )
    ]
    forwards[0].start()
    for d in range(1, chips):
        sends[d].wait_recv()
        slot = lax.rem(chip + chips - d, chips) * 2 + core
        forward = pltpu.make_async_remote_copy(
            src_ref=out_ref.at[:, pl.ds(slot, 1)],
            dst_ref=out_ref.at[:, pl.ds(slot, 1)],
            send_sem=fwd_send.at[d],
            recv_sem=fwd_recv.at[d],
            device_id=(chip, other, uly),
            device_id_type=mesh_ids,
        )
        forward.start()
        forwards.append(forward)
    for d in range(1, chips):
        sends[d].wait_send()
    for forward in forwards:
        forward.wait()
    local.wait()


def gather_seq(block):
    chips = lax.axis_size("chip")
    spec = pl.BlockSpec(memory_space=pltpu.VMEM)
    return pl.pallas_call(
        functools.partial(gather_kernel, chips),
        out_shape=jax.ShapeDtypeStruct((block.shape[0], 2 * chips) + block.shape[1:], block.dtype),
        in_specs=[spec],
        out_specs=spec,
        scratch_shapes=[
            pltpu.SemaphoreType.DMA(()),
            pltpu.SemaphoreType.DMA((chips,)),
            pltpu.SemaphoreType.DMA((chips,)),
            pltpu.SemaphoreType.DMA((chips,)),
            pltpu.SemaphoreType.DMA((chips,)),
        ],
        compiler_params=pltpu.CompilerParams(collective_id=0, has_side_effects=True),
    )(block[:, None])


def reduce_seq(blocks):
    chips = blocks.shape[0] // 2
    split = blocks.reshape((chips, 2) + blocks.shape[1:])
    core = lax.axis_index("core")
    keep = jnp.take(split, core, axis=1)
    send = jnp.take(split, 1 - core, axis=1)
    pair = (keep.astype(jnp.float32) + lax.ppermute(send, "core", SWAP).astype(jnp.float32))
    return jnp.sum(exchange(pair.astype(jnp.bfloat16), "chip").astype(jnp.float32), axis=0)


def attend_block(
    queries, key_block, value_block, grad_block, query_pos, key_pos, query_seg, key_seg
):
    scores = jnp.einsum("bhge,lhe->hgbl", queries, key_block, preferred_element_type=jnp.float32)
    allowed = (
        (key_pos[None, :] <= query_pos[:, None])
        & (key_pos[None, :] > query_pos[:, None] - WINDOW)
        & (key_seg[None, :] == query_seg[:, None])
    )
    exp_scores = jnp.where(allowed[None, None], jnp.exp(scores), 0.0)
    probs = exp_scores / jnp.sum(exp_scores, axis=-1, keepdims=True)
    weights = probs.astype(jnp.bfloat16)
    attended = jnp.einsum(
        "hgbl,lhe->bhge", weights, value_block, preferred_element_type=jnp.float32
    ).astype(jnp.bfloat16)
    dprob = jnp.einsum(
        "bhge,lhe->hgbl", grad_block, value_block, preferred_element_type=jnp.float32
    )
    delta_row = jnp.sum(probs * dprob, axis=-1, keepdims=True)
    dscore = (probs * (dprob - delta_row)).astype(jnp.bfloat16)
    dquery = jnp.einsum("hgbl,lhe->bhge", dscore, key_block, preferred_element_type=jnp.float32)
    dkey = jnp.einsum("hgbl,bhge->lhe", dscore, queries, preferred_element_type=jnp.float32)
    dvalue = jnp.einsum("hgbl,bhge->lhe", weights, grad_block, preferred_element_type=jnp.float32)
    return (attended, dquery, dkey, dvalue)


def attention_kernel(q_ref, do_ref, k_ref, v_ref, qseg_ref, kseg_ref, out_ref, dq_ref, dkv_ref):
    rows = q_ref.shape[0]
    block = 256
    span = block + WINDOW
    dkv_ref[...] = jnp.zeros(dkv_ref.shape, jnp.float32)
    nt = (((1,), (1,)), ((), ()))
    tn = (((0,), (0,)), ((), ()))
    for b in range(rows // block):
        r0 = b * block
        k = k_ref[pl.ds(r0, span), :]
        v = v_ref[pl.ds(r0, span), :]
        row = lax.broadcasted_iota(jnp.int32, (block, span), 0)
        col = lax.broadcasted_iota(jnp.int32, (block, span), 1)
        allowed = (col <= row + WINDOW) & (col > row)
        allowed = allowed & (qseg_ref[pl.ds(r0, block), :] == kseg_ref[:, pl.ds(r0, span)])
        dk_acc = jnp.zeros((span, HD), jnp.float32)
        dv_acc = jnp.zeros((span, HD), jnp.float32)
        for g in range(2):
            q = q_ref[pl.ds(r0, block), pl.ds(g * HD, HD)]
            do = do_ref[pl.ds(r0, block), pl.ds(g * HD, HD)]
            scores = lax.dot_general(q, k, nt, preferred_element_type=jnp.float32)
            exp_scores = jnp.where(allowed, jnp.exp(scores), 0.0)
            probs = exp_scores / jnp.sum(exp_scores, axis=1, keepdims=True)
            weights = probs.astype(jnp.bfloat16)
            out_ref[pl.ds(r0, block), pl.ds(g * HD, HD)] = jnp.dot(
                weights, v, preferred_element_type=jnp.float32
            ).astype(out_ref.dtype)
            dprob = lax.dot_general(do, v, nt, preferred_element_type=jnp.float32)
            delta_row = jnp.sum(probs * dprob, axis=1, keepdims=True)
            dscore = (probs * (dprob - delta_row)).astype(jnp.bfloat16)
            dq_ref[pl.ds(r0, block), pl.ds(g * HD, HD)] = jnp.dot(
                dscore, k, preferred_element_type=jnp.float32
            )
            dk_acc = dk_acc + lax.dot_general(dscore, q, tn, preferred_element_type=jnp.float32)
            dv_acc = dv_acc + lax.dot_general(weights, do, tn, preferred_element_type=jnp.float32)
        dkv_ref[0, pl.ds(r0, span), :] += dk_acc
        dkv_ref[1, pl.ds(r0, span), :] += dv_acc


def attend(queries, grad_out, keys, values, query_seg, key_seg):
    rows = queries.shape[0]
    spec = pl.BlockSpec(memory_space=pltpu.VMEM)
    return pl.pallas_call(
        attention_kernel,
        out_shape=(
            jax.ShapeDtypeStruct((rows, 2 * HD), jnp.bfloat16),
            jax.ShapeDtypeStruct((rows, 2 * HD), jnp.float32),
            jax.ShapeDtypeStruct((2, keys.shape[0], HD), jnp.float32),
        ),
        in_specs=[spec] * 6,
        out_specs=(spec, spec, spec),
        cost_estimate=pl.CostEstimate(
            flops=12 * rows * (rows + WINDOW) * HD * 2, transcendentals=2 * rows * (rows + WINDOW),
            bytes_accessed=16 * rows * HD * 4,
        ),
    )(queries, grad_out, keys, values, query_seg, key_seg)


def body(normed, q_raw, key_weight, value_weight, q_gain, k_gain, segment_ids, grad_out):
    rows_here = normed.shape[0]
    feats = normed.shape[1]
    heads_here = q_raw.shape[1] // (2 * HD)
    n_seq = lax.axis_size(SEQ)
    n_uly = lax.axis_size("uly")
    col_block = key_weight.shape[1]
    seq_index = lax.axis_index(SEQ)
    base_row = seq_index * rows_here
    pair_t = jnp.stack([key_weight.T, value_weight.T])
    weight_t = gather_seq(pair_t).reshape(2, n_seq * col_block, feats)
    terms = lax.dot_general(
        normed, weight_t, (((1,), (2,)), ((), ())), preferred_element_type=jnp.float32
    ).astype(jnp.bfloat16)
    terms = terms.reshape(rows_here, 2, n_uly, heads_here * HD).transpose(2, 0, 1, 3)
    received = exchange(terms, "uly")
    raw_pair = jnp.sum(received.astype(jnp.float32), axis=0)
    key_raw = raw_pair[:, 0]
    value_raw = raw_pair[:, 1]
    key_in = key_raw.reshape(rows_here, heads_here, HD)
    keys_bf = normalize(key_in, k_gain, 1.0).astype(jnp.bfloat16)
    values_bf = value_raw.reshape(rows_here, heads_here, HD).astype(jnp.bfloat16)
    query_in = q_raw.astype(jnp.float32).reshape(rows_here, heads_here, 2, HD)
    queries = normalize(query_in, q_gain, query_scale).astype(jnp.bfloat16)
    grad_heads = grad_out.reshape(rows_here, heads_here, 2, HD)
    stacked = jnp.stack([keys_bf, values_bf])
    behind = from_behind(stacked, SEQ, 1)
    extended = jnp.concatenate([behind, stacked], axis=1).reshape(2, WINDOW + rows_here, HD)
    seg_pad = jnp.concatenate([jnp.full((WINDOW,), -1, jnp.int32), segment_ids])
    query_seg = lax.dynamic_slice_in_dim(segment_ids, base_row, rows_here, 0)
    key_seg = lax.dynamic_slice_in_dim(seg_pad, base_row, WINDOW + rows_here, 0)
    attention, dquery, grad_acc = attend(
        queries.reshape(rows_here, 2 * HD),
        grad_out,
        extended[0],
        extended[1],
        query_seg.reshape(rows_here, 1),
        key_seg.reshape(1, WINDOW + rows_here),
    )
    dquery = dquery.reshape(rows_here, heads_here, 2, HD)
    grad_acc = grad_acc.reshape(2, WINDOW + rows_here, heads_here, HD)
    own_grads = grad_acc[:, WINDOW:]
    offset_row = 0
    distance = 1
    first_row = max(0, distance * rows_here - WINDOW)
    piece_rows = rows_here - first_row
    outgoing = grad_acc[:, offset_row : offset_row + piece_rows]
    returned = from_behind(outgoing.astype(jnp.bfloat16), SEQ, -distance).astype(outgoing.dtype)
    own_grads = own_grads.at[:, first_row:].add(returned)
    _, pull_query = jax.vjp(lambda raw_vals: normalize(raw_vals, q_gain, query_scale), query_in)
    grad_q = pull_query(dquery)[0].astype(jnp.bfloat16).reshape(rows_here, 2 * heads_here * HD)
    _, pull_key = jax.vjp(lambda raw_vals: normalize(raw_vals, k_gain, 1.0), key_in)
    key_grad = pull_key(own_grads[0])[0].astype(jnp.bfloat16).reshape(rows_here, heads_here * HD)
    value_grad = own_grads[1].astype(jnp.bfloat16).reshape(rows_here, heads_here * HD)
    grads_all = gather_all(jnp.stack([key_grad, value_grad], axis=1), "uly")
    weight_heads = weight_t.reshape(2, n_uly, heads_here * HD, feats)
    grad_normed = jnp.einsum(
        "htkc,khcf->tf", grads_all, weight_heads, preferred_element_type=jnp.float32
    ).astype(jnp.bfloat16)
    weight_part = jnp.einsum(
        "tf,htkc->fkhc", normed, grads_all, preferred_element_type=jnp.float32
    ).astype(jnp.bfloat16)
    to_owner = weight_part.reshape(feats, 2, n_seq, col_block).transpose(2, 0, 1, 3)
    summed = reduce_seq(to_owner)
    grad_key_weight = summed[:, 0]
    grad_value_weight = summed[:, 1]
    return (attention, grad_normed, grad_q, grad_key_weight, grad_value_weight)


def solution(mesh):
    n_seq, n_uly = mesh.shape["seq"], mesh.shape["uly"]
    fine = jax.sharding.Mesh(mesh.devices.reshape(n_seq // 2, 2, n_uly), ("chip", "core", "uly"))
    return jax.shard_map(
        body,
        mesh=fine,
        in_specs=(
            P(SEQ, "uly"),
            P(SEQ, "uly"),
            P("uly", SEQ),
            P("uly", SEQ),
            P(),
            P(),
            P(),
            P(SEQ, "uly"),
        ),
        out_specs=(
            P(SEQ, "uly"),
            P(SEQ, "uly"),
            P(SEQ, "uly"),
            P("uly", SEQ),
            P("uly", SEQ),
        ),
        check_vma=False,
    )
```

```python
import functools

import jax
import jax.numpy as jnp
from jax import lax
from jax.experimental import pallas as pl
from jax.experimental.pallas import tpu as pltpu
from jax.sharding import PartitionSpec as P

HD = 128
WINDOW = 1024


epsilon = 1e-06
query_scale = 168.0 ** (-0.5)


def from_behind(array, axis, by):
    devices = lax.axis_size(axis)
    pairs = [(i, i + by) for i in range(devices) if 0 <= i + by < devices]
    return lax.ppermute(array, axis, pairs)


def normalize(raw_vals, gain, factor):
    mean_sq = jnp.mean(raw_vals * raw_vals, axis=-1, keepdims=True)
    return raw_vals * lax.rsqrt(mean_sq + epsilon) * gain * factor


def exchange(blocks, axis):
    return lax.all_to_all(blocks, axis, 0, 0)


def gather_all(block, axis):
    count = lax.axis_size(axis)
    return exchange(jnp.broadcast_to(block[None], (count,) + block.shape), axis)


SEQ = ("chip", "core")
SWAP = [(0, 1), (1, 0)]


def gather_kernel(chips, x_ref, out_ref, local_sem, send_sem, recv_sem, fwd_send, fwd_recv):
    chip = lax.axis_index("chip")
    core = lax.axis_index("core")
    uly = lax.axis_index("uly")
    other = 1 - core
    mesh_ids = pl.DeviceIdType.MESH
    barrier = pltpu.get_barrier_semaphore()
    for d in range(1, chips):
        peer = (lax.rem(chip + d, chips), core, uly)
        pl.semaphore_signal(barrier, 1, device_id=peer, device_id_type=mesh_ids)
    pl.semaphore_signal(barrier, 1, device_id=(chip, other, uly), device_id_type=mesh_ids)
    pl.semaphore_wait(barrier, chips)
    mine = chip * 2 + core
    local = pltpu.make_async_copy(x_ref, out_ref.at[:, pl.ds(mine, 1)], local_sem)
    local.start()
    sends = {}
    for d in range(1, chips):
        sends[d] = pltpu.make_async_remote_copy(
            src_ref=x_ref,
            dst_ref=out_ref.at[:, pl.ds(mine, 1)],
            send_sem=send_sem.at[d],
            recv_sem=recv_sem.at[d],
            device_id=(lax.rem(chip + d, chips), core, uly),
            device_id_type=mesh_ids,
        )
        sends[d].start()
    forwards = [
        pltpu.make_async_remote_copy(
            src_ref=x_ref,
            dst_ref=out_ref.at[:, pl.ds(mine, 1)],
            send_sem=fwd_send.at[0],
            recv_sem=fwd_recv.at[0],
            device_id=(chip, other, uly),
            device_id_type=mesh_ids,
        )
    ]
    forwards[0].start()
    for d in range(1, chips):
        sends[d].wait_recv()
        slot = lax.rem(chip + chips - d, chips) * 2 + core
        forward = pltpu.make_async_remote_copy(
            src_ref=out_ref.at[:, pl.ds(slot, 1)],
            dst_ref=out_ref.at[:, pl.ds(slot, 1)],
            send_sem=fwd_send.at[d],
            recv_sem=fwd_recv.at[d],
            device_id=(chip, other, uly),
            device_id_type=mesh_ids,
        )
        forward.start()
        forwards.append(forward)
    for d in range(1, chips):
        sends[d].wait_send()
    for forward in forwards:
        forward.wait()
    local.wait()


def gather_seq(block):
    chips = lax.axis_size("chip")
    spec = pl.BlockSpec(memory_space=pltpu.VMEM)
    return pl.pallas_call(
        functools.partial(gather_kernel, chips),
        out_shape=jax.ShapeDtypeStruct((block.shape[0], 2 * chips) + block.shape[1:], block.dtype),
        in_specs=[spec],
        out_specs=spec,
        scratch_shapes=[
            pltpu.SemaphoreType.DMA(()),
            pltpu.SemaphoreType.DMA((chips,)),
            pltpu.SemaphoreType.DMA((chips,)),
            pltpu.SemaphoreType.DMA((chips,)),
            pltpu.SemaphoreType.DMA((chips,)),
        ],
        compiler_params=pltpu.CompilerParams(collective_id=0, has_side_effects=True),
    )(block[:, None])


def reduce_seq(blocks):
    chips = blocks.shape[1] // 2
    split = blocks.reshape((blocks.shape[0], chips, 2) + blocks.shape[2:])
    core = lax.axis_index("core")
    keep = jnp.take(split, core, axis=2)
    send = jnp.take(split, 1 - core, axis=2)
    pair = (keep.astype(jnp.float32) + lax.ppermute(send, "core", SWAP).astype(jnp.float32))
    pair = pair.astype(jnp.bfloat16).transpose(1, 0, 2, 3)
    return jnp.sum(exchange(pair, "chip").astype(jnp.float32), axis=0)


def attend_block(
    queries, key_block, value_block, grad_block, query_pos, key_pos, query_seg, key_seg
):
    scores = jnp.einsum("bhge,lhe->hgbl", queries, key_block, preferred_element_type=jnp.float32)
    allowed = (
        (key_pos[None, :] <= query_pos[:, None])
        & (key_pos[None, :] > query_pos[:, None] - WINDOW)
        & (key_seg[None, :] == query_seg[:, None])
    )
    exp_scores = jnp.where(allowed[None, None], jnp.exp(scores), 0.0)
    probs = exp_scores / jnp.sum(exp_scores, axis=-1, keepdims=True)
    weights = probs.astype(jnp.bfloat16)
    attended = jnp.einsum(
        "hgbl,lhe->bhge", weights, value_block, preferred_element_type=jnp.float32
    ).astype(jnp.bfloat16)
    dprob = jnp.einsum(
        "bhge,lhe->hgbl", grad_block, value_block, preferred_element_type=jnp.float32
    )
    delta_row = jnp.sum(probs * dprob, axis=-1, keepdims=True)
    dscore = (probs * (dprob - delta_row)).astype(jnp.bfloat16)
    dquery = jnp.einsum("hgbl,lhe->bhge", dscore, key_block, preferred_element_type=jnp.float32)
    dkey = jnp.einsum("hgbl,bhge->lhe", dscore, queries, preferred_element_type=jnp.float32)
    dvalue = jnp.einsum("hgbl,bhge->lhe", weights, grad_block, preferred_element_type=jnp.float32)
    return (attended, dquery, dkey, dvalue)


def attention_kernel(q_ref, do_ref, k_ref, v_ref, qseg_ref, kseg_ref, out_ref, dq_ref, dkv_ref):
    rows = q_ref.shape[0]
    block = 256
    span = block + WINDOW
    dkv_ref[...] = jnp.zeros(dkv_ref.shape, jnp.float32)
    nt = (((1,), (1,)), ((), ()))
    tn = (((0,), (0,)), ((), ()))
    for b in range(rows // block):
        r0 = b * block
        k = k_ref[pl.ds(r0, span), :]
        v = v_ref[pl.ds(r0, span), :]
        row = lax.broadcasted_iota(jnp.int32, (block, span), 0)
        col = lax.broadcasted_iota(jnp.int32, (block, span), 1)
        allowed = (col <= row + WINDOW) & (col > row)
        allowed = allowed & (qseg_ref[pl.ds(r0, block), :] == kseg_ref[:, pl.ds(r0, span)])
        dk_acc = jnp.zeros((span, HD), jnp.float32)
        dv_acc = jnp.zeros((span, HD), jnp.float32)
        for g in range(2):
            q = q_ref[pl.ds(r0, block), pl.ds(g * HD, HD)]
            do = do_ref[pl.ds(r0, block), pl.ds(g * HD, HD)]
            scores = lax.dot_general(q, k, nt, preferred_element_type=jnp.float32)
            exp_scores = jnp.where(allowed, jnp.exp(scores), 0.0)
            probs = exp_scores / jnp.sum(exp_scores, axis=1, keepdims=True)
            weights = probs.astype(jnp.bfloat16)
            out_ref[pl.ds(r0, block), pl.ds(g * HD, HD)] = jnp.dot(
                weights, v, preferred_element_type=jnp.float32
            ).astype(out_ref.dtype)
            dprob = lax.dot_general(do, v, nt, preferred_element_type=jnp.float32)
            delta_row = jnp.sum(probs * dprob, axis=1, keepdims=True)
            dscore = (probs * (dprob - delta_row)).astype(jnp.bfloat16)
            dq_ref[pl.ds(r0, block), pl.ds(g * HD, HD)] = jnp.dot(
                dscore, k, preferred_element_type=jnp.float32
            )
            dk_acc = dk_acc + lax.dot_general(dscore, q, tn, preferred_element_type=jnp.float32)
            dv_acc = dv_acc + lax.dot_general(weights, do, tn, preferred_element_type=jnp.float32)
        dkv_ref[0, pl.ds(r0, span), :] += dk_acc
        dkv_ref[1, pl.ds(r0, span), :] += dv_acc


def attend(queries, grad_out, keys, values, query_seg, key_seg):
    rows = queries.shape[0]
    spec = pl.BlockSpec(memory_space=pltpu.VMEM)
    return pl.pallas_call(
        attention_kernel,
        out_shape=(
            jax.ShapeDtypeStruct((rows, 2 * HD), jnp.bfloat16),
            jax.ShapeDtypeStruct((rows, 2 * HD), jnp.float32),
            jax.ShapeDtypeStruct((2, keys.shape[0], HD), jnp.float32),
        ),
        in_specs=[spec] * 6,
        out_specs=(spec, spec, spec),
        cost_estimate=pl.CostEstimate(
            flops=12 * rows * (rows + WINDOW) * HD * 2, transcendentals=2 * rows * (rows + WINDOW),
            bytes_accessed=16 * rows * HD * 4,
        ),
    )(queries, grad_out, keys, values, query_seg, key_seg)


def body(normed, q_raw, key_weight, value_weight, q_gain, k_gain, segment_ids, grad_out):
    rows_here = normed.shape[0]
    feats = normed.shape[1]
    heads_here = q_raw.shape[1] // (2 * HD)
    n_seq = lax.axis_size(SEQ)
    n_uly = lax.axis_size("uly")
    col_block = key_weight.shape[1]
    seq_index = lax.axis_index(SEQ)
    base_row = seq_index * rows_here
    pair_t = jnp.stack([key_weight.T, value_weight.T])
    weight_t = gather_seq(pair_t).reshape(2, n_seq * col_block, feats)
    terms = lax.dot_general(
        normed, weight_t, (((1,), (2,)), ((), ())), preferred_element_type=jnp.float32
    ).astype(jnp.bfloat16)
    terms = terms.reshape(rows_here, 2, n_uly, heads_here * HD).transpose(2, 0, 1, 3)
    received = exchange(terms, "uly")
    raw_pair = jnp.sum(received.astype(jnp.float32), axis=0)
    key_raw = raw_pair[:, 0]
    value_raw = raw_pair[:, 1]
    key_in = key_raw.reshape(rows_here, heads_here, HD)
    keys_bf = normalize(key_in, k_gain, 1.0).astype(jnp.bfloat16)
    values_bf = value_raw.reshape(rows_here, heads_here, HD).astype(jnp.bfloat16)
    query_in = q_raw.astype(jnp.float32).reshape(rows_here, heads_here, 2, HD)
    queries = normalize(query_in, q_gain, query_scale).astype(jnp.bfloat16)
    grad_heads = grad_out.reshape(rows_here, heads_here, 2, HD)
    stacked = jnp.stack([keys_bf, values_bf])
    behind = from_behind(stacked, SEQ, 1)
    extended = jnp.concatenate([behind, stacked], axis=1).reshape(2, WINDOW + rows_here, HD)
    seg_pad = jnp.concatenate([jnp.full((WINDOW,), -1, jnp.int32), segment_ids])
    query_seg = lax.dynamic_slice_in_dim(segment_ids, base_row, rows_here, 0)
    key_seg = lax.dynamic_slice_in_dim(seg_pad, base_row, WINDOW + rows_here, 0)
    attention, dquery, grad_acc = attend(
        queries.reshape(rows_here, 2 * HD),
        grad_out,
        extended[0],
        extended[1],
        query_seg.reshape(rows_here, 1),
        key_seg.reshape(1, WINDOW + rows_here),
    )
    dquery = dquery.reshape(rows_here, heads_here, 2, HD)
    grad_acc = grad_acc.reshape(2, WINDOW + rows_here, heads_here, HD)
    own_grads = grad_acc[:, WINDOW:]
    offset_row = 0
    distance = 1
    first_row = max(0, distance * rows_here - WINDOW)
    piece_rows = rows_here - first_row
    outgoing = grad_acc[:, offset_row : offset_row + piece_rows]
    returned = from_behind(outgoing.astype(jnp.bfloat16), SEQ, -distance).astype(outgoing.dtype)
    own_grads = own_grads.at[:, first_row:].add(returned)
    _, pull_query = jax.vjp(lambda raw_vals: normalize(raw_vals, q_gain, query_scale), query_in)
    grad_q = pull_query(dquery)[0].astype(jnp.bfloat16).reshape(rows_here, 2 * heads_here * HD)
    _, pull_key = jax.vjp(lambda raw_vals: normalize(raw_vals, k_gain, 1.0), key_in)
    key_grad = pull_key(own_grads[0])[0].astype(jnp.bfloat16).reshape(rows_here, heads_here * HD)
    value_grad = own_grads[1].astype(jnp.bfloat16).reshape(rows_here, heads_here * HD)
    grads_all = gather_all(jnp.stack([key_grad, value_grad], axis=1), "uly")
    weight_heads = weight_t.reshape(2, n_uly, heads_here * HD, feats)
    grad_normed = jnp.einsum(
        "htkc,khcf->tf", grads_all, weight_heads, preferred_element_type=jnp.float32
    ).astype(jnp.bfloat16)
    weight_part = jnp.einsum(
        "htkc,tf->khcf", grads_all, normed, preferred_element_type=jnp.float32
    ).astype(jnp.bfloat16)
    summed = reduce_seq(weight_part.reshape(2, n_seq, col_block, feats))
    grad_key_weight = summed[0].T
    grad_value_weight = summed[1].T
    return (attention, grad_normed, grad_q, grad_key_weight, grad_value_weight)


def solution(mesh):
    n_seq, n_uly = mesh.shape["seq"], mesh.shape["uly"]
    fine = jax.sharding.Mesh(mesh.devices.reshape(n_seq // 2, 2, n_uly), ("chip", "core", "uly"))
    return jax.shard_map(
        body,
        mesh=fine,
        in_specs=(
            P(SEQ, "uly"),
            P(SEQ, "uly"),
            P("uly", SEQ),
            P("uly", SEQ),
            P(),
            P(),
            P(),
            P(SEQ, "uly"),
        ),
        out_specs=(
            P(SEQ, "uly"),
            P(SEQ, "uly"),
            P(SEQ, "uly"),
            P("uly", SEQ),
            P("uly", SEQ),
        ),
        check_vma=False,
    )
```

```python
import functools

import jax
import jax.numpy as jnp
from jax import lax
from jax.experimental import pallas as pl
from jax.experimental.pallas import tpu as pltpu
from jax.sharding import PartitionSpec as P

HD = 128
WINDOW = 1024


epsilon = 1e-06
query_scale = 168.0 ** (-0.5)


def from_behind(array, axis, by):
    devices = lax.axis_size(axis)
    pairs = [(i, i + by) for i in range(devices) if 0 <= i + by < devices]
    return lax.ppermute(array, axis, pairs)


def normalize(raw_vals, gain, factor):
    mean_sq = jnp.mean(raw_vals * raw_vals, axis=-1, keepdims=True)
    return raw_vals * lax.rsqrt(mean_sq + epsilon) * gain * factor


def exchange(blocks, axis):
    return lax.all_to_all(blocks, axis, 0, 0)


def gather_all(block, axis):
    count = lax.axis_size(axis)
    return exchange(jnp.broadcast_to(block[None], (count,) + block.shape), axis)


SEQ = ("chip", "core")
SWAP = [(0, 1), (1, 0)]


def gather_kernel(chips, x_ref, out_ref, local_sem, send_sem, recv_sem, fwd_send, fwd_recv):
    chip = lax.axis_index("chip")
    core = lax.axis_index("core")
    uly = lax.axis_index("uly")
    other = 1 - core
    mesh_ids = pl.DeviceIdType.MESH
    barrier = pltpu.get_barrier_semaphore()
    for d in range(1, chips):
        peer = (lax.rem(chip + d, chips), core, uly)
        pl.semaphore_signal(barrier, 1, device_id=peer, device_id_type=mesh_ids)
    pl.semaphore_signal(barrier, 1, device_id=(chip, other, uly), device_id_type=mesh_ids)
    pl.semaphore_wait(barrier, chips)
    mine = chip * 2 + core
    local = pltpu.make_async_copy(x_ref, out_ref.at[:, pl.ds(mine, 1)], local_sem)
    local.start()
    sends = {}
    for d in range(1, chips):
        sends[d] = pltpu.make_async_remote_copy(
            src_ref=x_ref,
            dst_ref=out_ref.at[:, pl.ds(mine, 1)],
            send_sem=send_sem.at[d],
            recv_sem=recv_sem.at[d],
            device_id=(lax.rem(chip + d, chips), core, uly),
            device_id_type=mesh_ids,
        )
        sends[d].start()
    forwards = [
        pltpu.make_async_remote_copy(
            src_ref=x_ref,
            dst_ref=out_ref.at[:, pl.ds(mine, 1)],
            send_sem=fwd_send.at[0],
            recv_sem=fwd_recv.at[0],
            device_id=(chip, other, uly),
            device_id_type=mesh_ids,
        )
    ]
    forwards[0].start()
    for d in range(1, chips):
        sends[d].wait_recv()
        slot = lax.rem(chip + chips - d, chips) * 2 + core
        forward = pltpu.make_async_remote_copy(
            src_ref=out_ref.at[:, pl.ds(slot, 1)],
            dst_ref=out_ref.at[:, pl.ds(slot, 1)],
            send_sem=fwd_send.at[d],
            recv_sem=fwd_recv.at[d],
            device_id=(chip, other, uly),
            device_id_type=mesh_ids,
        )
        forward.start()
        forwards.append(forward)
    for d in range(1, chips):
        sends[d].wait_send()
    for forward in forwards:
        forward.wait()
    local.wait()


def gather_seq(block):
    chips = lax.axis_size("chip")
    spec = pl.BlockSpec(memory_space=pltpu.VMEM)
    return pl.pallas_call(
        functools.partial(gather_kernel, chips),
        out_shape=jax.ShapeDtypeStruct((block.shape[0], 2 * chips) + block.shape[1:], block.dtype),
        in_specs=[spec],
        out_specs=spec,
        scratch_shapes=[
            pltpu.SemaphoreType.DMA(()),
            pltpu.SemaphoreType.DMA((chips,)),
            pltpu.SemaphoreType.DMA((chips,)),
            pltpu.SemaphoreType.DMA((chips,)),
            pltpu.SemaphoreType.DMA((chips,)),
        ],
        compiler_params=pltpu.CompilerParams(collective_id=0, has_side_effects=True),
    )(block[:, None])


def uly_kernel(count, scatter, x_ref, out_ref, local_sem, send_sem, recv_sem):
    chip = lax.axis_index("chip")
    core = lax.axis_index("core")
    me = lax.axis_index("uly")
    mesh_ids = pl.DeviceIdType.MESH
    barrier = pltpu.get_barrier_semaphore()
    for d in range(1, count):
        peer = (chip, core, lax.rem(me + d, count))
        pl.semaphore_signal(barrier, 1, device_id=peer, device_id_type=mesh_ids)
    pl.semaphore_wait(barrier, count - 1)
    local = pltpu.make_async_copy(x_ref.at[me] if scatter else x_ref, out_ref.at[me], local_sem)
    local.start()
    sends = []
    for d in range(1, count):
        target = lax.rem(me + d, count)
        send = pltpu.make_async_remote_copy(
            src_ref=x_ref.at[target] if scatter else x_ref,
            dst_ref=out_ref.at[me],
            send_sem=send_sem.at[d],
            recv_sem=recv_sem.at[d],
            device_id=(chip, core, target),
            device_id_type=mesh_ids,
        )
        send.start()
        sends.append(send)
    for send in sends:
        send.wait()
    local.wait()


def exchange_uly(x, scatter, kernel_id):
    count = lax.axis_size("uly")
    block = x.shape[1:] if scatter else x.shape
    spec = pl.BlockSpec(memory_space=pltpu.VMEM)
    return pl.pallas_call(
        functools.partial(uly_kernel, count, scatter),
        out_shape=jax.ShapeDtypeStruct((count,) + block, x.dtype),
        in_specs=[spec],
        out_specs=spec,
        scratch_shapes=[
            pltpu.SemaphoreType.DMA(()),
            pltpu.SemaphoreType.DMA((count,)),
            pltpu.SemaphoreType.DMA((count,)),
        ],
        compiler_params=pltpu.CompilerParams(collective_id=kernel_id, has_side_effects=True),
    )(x)


def reduce_seq(blocks):
    chips = blocks.shape[1] // 2
    split = blocks.reshape((blocks.shape[0], chips, 2) + blocks.shape[2:])
    core = lax.axis_index("core")
    keep = jnp.take(split, core, axis=2)
    send = jnp.take(split, 1 - core, axis=2)
    pair = (keep.astype(jnp.float32) + lax.ppermute(send, "core", SWAP).astype(jnp.float32))
    pair = pair.astype(jnp.bfloat16).transpose(1, 0, 2, 3)
    return jnp.sum(exchange(pair, "chip").astype(jnp.float32), axis=0)


def attend_block(
    queries, key_block, value_block, grad_block, query_pos, key_pos, query_seg, key_seg
):
    scores = jnp.einsum("bhge,lhe->hgbl", queries, key_block, preferred_element_type=jnp.float32)
    allowed = (
        (key_pos[None, :] <= query_pos[:, None])
        & (key_pos[None, :] > query_pos[:, None] - WINDOW)
        & (key_seg[None, :] == query_seg[:, None])
    )
    exp_scores = jnp.where(allowed[None, None], jnp.exp(scores), 0.0)
    probs = exp_scores / jnp.sum(exp_scores, axis=-1, keepdims=True)
    weights = probs.astype(jnp.bfloat16)
    attended = jnp.einsum(
        "hgbl,lhe->bhge", weights, value_block, preferred_element_type=jnp.float32
    ).astype(jnp.bfloat16)
    dprob = jnp.einsum(
        "bhge,lhe->hgbl", grad_block, value_block, preferred_element_type=jnp.float32
    )
    delta_row = jnp.sum(probs * dprob, axis=-1, keepdims=True)
    dscore = (probs * (dprob - delta_row)).astype(jnp.bfloat16)
    dquery = jnp.einsum("hgbl,lhe->bhge", dscore, key_block, preferred_element_type=jnp.float32)
    dkey = jnp.einsum("hgbl,bhge->lhe", dscore, queries, preferred_element_type=jnp.float32)
    dvalue = jnp.einsum("hgbl,bhge->lhe", weights, grad_block, preferred_element_type=jnp.float32)
    return (attended, dquery, dkey, dvalue)


def attention_kernel(q_ref, do_ref, k_ref, v_ref, qseg_ref, kseg_ref, out_ref, dq_ref, dkv_ref):
    rows = q_ref.shape[0]
    block = 256
    span = block + WINDOW
    dkv_ref[...] = jnp.zeros(dkv_ref.shape, jnp.float32)
    nt = (((1,), (1,)), ((), ()))
    tn = (((0,), (0,)), ((), ()))
    for b in range(rows // block):
        r0 = b * block
        k = k_ref[pl.ds(r0, span), :]
        v = v_ref[pl.ds(r0, span), :]
        row = lax.broadcasted_iota(jnp.int32, (block, span), 0)
        col = lax.broadcasted_iota(jnp.int32, (block, span), 1)
        allowed = (col <= row + WINDOW) & (col > row)
        allowed = allowed & (qseg_ref[pl.ds(r0, block), :] == kseg_ref[:, pl.ds(r0, span)])
        dk_acc = jnp.zeros((span, HD), jnp.float32)
        dv_acc = jnp.zeros((span, HD), jnp.float32)
        for g in range(2):
            q = q_ref[pl.ds(r0, block), pl.ds(g * HD, HD)]
            do = do_ref[pl.ds(r0, block), pl.ds(g * HD, HD)]
            scores = lax.dot_general(q, k, nt, preferred_element_type=jnp.float32)
            exp_scores = jnp.where(allowed, jnp.exp(scores), 0.0)
            probs = exp_scores / jnp.sum(exp_scores, axis=1, keepdims=True)
            weights = probs.astype(jnp.bfloat16)
            out_ref[pl.ds(r0, block), pl.ds(g * HD, HD)] = jnp.dot(
                weights, v, preferred_element_type=jnp.float32
            ).astype(out_ref.dtype)
            dprob = lax.dot_general(do, v, nt, preferred_element_type=jnp.float32)
            delta_row = jnp.sum(probs * dprob, axis=1, keepdims=True)
            dscore = (probs * (dprob - delta_row)).astype(jnp.bfloat16)
            dq_ref[pl.ds(r0, block), pl.ds(g * HD, HD)] = jnp.dot(
                dscore, k, preferred_element_type=jnp.float32
            )
            dk_acc = dk_acc + lax.dot_general(dscore, q, tn, preferred_element_type=jnp.float32)
            dv_acc = dv_acc + lax.dot_general(weights, do, tn, preferred_element_type=jnp.float32)
        dkv_ref[0, pl.ds(r0, span), :] += dk_acc
        dkv_ref[1, pl.ds(r0, span), :] += dv_acc


def attend(queries, grad_out, keys, values, query_seg, key_seg):
    rows = queries.shape[0]
    spec = pl.BlockSpec(memory_space=pltpu.VMEM)
    return pl.pallas_call(
        attention_kernel,
        out_shape=(
            jax.ShapeDtypeStruct((rows, 2 * HD), jnp.bfloat16),
            jax.ShapeDtypeStruct((rows, 2 * HD), jnp.float32),
            jax.ShapeDtypeStruct((2, keys.shape[0], HD), jnp.float32),
        ),
        in_specs=[spec] * 6,
        out_specs=(spec, spec, spec),
        cost_estimate=pl.CostEstimate(
            flops=12 * rows * (rows + WINDOW) * HD * 2, transcendentals=2 * rows * (rows + WINDOW),
            bytes_accessed=16 * rows * HD * 4,
        ),
    )(queries, grad_out, keys, values, query_seg, key_seg)


def body(normed, q_raw, key_weight, value_weight, q_gain, k_gain, segment_ids, grad_out):
    rows_here = normed.shape[0]
    feats = normed.shape[1]
    heads_here = q_raw.shape[1] // (2 * HD)
    n_seq = lax.axis_size(SEQ)
    n_uly = lax.axis_size("uly")
    col_block = key_weight.shape[1]
    seq_index = lax.axis_index(SEQ)
    base_row = seq_index * rows_here
    pair_t = jnp.stack([key_weight.T, value_weight.T])
    weight_t = gather_seq(pair_t).reshape(2, n_seq * col_block, feats)
    terms = lax.dot_general(
        normed, weight_t, (((1,), (2,)), ((), ())), preferred_element_type=jnp.float32
    ).astype(jnp.bfloat16)
    terms = terms.reshape(rows_here, 2, n_uly, heads_here * HD).transpose(2, 0, 1, 3)
    received = exchange_uly(terms.reshape(n_uly, rows_here, 2 * HD), True, 1)
    received = received.reshape(n_uly, rows_here, 2, HD)
    raw_pair = jnp.sum(received.astype(jnp.float32), axis=0)
    key_raw = raw_pair[:, 0]
    value_raw = raw_pair[:, 1]
    key_in = key_raw.reshape(rows_here, heads_here, HD)
    keys_bf = normalize(key_in, k_gain, 1.0).astype(jnp.bfloat16)
    values_bf = value_raw.reshape(rows_here, heads_here, HD).astype(jnp.bfloat16)
    query_in = q_raw.astype(jnp.float32).reshape(rows_here, heads_here, 2, HD)
    queries = normalize(query_in, q_gain, query_scale).astype(jnp.bfloat16)
    grad_heads = grad_out.reshape(rows_here, heads_here, 2, HD)
    stacked = jnp.stack([keys_bf, values_bf])
    behind = from_behind(stacked, SEQ, 1)
    extended = jnp.concatenate([behind, stacked], axis=1).reshape(2, WINDOW + rows_here, HD)
    seg_pad = jnp.concatenate([jnp.full((WINDOW,), -1, jnp.int32), segment_ids])
    query_seg = lax.dynamic_slice_in_dim(segment_ids, base_row, rows_here, 0)
    key_seg = lax.dynamic_slice_in_dim(seg_pad, base_row, WINDOW + rows_here, 0)
    attention, dquery, grad_acc = attend(
        queries.reshape(rows_here, 2 * HD),
        grad_out,
        extended[0],
        extended[1],
        query_seg.reshape(rows_here, 1),
        key_seg.reshape(1, WINDOW + rows_here),
    )
    dquery = dquery.reshape(rows_here, heads_here, 2, HD)
    grad_acc = grad_acc.reshape(2, WINDOW + rows_here, heads_here, HD)
    own_grads = grad_acc[:, WINDOW:]
    offset_row = 0
    distance = 1
    first_row = max(0, distance * rows_here - WINDOW)
    piece_rows = rows_here - first_row
    outgoing = grad_acc[:, offset_row : offset_row + piece_rows]
    returned = from_behind(outgoing.astype(jnp.bfloat16), SEQ, -distance).astype(outgoing.dtype)
    own_grads = own_grads.at[:, first_row:].add(returned)
    _, pull_query = jax.vjp(lambda raw_vals: normalize(raw_vals, q_gain, query_scale), query_in)
    grad_q = pull_query(dquery)[0].astype(jnp.bfloat16).reshape(rows_here, 2 * heads_here * HD)
    _, pull_key = jax.vjp(lambda raw_vals: normalize(raw_vals, k_gain, 1.0), key_in)
    key_grad = pull_key(own_grads[0])[0].astype(jnp.bfloat16).reshape(rows_here, heads_here * HD)
    value_grad = own_grads[1].astype(jnp.bfloat16).reshape(rows_here, heads_here * HD)
    grads_all = exchange_uly(jnp.concatenate([key_grad, value_grad], axis=1), False, 2)
    grads_all = grads_all.reshape(n_uly, rows_here, 2, heads_here * HD)
    weight_heads = weight_t.reshape(2, n_uly, heads_here * HD, feats)
    grad_normed = jnp.einsum(
        "htkc,khcf->tf", grads_all, weight_heads, preferred_element_type=jnp.float32
    ).astype(jnp.bfloat16)
    weight_part = jnp.einsum(
        "htkc,tf->khcf", grads_all, normed, preferred_element_type=jnp.float32
    ).astype(jnp.bfloat16)
    summed = reduce_seq(weight_part.reshape(2, n_seq, col_block, feats))
    grad_key_weight = summed[0].T
    grad_value_weight = summed[1].T
    return (attention, grad_normed, grad_q, grad_key_weight, grad_value_weight)


def solution(mesh):
    n_seq, n_uly = mesh.shape["seq"], mesh.shape["uly"]
    fine = jax.sharding.Mesh(mesh.devices.reshape(n_seq // 2, 2, n_uly), ("chip", "core", "uly"))
    return jax.shard_map(
        body,
        mesh=fine,
        in_specs=(
            P(SEQ, "uly"),
            P(SEQ, "uly"),
            P("uly", SEQ),
            P("uly", SEQ),
            P(),
            P(),
            P(),
            P(SEQ, "uly"),
        ),
        out_specs=(
            P(SEQ, "uly"),
            P(SEQ, "uly"),
            P(SEQ, "uly"),
            P("uly", SEQ),
            P("uly", SEQ),
        ),
        check_vma=False,
    )
```

```python
import functools

import jax
import jax.numpy as jnp
from jax import lax
from jax.experimental import pallas as pl
from jax.experimental.pallas import tpu as pltpu
from jax.sharding import PartitionSpec as P

HD = 128
WINDOW = 1024


epsilon = 1e-06
query_scale = 168.0 ** (-0.5)


def from_behind(array, axis, by):
    devices = lax.axis_size(axis)
    pairs = [(i, i + by) for i in range(devices) if 0 <= i + by < devices]
    return lax.ppermute(array, axis, pairs)


def normalize(raw_vals, gain, factor):
    mean_sq = jnp.mean(raw_vals * raw_vals, axis=-1, keepdims=True)
    return raw_vals * lax.rsqrt(mean_sq + epsilon) * gain * factor


def exchange(blocks, axis):
    return lax.all_to_all(blocks, axis, 0, 0)


def gather_all(block, axis):
    count = lax.axis_size(axis)
    return exchange(jnp.broadcast_to(block[None], (count,) + block.shape), axis)


SEQ = ("chip", "core")
SWAP = [(0, 1), (1, 0)]


def gather_kernel(chips, x_ref, out_ref, local_sem, send_sem, recv_sem, fwd_send, fwd_recv):
    chip = lax.axis_index("chip")
    core = lax.axis_index("core")
    uly = lax.axis_index("uly")
    other = 1 - core
    mesh_ids = pl.DeviceIdType.MESH
    barrier = pltpu.get_barrier_semaphore()
    for d in range(1, chips):
        peer = (lax.rem(chip + d, chips), core, uly)
        pl.semaphore_signal(barrier, 1, device_id=peer, device_id_type=mesh_ids)
    pl.semaphore_signal(barrier, 1, device_id=(chip, other, uly), device_id_type=mesh_ids)
    pl.semaphore_wait(barrier, chips)
    mine = chip * 2 + core
    local = pltpu.make_async_copy(x_ref, out_ref.at[:, pl.ds(mine, 1)], local_sem)
    local.start()
    sends = {}
    for d in range(1, chips):
        sends[d] = pltpu.make_async_remote_copy(
            src_ref=x_ref,
            dst_ref=out_ref.at[:, pl.ds(mine, 1)],
            send_sem=send_sem.at[d],
            recv_sem=recv_sem.at[d],
            device_id=(lax.rem(chip + d, chips), core, uly),
            device_id_type=mesh_ids,
        )
        sends[d].start()
    forwards = [
        pltpu.make_async_remote_copy(
            src_ref=x_ref,
            dst_ref=out_ref.at[:, pl.ds(mine, 1)],
            send_sem=fwd_send.at[0],
            recv_sem=fwd_recv.at[0],
            device_id=(chip, other, uly),
            device_id_type=mesh_ids,
        )
    ]
    forwards[0].start()
    for d in range(1, chips):
        sends[d].wait_recv()
        slot = lax.rem(chip + chips - d, chips) * 2 + core
        forward = pltpu.make_async_remote_copy(
            src_ref=out_ref.at[:, pl.ds(slot, 1)],
            dst_ref=out_ref.at[:, pl.ds(slot, 1)],
            send_sem=fwd_send.at[d],
            recv_sem=fwd_recv.at[d],
            device_id=(chip, other, uly),
            device_id_type=mesh_ids,
        )
        forward.start()
        forwards.append(forward)
    for d in range(1, chips):
        sends[d].wait_send()
    for forward in forwards:
        forward.wait()
    local.wait()


def gather_seq(block, kernel_id):
    chips = lax.axis_size("chip")
    spec = pl.BlockSpec(memory_space=pltpu.VMEM)
    return pl.pallas_call(
        functools.partial(gather_kernel, chips),
        out_shape=jax.ShapeDtypeStruct((block.shape[0], 2 * chips) + block.shape[1:], block.dtype),
        in_specs=[spec],
        out_specs=spec,
        scratch_shapes=[
            pltpu.SemaphoreType.DMA(()),
            pltpu.SemaphoreType.DMA((chips,)),
            pltpu.SemaphoreType.DMA((chips,)),
            pltpu.SemaphoreType.DMA((chips,)),
            pltpu.SemaphoreType.DMA((chips,)),
        ],
        compiler_params=pltpu.CompilerParams(collective_id=kernel_id, has_side_effects=True),
    )(block[:, None])


def reduce_seq(blocks):
    chips = blocks.shape[1] // 2
    split = blocks.reshape((blocks.shape[0], chips, 2) + blocks.shape[2:])
    core = lax.axis_index("core")
    keep = jnp.take(split, core, axis=2)
    send = jnp.take(split, 1 - core, axis=2)
    pair = (keep.astype(jnp.float32) + lax.ppermute(send, "core", SWAP).astype(jnp.float32))
    pair = pair.astype(jnp.bfloat16).transpose(1, 0, 2, 3)
    return jnp.sum(exchange(pair, "chip").astype(jnp.float32), axis=0)


def attend_block(
    queries, key_block, value_block, grad_block, query_pos, key_pos, query_seg, key_seg
):
    scores = jnp.einsum("bhge,lhe->hgbl", queries, key_block, preferred_element_type=jnp.float32)
    allowed = (
        (key_pos[None, :] <= query_pos[:, None])
        & (key_pos[None, :] > query_pos[:, None] - WINDOW)
        & (key_seg[None, :] == query_seg[:, None])
    )
    exp_scores = jnp.where(allowed[None, None], jnp.exp(scores), 0.0)
    probs = exp_scores / jnp.sum(exp_scores, axis=-1, keepdims=True)
    weights = probs.astype(jnp.bfloat16)
    attended = jnp.einsum(
        "hgbl,lhe->bhge", weights, value_block, preferred_element_type=jnp.float32
    ).astype(jnp.bfloat16)
    dprob = jnp.einsum(
        "bhge,lhe->hgbl", grad_block, value_block, preferred_element_type=jnp.float32
    )
    delta_row = jnp.sum(probs * dprob, axis=-1, keepdims=True)
    dscore = (probs * (dprob - delta_row)).astype(jnp.bfloat16)
    dquery = jnp.einsum("hgbl,lhe->bhge", dscore, key_block, preferred_element_type=jnp.float32)
    dkey = jnp.einsum("hgbl,bhge->lhe", dscore, queries, preferred_element_type=jnp.float32)
    dvalue = jnp.einsum("hgbl,bhge->lhe", weights, grad_block, preferred_element_type=jnp.float32)
    return (attended, dquery, dkey, dvalue)


def attention_kernel(q_ref, do_ref, k_ref, v_ref, qseg_ref, kseg_ref, out_ref, dq_ref, dkv_ref):
    rows = q_ref.shape[0]
    block = 256
    span = block + WINDOW
    dkv_ref[...] = jnp.zeros(dkv_ref.shape, jnp.float32)
    nt = (((1,), (1,)), ((), ()))
    tn = (((0,), (0,)), ((), ()))
    for b in range(rows // block):
        r0 = b * block
        k = k_ref[pl.ds(r0, span), :]
        v = v_ref[pl.ds(r0, span), :]
        row = lax.broadcasted_iota(jnp.int32, (block, span), 0)
        col = lax.broadcasted_iota(jnp.int32, (block, span), 1)
        allowed = (col <= row + WINDOW) & (col > row)
        allowed = allowed & (qseg_ref[pl.ds(r0, block), :] == kseg_ref[:, pl.ds(r0, span)])
        dk_acc = jnp.zeros((span, HD), jnp.float32)
        dv_acc = jnp.zeros((span, HD), jnp.float32)
        for g in range(2):
            q = q_ref[pl.ds(r0, block), pl.ds(g * HD, HD)]
            do = do_ref[pl.ds(r0, block), pl.ds(g * HD, HD)]
            scores = lax.dot_general(q, k, nt, preferred_element_type=jnp.float32)
            exp_scores = jnp.where(allowed, jnp.exp(scores), 0.0)
            probs = exp_scores / jnp.sum(exp_scores, axis=1, keepdims=True)
            weights = probs.astype(jnp.bfloat16)
            out_ref[pl.ds(r0, block), pl.ds(g * HD, HD)] = jnp.dot(
                weights, v, preferred_element_type=jnp.float32
            ).astype(out_ref.dtype)
            dprob = lax.dot_general(do, v, nt, preferred_element_type=jnp.float32)
            delta_row = jnp.sum(probs * dprob, axis=1, keepdims=True)
            dscore = (probs * (dprob - delta_row)).astype(jnp.bfloat16)
            dq_ref[pl.ds(r0, block), pl.ds(g * HD, HD)] = jnp.dot(
                dscore, k, preferred_element_type=jnp.float32
            )
            dk_acc = dk_acc + lax.dot_general(dscore, q, tn, preferred_element_type=jnp.float32)
            dv_acc = dv_acc + lax.dot_general(weights, do, tn, preferred_element_type=jnp.float32)
        dkv_ref[0, pl.ds(r0, span), :] += dk_acc
        dkv_ref[1, pl.ds(r0, span), :] += dv_acc


def attend(queries, grad_out, keys, values, query_seg, key_seg):
    rows = queries.shape[0]
    spec = pl.BlockSpec(memory_space=pltpu.VMEM)
    return pl.pallas_call(
        attention_kernel,
        out_shape=(
            jax.ShapeDtypeStruct((rows, 2 * HD), jnp.bfloat16),
            jax.ShapeDtypeStruct((rows, 2 * HD), jnp.float32),
            jax.ShapeDtypeStruct((2, keys.shape[0], HD), jnp.float32),
        ),
        in_specs=[spec] * 6,
        out_specs=(spec, spec, spec),
        cost_estimate=pl.CostEstimate(
            flops=12 * rows * (rows + WINDOW) * HD * 2, transcendentals=2 * rows * (rows + WINDOW),
            bytes_accessed=16 * rows * HD * 4,
        ),
    )(queries, grad_out, keys, values, query_seg, key_seg)


def body(normed, q_raw, key_weight, value_weight, q_gain, k_gain, segment_ids, grad_out):
    rows_here = normed.shape[0]
    feats = normed.shape[1]
    heads_here = q_raw.shape[1] // (2 * HD)
    n_seq = lax.axis_size(SEQ)
    n_uly = lax.axis_size("uly")
    col_block = key_weight.shape[1]
    seq_index = lax.axis_index(SEQ)
    base_row = seq_index * rows_here
    weight_ts = []
    raws = []
    for index, weight in enumerate((key_weight, value_weight)):
        weight_t = gather_seq(weight.T[None], index).reshape(n_seq * col_block, feats)
        weight_ts.append(weight_t)
        terms = lax.dot_general(
            normed, weight_t, (((1,), (1,)), ((), ())), preferred_element_type=jnp.float32
        ).astype(jnp.bfloat16)
        terms = terms.reshape(rows_here, n_uly, heads_here * HD).transpose(1, 0, 2)
        raws.append(jnp.sum(exchange(terms, "uly").astype(jnp.float32), axis=0))
    key_raw, value_raw = raws
    key_in = key_raw.reshape(rows_here, heads_here, HD)
    keys_bf = normalize(key_in, k_gain, 1.0).astype(jnp.bfloat16)
    values_bf = value_raw.reshape(rows_here, heads_here, HD).astype(jnp.bfloat16)
    query_in = q_raw.astype(jnp.float32).reshape(rows_here, heads_here, 2, HD)
    queries = normalize(query_in, q_gain, query_scale).astype(jnp.bfloat16)
    grad_heads = grad_out.reshape(rows_here, heads_here, 2, HD)
    stacked = jnp.stack([keys_bf, values_bf])
    behind = from_behind(stacked, SEQ, 1)
    extended = jnp.concatenate([behind, stacked], axis=1).reshape(2, WINDOW + rows_here, HD)
    seg_pad = jnp.concatenate([jnp.full((WINDOW,), -1, jnp.int32), segment_ids])
    query_seg = lax.dynamic_slice_in_dim(segment_ids, base_row, rows_here, 0)
    key_seg = lax.dynamic_slice_in_dim(seg_pad, base_row, WINDOW + rows_here, 0)
    attention, dquery, grad_acc = attend(
        queries.reshape(rows_here, 2 * HD),
        grad_out,
        extended[0],
        extended[1],
        query_seg.reshape(rows_here, 1),
        key_seg.reshape(1, WINDOW + rows_here),
    )
    dquery = dquery.reshape(rows_here, heads_here, 2, HD)
    grad_acc = grad_acc.reshape(2, WINDOW + rows_here, heads_here, HD)
    own_grads = grad_acc[:, WINDOW:]
    offset_row = 0
    distance = 1
    first_row = max(0, distance * rows_here - WINDOW)
    piece_rows = rows_here - first_row
    outgoing = grad_acc[:, offset_row : offset_row + piece_rows]
    returned = from_behind(outgoing.astype(jnp.bfloat16), SEQ, -distance).astype(outgoing.dtype)
    own_grads = own_grads.at[:, first_row:].add(returned)
    _, pull_query = jax.vjp(lambda raw_vals: normalize(raw_vals, q_gain, query_scale), query_in)
    grad_q = pull_query(dquery)[0].astype(jnp.bfloat16).reshape(rows_here, 2 * heads_here * HD)
    _, pull_key = jax.vjp(lambda raw_vals: normalize(raw_vals, k_gain, 1.0), key_in)
    key_grad = pull_key(own_grads[0])[0].astype(jnp.bfloat16).reshape(rows_here, heads_here * HD)
    value_grad = own_grads[1].astype(jnp.bfloat16).reshape(rows_here, heads_here * HD)
    grads_all = gather_all(jnp.stack([key_grad, value_grad], axis=1), "uly")
    weight_heads = jnp.stack(weight_ts).reshape(2, n_uly, heads_here * HD, feats)
    grad_normed = jnp.einsum(
        "htkc,khcf->tf", grads_all, weight_heads, preferred_element_type=jnp.float32
    ).astype(jnp.bfloat16)
    weight_part = jnp.einsum(
        "htkc,tf->khcf", grads_all, normed, preferred_element_type=jnp.float32
    ).astype(jnp.bfloat16)
    summed = reduce_seq(weight_part.reshape(2, n_seq, col_block, feats))
    grad_key_weight = summed[0].T
    grad_value_weight = summed[1].T
    return (attention, grad_normed, grad_q, grad_key_weight, grad_value_weight)


def solution(mesh):
    n_seq, n_uly = mesh.shape["seq"], mesh.shape["uly"]
    fine = jax.sharding.Mesh(mesh.devices.reshape(n_seq // 2, 2, n_uly), ("chip", "core", "uly"))
    return jax.shard_map(
        body,
        mesh=fine,
        in_specs=(
            P(SEQ, "uly"),
            P(SEQ, "uly"),
            P("uly", SEQ),
            P("uly", SEQ),
            P(),
            P(),
            P(),
            P(SEQ, "uly"),
        ),
        out_specs=(
            P(SEQ, "uly"),
            P(SEQ, "uly"),
            P(SEQ, "uly"),
            P("uly", SEQ),
            P("uly", SEQ),
        ),
        check_vma=False,
    )
```

```python
import functools

import jax
import jax.numpy as jnp
from jax import lax
from jax.experimental import pallas as pl
from jax.experimental.pallas import tpu as pltpu
from jax.sharding import PartitionSpec as P

HD = 128
WINDOW = 1024


epsilon = 1e-06
query_scale = 168.0 ** (-0.5)


def from_behind(array, axis, by):
    devices = lax.axis_size(axis)
    pairs = [(i, i + by) for i in range(devices) if 0 <= i + by < devices]
    return lax.ppermute(array, axis, pairs)


def normalize(raw_vals, gain, factor):
    mean_sq = jnp.mean(raw_vals * raw_vals, axis=-1, keepdims=True)
    return raw_vals * lax.rsqrt(mean_sq + epsilon) * gain * factor


def exchange(blocks, axis):
    return lax.all_to_all(blocks, axis, 0, 0)


def gather_all(block, axis):
    count = lax.axis_size(axis)
    return exchange(jnp.broadcast_to(block[None], (count,) + block.shape), axis)


SEQ = ("level", "row", "core")
CHIP = ("level", "row")
SWAP = [(0, 1), (1, 0)]


def gather_kernel(levels, rows, x_ref, out_ref, local_sem, z_send, z_recv, x_send, x_recv, f_send, f_recv):
    level = lax.axis_index("level")
    row = lax.axis_index("row")
    core = lax.axis_index("core")
    uly = lax.axis_index("uly")
    other = 1 - core
    mesh_ids = pl.DeviceIdType.MESH

    def slot(at_level, at_row):
        return (lax.rem(at_level, levels) * rows + lax.rem(at_row, rows)) * 2 + core

    def window(index):
        return out_ref.at[:, pl.ds(index, 1)]

    def to_partner(index, dx, dz):
        return pltpu.make_async_remote_copy(
            src_ref=window(index),
            dst_ref=window(index),
            send_sem=f_send.at[dx, dz],
            recv_sem=f_recv.at[dx, dz],
            device_id=(level, row, other, uly),
            device_id_type=mesh_ids,
        )

    barrier = pltpu.get_barrier_semaphore()
    for dz in range(1, levels):
        peer = (lax.rem(level + dz, levels), row, core, uly)
        pl.semaphore_signal(barrier, 1, device_id=peer, device_id_type=mesh_ids)
    for dx in range(1, rows):
        peer = (level, lax.rem(row + dx, rows), core, uly)
        pl.semaphore_signal(barrier, 1, device_id=peer, device_id_type=mesh_ids)
    pl.semaphore_signal(barrier, 1, device_id=(level, row, other, uly), device_id_type=mesh_ids)
    pl.semaphore_wait(barrier, levels + rows - 1)
    mine = slot(level, row)
    local = pltpu.make_async_copy(x_ref, window(mine), local_sem)
    local.start()
    z_copies = {}
    for dz in range(1, levels):
        z_copies[dz] = pltpu.make_async_remote_copy(
            src_ref=x_ref,
            dst_ref=window(mine),
            send_sem=z_send.at[dz],
            recv_sem=z_recv.at[dz],
            device_id=(lax.rem(level + dz, levels), row, core, uly),
            device_id_type=mesh_ids,
        )
        z_copies[dz].start()
    local.wait()
    x_moves = {}
    forwards = []

    def spread(dz, index):
        for dx in range(1, rows):
            move = pltpu.make_async_remote_copy(
                src_ref=window(index),
                dst_ref=window(index),
                send_sem=x_send.at[dx, dz],
                recv_sem=x_recv.at[dx, dz],
                device_id=(level, lax.rem(row + dx, rows), core, uly),
                device_id_type=mesh_ids,
            )
            move.start()
            x_moves[dx, dz] = move
        forward = to_partner(index, 0, dz)
        forward.start()
        forwards.append(forward)

    spread(0, mine)
    for dz in range(1, levels):
        z_copies[dz].wait_recv()
        spread(dz, slot(level + levels - dz, row))
    for dx in range(1, rows):
        for dz in range(levels):
            x_moves[dx, dz].wait_recv()
            forward = to_partner(slot(level + levels - dz, row + rows - dx), dx, dz)
            forward.start()
            forwards.append(forward)
    for dz in range(1, levels):
        z_copies[dz].wait_send()
    for move in x_moves.values():
        move.wait_send()
    for forward in forwards:
        forward.wait()


def gather_seq(block):
    levels = lax.axis_size("level")
    rows = lax.axis_size("row")
    spec = pl.BlockSpec(memory_space=pltpu.VMEM)
    return pl.pallas_call(
        functools.partial(gather_kernel, levels, rows),
        out_shape=jax.ShapeDtypeStruct((block.shape[0], 2 * levels * rows) + block.shape[1:], block.dtype),
        in_specs=[spec],
        out_specs=spec,
        scratch_shapes=[
            pltpu.SemaphoreType.DMA(()),
            pltpu.SemaphoreType.DMA((levels,)),
            pltpu.SemaphoreType.DMA((levels,)),
            pltpu.SemaphoreType.DMA((rows, levels)),
            pltpu.SemaphoreType.DMA((rows, levels)),
            pltpu.SemaphoreType.DMA((rows, levels)),
            pltpu.SemaphoreType.DMA((rows, levels)),
        ],
        compiler_params=pltpu.CompilerParams(collective_id=0, has_side_effects=True),
    )(block[:, None])


def reduce_seq(blocks):
    chips = blocks.shape[1] // 2
    split = blocks.reshape((blocks.shape[0], chips, 2) + blocks.shape[2:])
    core = lax.axis_index("core")
    keep = jnp.take(split, core, axis=2)
    send = jnp.take(split, 1 - core, axis=2)
    pair = (keep.astype(jnp.float32) + lax.ppermute(send, "core", SWAP).astype(jnp.float32))
    pair = pair.astype(jnp.bfloat16).transpose(1, 0, 2, 3)
    return jnp.sum(exchange(pair, CHIP).astype(jnp.float32), axis=0)


def attend_block(
    queries, key_block, value_block, grad_block, query_pos, key_pos, query_seg, key_seg
):
    scores = jnp.einsum("bhge,lhe->hgbl", queries, key_block, preferred_element_type=jnp.float32)
    allowed = (
        (key_pos[None, :] <= query_pos[:, None])
        & (key_pos[None, :] > query_pos[:, None] - WINDOW)
        & (key_seg[None, :] == query_seg[:, None])
    )
    exp_scores = jnp.where(allowed[None, None], jnp.exp(scores), 0.0)
    probs = exp_scores / jnp.sum(exp_scores, axis=-1, keepdims=True)
    weights = probs.astype(jnp.bfloat16)
    attended = jnp.einsum(
        "hgbl,lhe->bhge", weights, value_block, preferred_element_type=jnp.float32
    ).astype(jnp.bfloat16)
    dprob = jnp.einsum(
        "bhge,lhe->hgbl", grad_block, value_block, preferred_element_type=jnp.float32
    )
    delta_row = jnp.sum(probs * dprob, axis=-1, keepdims=True)
    dscore = (probs * (dprob - delta_row)).astype(jnp.bfloat16)
    dquery = jnp.einsum("hgbl,lhe->bhge", dscore, key_block, preferred_element_type=jnp.float32)
    dkey = jnp.einsum("hgbl,bhge->lhe", dscore, queries, preferred_element_type=jnp.float32)
    dvalue = jnp.einsum("hgbl,bhge->lhe", weights, grad_block, preferred_element_type=jnp.float32)
    return (attended, dquery, dkey, dvalue)


def attention_kernel(q_ref, do_ref, k_ref, v_ref, qseg_ref, kseg_ref, out_ref, dq_ref, dkv_ref):
    rows = q_ref.shape[0]
    block = 256
    span = block + WINDOW
    dkv_ref[...] = jnp.zeros(dkv_ref.shape, jnp.float32)
    nt = (((1,), (1,)), ((), ()))
    tn = (((0,), (0,)), ((), ()))
    for b in range(rows // block):
        r0 = b * block
        k = k_ref[pl.ds(r0, span), :]
        v = v_ref[pl.ds(r0, span), :]
        row = lax.broadcasted_iota(jnp.int32, (block, span), 0)
        col = lax.broadcasted_iota(jnp.int32, (block, span), 1)
        allowed = (col <= row + WINDOW) & (col > row)
        allowed = allowed & (qseg_ref[pl.ds(r0, block), :] == kseg_ref[:, pl.ds(r0, span)])
        dk_acc = jnp.zeros((span, HD), jnp.float32)
        dv_acc = jnp.zeros((span, HD), jnp.float32)
        for g in range(2):
            q = q_ref[pl.ds(r0, block), pl.ds(g * HD, HD)]
            do = do_ref[pl.ds(r0, block), pl.ds(g * HD, HD)]
            scores = lax.dot_general(q, k, nt, preferred_element_type=jnp.float32)
            exp_scores = jnp.where(allowed, jnp.exp(scores), 0.0)
            probs = exp_scores / jnp.sum(exp_scores, axis=1, keepdims=True)
            weights = probs.astype(jnp.bfloat16)
            out_ref[pl.ds(r0, block), pl.ds(g * HD, HD)] = jnp.dot(
                weights, v, preferred_element_type=jnp.float32
            ).astype(out_ref.dtype)
            dprob = lax.dot_general(do, v, nt, preferred_element_type=jnp.float32)
            delta_row = jnp.sum(probs * dprob, axis=1, keepdims=True)
            dscore = (probs * (dprob - delta_row)).astype(jnp.bfloat16)
            dq_ref[pl.ds(r0, block), pl.ds(g * HD, HD)] = jnp.dot(
                dscore, k, preferred_element_type=jnp.float32
            )
            dk_acc = dk_acc + lax.dot_general(dscore, q, tn, preferred_element_type=jnp.float32)
            dv_acc = dv_acc + lax.dot_general(weights, do, tn, preferred_element_type=jnp.float32)
        dkv_ref[0, pl.ds(r0, span), :] += dk_acc
        dkv_ref[1, pl.ds(r0, span), :] += dv_acc


def attend(queries, grad_out, keys, values, query_seg, key_seg):
    rows = queries.shape[0]
    spec = pl.BlockSpec(memory_space=pltpu.VMEM)
    return pl.pallas_call(
        attention_kernel,
        out_shape=(
            jax.ShapeDtypeStruct((rows, 2 * HD), jnp.bfloat16),
            jax.ShapeDtypeStruct((rows, 2 * HD), jnp.float32),
            jax.ShapeDtypeStruct((2, keys.shape[0], HD), jnp.float32),
        ),
        in_specs=[spec] * 6,
        out_specs=(spec, spec, spec),
        cost_estimate=pl.CostEstimate(
            flops=12 * rows * (rows + WINDOW) * HD * 2, transcendentals=2 * rows * (rows + WINDOW),
            bytes_accessed=16 * rows * HD * 4,
        ),
    )(queries, grad_out, keys, values, query_seg, key_seg)


def body(normed, q_raw, key_weight, value_weight, q_gain, k_gain, segment_ids, grad_out):
    rows_here = normed.shape[0]
    feats = normed.shape[1]
    heads_here = q_raw.shape[1] // (2 * HD)
    n_seq = lax.axis_size(SEQ)
    n_uly = lax.axis_size("uly")
    col_block = key_weight.shape[1]
    seq_index = lax.axis_index(SEQ)
    base_row = seq_index * rows_here
    pair_t = jnp.stack([key_weight.T, value_weight.T])
    weight_t = gather_seq(pair_t).reshape(2, n_seq * col_block, feats)
    terms = lax.dot_general(
        normed, weight_t, (((1,), (2,)), ((), ())), preferred_element_type=jnp.float32
    ).astype(jnp.bfloat16)
    terms = terms.reshape(rows_here, 2, n_uly, heads_here * HD).transpose(2, 0, 1, 3)
    received = exchange(terms, "uly")
    raw_pair = jnp.sum(received.astype(jnp.float32), axis=0)
    key_raw = raw_pair[:, 0]
    value_raw = raw_pair[:, 1]
    key_in = key_raw.reshape(rows_here, heads_here, HD)
    keys_bf = normalize(key_in, k_gain, 1.0).astype(jnp.bfloat16)
    values_bf = value_raw.reshape(rows_here, heads_here, HD).astype(jnp.bfloat16)
    query_in = q_raw.astype(jnp.float32).reshape(rows_here, heads_here, 2, HD)
    queries = normalize(query_in, q_gain, query_scale).astype(jnp.bfloat16)
    grad_heads = grad_out.reshape(rows_here, heads_here, 2, HD)
    stacked = jnp.stack([keys_bf, values_bf])
    behind = from_behind(stacked, SEQ, 1)
    extended = jnp.concatenate([behind, stacked], axis=1).reshape(2, WINDOW + rows_here, HD)
    seg_pad = jnp.concatenate([jnp.full((WINDOW,), -1, jnp.int32), segment_ids])
    query_seg = lax.dynamic_slice_in_dim(segment_ids, base_row, rows_here, 0)
    key_seg = lax.dynamic_slice_in_dim(seg_pad, base_row, WINDOW + rows_here, 0)
    attention, dquery, grad_acc = attend(
        queries.reshape(rows_here, 2 * HD),
        grad_out,
        extended[0],
        extended[1],
        query_seg.reshape(rows_here, 1),
        key_seg.reshape(1, WINDOW + rows_here),
    )
    dquery = dquery.reshape(rows_here, heads_here, 2, HD)
    grad_acc = grad_acc.reshape(2, WINDOW + rows_here, heads_here, HD)
    own_grads = grad_acc[:, WINDOW:]
    offset_row = 0
    distance = 1
    first_row = max(0, distance * rows_here - WINDOW)
    piece_rows = rows_here - first_row
    outgoing = grad_acc[:, offset_row : offset_row + piece_rows]
    returned = from_behind(outgoing.astype(jnp.bfloat16), SEQ, -distance).astype(outgoing.dtype)
    own_grads = own_grads.at[:, first_row:].add(returned)
    _, pull_query = jax.vjp(lambda raw_vals: normalize(raw_vals, q_gain, query_scale), query_in)
    grad_q = pull_query(dquery)[0].astype(jnp.bfloat16).reshape(rows_here, 2 * heads_here * HD)
    _, pull_key = jax.vjp(lambda raw_vals: normalize(raw_vals, k_gain, 1.0), key_in)
    key_grad = pull_key(own_grads[0])[0].astype(jnp.bfloat16).reshape(rows_here, heads_here * HD)
    value_grad = own_grads[1].astype(jnp.bfloat16).reshape(rows_here, heads_here * HD)
    grads_all = gather_all(jnp.stack([key_grad, value_grad], axis=1), "uly")
    weight_heads = weight_t.reshape(2, n_uly, heads_here * HD, feats)
    grad_normed = jnp.einsum(
        "htkc,khcf->tf", grads_all, weight_heads, preferred_element_type=jnp.float32
    ).astype(jnp.bfloat16)
    weight_part = jnp.einsum(
        "htkc,tf->khcf", grads_all, normed, preferred_element_type=jnp.float32
    ).astype(jnp.bfloat16)
    summed = reduce_seq(weight_part.reshape(2, n_seq, col_block, feats))
    grad_key_weight = summed[0].T
    grad_value_weight = summed[1].T
    return (attention, grad_normed, grad_q, grad_key_weight, grad_value_weight)


def solution(mesh):
    n_seq, n_uly = mesh.shape["seq"], mesh.shape["uly"]
    rows = 4
    fine = jax.sharding.Mesh(
        mesh.devices.reshape(n_seq // (2 * rows), rows, 2, n_uly), ("level", "row", "core", "uly")
    )
    return jax.shard_map(
        body,
        mesh=fine,
        in_specs=(
            P(SEQ, "uly"),
            P(SEQ, "uly"),
            P("uly", SEQ),
            P("uly", SEQ),
            P(),
            P(),
            P(),
            P(SEQ, "uly"),
        ),
        out_specs=(
            P(SEQ, "uly"),
            P(SEQ, "uly"),
            P(SEQ, "uly"),
            P("uly", SEQ),
            P("uly", SEQ),
        ),
        check_vma=False,
    )
```

```python
import functools

import jax
import jax.numpy as jnp
from jax import lax
from jax.experimental import pallas as pl
from jax.experimental.pallas import tpu as pltpu
from jax.sharding import PartitionSpec as P

HD = 128
WINDOW = 1024


epsilon = 1e-06
query_scale = 168.0 ** (-0.5)


def from_behind(array, axis, by):
    devices = lax.axis_size(axis)
    pairs = [(i, i + by) for i in range(devices) if 0 <= i + by < devices]
    return lax.ppermute(array, axis, pairs)


def normalize(raw_vals, gain, factor):
    mean_sq = jnp.mean(raw_vals * raw_vals, axis=-1, keepdims=True)
    return raw_vals * lax.rsqrt(mean_sq + epsilon) * gain * factor


def exchange(blocks, axis):
    return lax.all_to_all(blocks, axis, 0, 0)


def gather_all(block, axis):
    count = lax.axis_size(axis)
    return exchange(jnp.broadcast_to(block[None], (count,) + block.shape), axis)


SEQ = ("level", "row", "core")
CHIP = ("level", "row")
SWAP = [(0, 1), (1, 0)]


def gather_kernel(levels, rows, x_ref, out_ref, local_sem, z_send, z_recv, x_send, x_recv, f_send, f_recv):
    level = lax.axis_index("level")
    row = lax.axis_index("row")
    core = lax.axis_index("core")
    uly = lax.axis_index("uly")
    other = 1 - core
    mesh_ids = pl.DeviceIdType.MESH

    def slot(at_level, at_row):
        return (lax.rem(at_level, levels) * rows + lax.rem(at_row, rows)) * 2 + core

    def window(index):
        return out_ref.at[:, pl.ds(index, 1)]

    def to_partner(index, dx, dz):
        return pltpu.make_async_remote_copy(
            src_ref=window(index),
            dst_ref=window(index),
            send_sem=f_send.at[dx, dz],
            recv_sem=f_recv.at[dx, dz],
            device_id=(level, row, other, uly),
            device_id_type=mesh_ids,
        )

    barrier = pltpu.get_barrier_semaphore()
    for dz in range(1, levels):
        peer = (lax.rem(level + dz, levels), row, core, uly)
        pl.semaphore_signal(barrier, 1, device_id=peer, device_id_type=mesh_ids)
    for dx in range(1, rows):
        peer = (level, lax.rem(row + dx, rows), core, uly)
        pl.semaphore_signal(barrier, 1, device_id=peer, device_id_type=mesh_ids)
    pl.semaphore_signal(barrier, 1, device_id=(level, row, other, uly), device_id_type=mesh_ids)
    pl.semaphore_wait(barrier, levels + rows - 1)
    mine = slot(level, row)
    local = pltpu.make_async_copy(x_ref, window(mine), local_sem)
    local.start()
    z_copies = {}
    for dz in range(1, levels):
        z_copies[dz] = pltpu.make_async_remote_copy(
            src_ref=x_ref,
            dst_ref=window(mine),
            send_sem=z_send.at[dz],
            recv_sem=z_recv.at[dz],
            device_id=(lax.rem(level + dz, levels), row, core, uly),
            device_id_type=mesh_ids,
        )
        z_copies[dz].start()
    local.wait()
    x_moves = {}
    forwards = []

    def spread(dz, index):
        for dx in range(1, rows):
            move = pltpu.make_async_remote_copy(
                src_ref=window(index),
                dst_ref=window(index),
                send_sem=x_send.at[dx, dz],
                recv_sem=x_recv.at[dx, dz],
                device_id=(level, lax.rem(row + dx, rows), core, uly),
                device_id_type=mesh_ids,
            )
            move.start()
            x_moves[dx, dz] = move
        forward = to_partner(index, 0, dz)
        forward.start()
        forwards.append(forward)

    spread(0, mine)
    for dz in range(1, levels):
        z_copies[dz].wait_recv()
        spread(dz, slot(level + levels - dz, row))
    for dx in range(1, rows):
        for dz in range(levels):
            x_moves[dx, dz].wait_recv()
            forward = to_partner(slot(level + levels - dz, row + rows - dx), dx, dz)
            forward.start()
            forwards.append(forward)
    for dz in range(1, levels):
        z_copies[dz].wait_send()
    for move in x_moves.values():
        move.wait_send()
    for forward in forwards:
        forward.wait()


def gather_seq(block):
    levels = lax.axis_size("level")
    rows = lax.axis_size("row")
    spec = pl.BlockSpec(memory_space=pltpu.VMEM)
    return pl.pallas_call(
        functools.partial(gather_kernel, levels, rows),
        out_shape=jax.ShapeDtypeStruct((block.shape[0], 2 * levels * rows) + block.shape[1:], block.dtype),
        in_specs=[spec],
        out_specs=spec,
        scratch_shapes=[
            pltpu.SemaphoreType.DMA(()),
            pltpu.SemaphoreType.DMA((levels,)),
            pltpu.SemaphoreType.DMA((levels,)),
            pltpu.SemaphoreType.DMA((rows, levels)),
            pltpu.SemaphoreType.DMA((rows, levels)),
            pltpu.SemaphoreType.DMA((rows, levels)),
            pltpu.SemaphoreType.DMA((rows, levels)),
        ],
        compiler_params=pltpu.CompilerParams(collective_id=0, has_side_effects=True),
    )(block[:, None])


def reduce_seq(blocks):
    chips = blocks.shape[1] // 2
    split = blocks.reshape((blocks.shape[0], chips, 2) + blocks.shape[2:])
    core = lax.axis_index("core")
    keep = jnp.take(split, core, axis=2)
    send = jnp.take(split, 1 - core, axis=2)
    pair = (keep.astype(jnp.float32) + lax.ppermute(send, "core", SWAP).astype(jnp.float32))
    pair = pair.astype(jnp.bfloat16).transpose(1, 0, 2, 3)
    levels = lax.axis_size("level")
    by_row = pair.reshape((levels, chips // levels) + pair.shape[1:]).transpose(1, 0, 2, 3, 4)
    part = jnp.sum(exchange(by_row, "row").astype(jnp.float32), axis=0)
    return jnp.sum(exchange(part.astype(jnp.bfloat16), "level").astype(jnp.float32), axis=0)


def attend_block(
    queries, key_block, value_block, grad_block, query_pos, key_pos, query_seg, key_seg
):
    scores = jnp.einsum("bhge,lhe->hgbl", queries, key_block, preferred_element_type=jnp.float32)
    allowed = (
        (key_pos[None, :] <= query_pos[:, None])
        & (key_pos[None, :] > query_pos[:, None] - WINDOW)
        & (key_seg[None, :] == query_seg[:, None])
    )
    exp_scores = jnp.where(allowed[None, None], jnp.exp(scores), 0.0)
    probs = exp_scores / jnp.sum(exp_scores, axis=-1, keepdims=True)
    weights = probs.astype(jnp.bfloat16)
    attended = jnp.einsum(
        "hgbl,lhe->bhge", weights, value_block, preferred_element_type=jnp.float32
    ).astype(jnp.bfloat16)
    dprob = jnp.einsum(
        "bhge,lhe->hgbl", grad_block, value_block, preferred_element_type=jnp.float32
    )
    delta_row = jnp.sum(probs * dprob, axis=-1, keepdims=True)
    dscore = (probs * (dprob - delta_row)).astype(jnp.bfloat16)
    dquery = jnp.einsum("hgbl,lhe->bhge", dscore, key_block, preferred_element_type=jnp.float32)
    dkey = jnp.einsum("hgbl,bhge->lhe", dscore, queries, preferred_element_type=jnp.float32)
    dvalue = jnp.einsum("hgbl,bhge->lhe", weights, grad_block, preferred_element_type=jnp.float32)
    return (attended, dquery, dkey, dvalue)


def attention_kernel(q_ref, do_ref, k_ref, v_ref, qseg_ref, kseg_ref, out_ref, dq_ref, dkv_ref):
    rows = q_ref.shape[0]
    block = 256
    span = block + WINDOW
    dkv_ref[...] = jnp.zeros(dkv_ref.shape, jnp.float32)
    nt = (((1,), (1,)), ((), ()))
    tn = (((0,), (0,)), ((), ()))
    for b in range(rows // block):
        r0 = b * block
        k = k_ref[pl.ds(r0, span), :]
        v = v_ref[pl.ds(r0, span), :]
        row = lax.broadcasted_iota(jnp.int32, (block, span), 0)
        col = lax.broadcasted_iota(jnp.int32, (block, span), 1)
        allowed = (col <= row + WINDOW) & (col > row)
        allowed = allowed & (qseg_ref[pl.ds(r0, block), :] == kseg_ref[:, pl.ds(r0, span)])
        dk_acc = jnp.zeros((span, HD), jnp.float32)
        dv_acc = jnp.zeros((span, HD), jnp.float32)
        for g in range(2):
            q = q_ref[pl.ds(r0, block), pl.ds(g * HD, HD)]
            do = do_ref[pl.ds(r0, block), pl.ds(g * HD, HD)]
            scores = lax.dot_general(q, k, nt, preferred_element_type=jnp.float32)
            exp_scores = jnp.where(allowed, jnp.exp(scores), 0.0)
            probs = exp_scores / jnp.sum(exp_scores, axis=1, keepdims=True)
            weights = probs.astype(jnp.bfloat16)
            out_ref[pl.ds(r0, block), pl.ds(g * HD, HD)] = jnp.dot(
                weights, v, preferred_element_type=jnp.float32
            ).astype(out_ref.dtype)
            dprob = lax.dot_general(do, v, nt, preferred_element_type=jnp.float32)
            delta_row = jnp.sum(probs * dprob, axis=1, keepdims=True)
            dscore = (probs * (dprob - delta_row)).astype(jnp.bfloat16)
            dq_ref[pl.ds(r0, block), pl.ds(g * HD, HD)] = jnp.dot(
                dscore, k, preferred_element_type=jnp.float32
            )
            dk_acc = dk_acc + lax.dot_general(dscore, q, tn, preferred_element_type=jnp.float32)
            dv_acc = dv_acc + lax.dot_general(weights, do, tn, preferred_element_type=jnp.float32)
        dkv_ref[0, pl.ds(r0, span), :] += dk_acc
        dkv_ref[1, pl.ds(r0, span), :] += dv_acc


def attend(queries, grad_out, keys, values, query_seg, key_seg):
    rows = queries.shape[0]
    spec = pl.BlockSpec(memory_space=pltpu.VMEM)
    return pl.pallas_call(
        attention_kernel,
        out_shape=(
            jax.ShapeDtypeStruct((rows, 2 * HD), jnp.bfloat16),
            jax.ShapeDtypeStruct((rows, 2 * HD), jnp.float32),
            jax.ShapeDtypeStruct((2, keys.shape[0], HD), jnp.float32),
        ),
        in_specs=[spec] * 6,
        out_specs=(spec, spec, spec),
        cost_estimate=pl.CostEstimate(
            flops=12 * rows * (rows + WINDOW) * HD * 2, transcendentals=2 * rows * (rows + WINDOW),
            bytes_accessed=16 * rows * HD * 4,
        ),
    )(queries, grad_out, keys, values, query_seg, key_seg)


def body(normed, q_raw, key_weight, value_weight, q_gain, k_gain, segment_ids, grad_out):
    rows_here = normed.shape[0]
    feats = normed.shape[1]
    heads_here = q_raw.shape[1] // (2 * HD)
    n_seq = lax.axis_size(SEQ)
    n_uly = lax.axis_size("uly")
    col_block = key_weight.shape[1]
    seq_index = lax.axis_index(SEQ)
    base_row = seq_index * rows_here
    pair_t = jnp.stack([key_weight.T, value_weight.T])
    weight_t = gather_seq(pair_t).reshape(2, n_seq * col_block, feats)
    terms = lax.dot_general(
        normed, weight_t, (((1,), (2,)), ((), ())), preferred_element_type=jnp.float32
    ).astype(jnp.bfloat16)
    terms = terms.reshape(rows_here, 2, n_uly, heads_here * HD).transpose(2, 0, 1, 3)
    received = exchange(terms, "uly")
    raw_pair = jnp.sum(received.astype(jnp.float32), axis=0)
    key_raw = raw_pair[:, 0]
    value_raw = raw_pair[:, 1]
    key_in = key_raw.reshape(rows_here, heads_here, HD)
    keys_bf = normalize(key_in, k_gain, 1.0).astype(jnp.bfloat16)
    values_bf = value_raw.reshape(rows_here, heads_here, HD).astype(jnp.bfloat16)
    query_in = q_raw.astype(jnp.float32).reshape(rows_here, heads_here, 2, HD)
    queries = normalize(query_in, q_gain, query_scale).astype(jnp.bfloat16)
    grad_heads = grad_out.reshape(rows_here, heads_here, 2, HD)
    stacked = jnp.stack([keys_bf, values_bf])
    behind = from_behind(stacked, SEQ, 1)
    extended = jnp.concatenate([behind, stacked], axis=1).reshape(2, WINDOW + rows_here, HD)
    seg_pad = jnp.concatenate([jnp.full((WINDOW,), -1, jnp.int32), segment_ids])
    query_seg = lax.dynamic_slice_in_dim(segment_ids, base_row, rows_here, 0)
    key_seg = lax.dynamic_slice_in_dim(seg_pad, base_row, WINDOW + rows_here, 0)
    attention, dquery, grad_acc = attend(
        queries.reshape(rows_here, 2 * HD),
        grad_out,
        extended[0],
        extended[1],
        query_seg.reshape(rows_here, 1),
        key_seg.reshape(1, WINDOW + rows_here),
    )
    dquery = dquery.reshape(rows_here, heads_here, 2, HD)
    grad_acc = grad_acc.reshape(2, WINDOW + rows_here, heads_here, HD)
    own_grads = grad_acc[:, WINDOW:]
    offset_row = 0
    distance = 1
    first_row = max(0, distance * rows_here - WINDOW)
    piece_rows = rows_here - first_row
    outgoing = grad_acc[:, offset_row : offset_row + piece_rows]
    returned = from_behind(outgoing.astype(jnp.bfloat16), SEQ, -distance).astype(outgoing.dtype)
    own_grads = own_grads.at[:, first_row:].add(returned)
    _, pull_query = jax.vjp(lambda raw_vals: normalize(raw_vals, q_gain, query_scale), query_in)
    grad_q = pull_query(dquery)[0].astype(jnp.bfloat16).reshape(rows_here, 2 * heads_here * HD)
    _, pull_key = jax.vjp(lambda raw_vals: normalize(raw_vals, k_gain, 1.0), key_in)
    key_grad = pull_key(own_grads[0])[0].astype(jnp.bfloat16).reshape(rows_here, heads_here * HD)
    value_grad = own_grads[1].astype(jnp.bfloat16).reshape(rows_here, heads_here * HD)
    grads_all = gather_all(jnp.stack([key_grad, value_grad], axis=1), "uly")
    weight_heads = weight_t.reshape(2, n_uly, heads_here * HD, feats)
    grad_normed = jnp.einsum(
        "htkc,khcf->tf", grads_all, weight_heads, preferred_element_type=jnp.float32
    ).astype(jnp.bfloat16)
    weight_part = jnp.einsum(
        "htkc,tf->khcf", grads_all, normed, preferred_element_type=jnp.float32
    ).astype(jnp.bfloat16)
    summed = reduce_seq(weight_part.reshape(2, n_seq, col_block, feats))
    grad_key_weight = summed[0].T
    grad_value_weight = summed[1].T
    return (attention, grad_normed, grad_q, grad_key_weight, grad_value_weight)


def solution(mesh):
    n_seq, n_uly = mesh.shape["seq"], mesh.shape["uly"]
    rows = 4
    fine = jax.sharding.Mesh(
        mesh.devices.reshape(n_seq // (2 * rows), rows, 2, n_uly), ("level", "row", "core", "uly")
    )
    return jax.shard_map(
        body,
        mesh=fine,
        in_specs=(
            P(SEQ, "uly"),
            P(SEQ, "uly"),
            P("uly", SEQ),
            P("uly", SEQ),
            P(),
            P(),
            P(),
            P(SEQ, "uly"),
        ),
        out_specs=(
            P(SEQ, "uly"),
            P(SEQ, "uly"),
            P(SEQ, "uly"),
            P("uly", SEQ),
            P("uly", SEQ),
        ),
        check_vma=False,
    )
```

```python
import functools

import jax
import jax.numpy as jnp
from jax import lax
from jax.experimental import pallas as pl
from jax.experimental.pallas import tpu as pltpu
from jax.sharding import PartitionSpec as P

HD = 128
WINDOW = 1024


epsilon = 1e-06
query_scale = 168.0 ** (-0.5)


def from_behind(array, axis, by):
    devices = lax.axis_size(axis)
    pairs = [(i, i + by) for i in range(devices) if 0 <= i + by < devices]
    return lax.ppermute(array, axis, pairs)


def normalize(raw_vals, gain, factor):
    mean_sq = jnp.mean(raw_vals * raw_vals, axis=-1, keepdims=True)
    return raw_vals * lax.rsqrt(mean_sq + epsilon) * gain * factor


def exchange(blocks, axis):
    return lax.all_to_all(blocks, axis, 0, 0)


def gather_all(block, axis):
    count = lax.axis_size(axis)
    return exchange(jnp.broadcast_to(block[None], (count,) + block.shape), axis)


SEQ = ("level", "row", "core")
CHIP = ("level", "row")
SWAP = [(0, 1), (1, 0)]


def gather_kernel(levels, rows, x_ref, out_ref, local_sem, z_send, z_recv, x_send, x_recv, f_send, f_recv):
    level = lax.axis_index("level")
    row = lax.axis_index("row")
    core = lax.axis_index("core")
    uly = lax.axis_index("uly")
    other = 1 - core
    mesh_ids = pl.DeviceIdType.MESH

    def slot(at_level, at_row):
        return (lax.rem(at_level, levels) * rows + lax.rem(at_row, rows)) * 2 + core

    def window(index):
        return out_ref.at[:, pl.ds(index, 1)]

    def to_partner(index, dx, dz):
        return pltpu.make_async_remote_copy(
            src_ref=window(index),
            dst_ref=window(index),
            send_sem=f_send.at[dx, dz],
            recv_sem=f_recv.at[dx, dz],
            device_id=(level, row, other, uly),
            device_id_type=mesh_ids,
        )

    barrier = pltpu.get_barrier_semaphore()
    for dz in range(1, levels):
        peer = (lax.rem(level + dz, levels), row, core, uly)
        pl.semaphore_signal(barrier, 1, device_id=peer, device_id_type=mesh_ids)
    for dx in range(1, rows):
        peer = (level, lax.rem(row + dx, rows), core, uly)
        pl.semaphore_signal(barrier, 1, device_id=peer, device_id_type=mesh_ids)
    pl.semaphore_signal(barrier, 1, device_id=(level, row, other, uly), device_id_type=mesh_ids)
    pl.semaphore_wait(barrier, levels + rows - 1)
    mine = slot(level, row)
    local = pltpu.make_async_copy(x_ref, window(mine), local_sem)
    local.start()
    z_copies = {}
    for dz in range(1, levels):
        z_copies[dz] = pltpu.make_async_remote_copy(
            src_ref=x_ref,
            dst_ref=window(mine),
            send_sem=z_send.at[dz],
            recv_sem=z_recv.at[dz],
            device_id=(lax.rem(level + dz, levels), row, core, uly),
            device_id_type=mesh_ids,
        )
        z_copies[dz].start()
    local.wait()
    x_moves = {}
    forwards = []

    def spread(dz, index):
        for dx in range(1, rows):
            move = pltpu.make_async_remote_copy(
                src_ref=window(index),
                dst_ref=window(index),
                send_sem=x_send.at[dx, dz],
                recv_sem=x_recv.at[dx, dz],
                device_id=(level, lax.rem(row + dx, rows), core, uly),
                device_id_type=mesh_ids,
            )
            move.start()
            x_moves[dx, dz] = move
        forward = to_partner(index, 0, dz)
        forward.start()
        forwards.append(forward)

    spread(0, mine)
    for dz in range(1, levels):
        z_copies[dz].wait_recv()
        spread(dz, slot(level + levels - dz, row))
    for dx in range(1, rows):
        for dz in range(levels):
            x_moves[dx, dz].wait_recv()
            forward = to_partner(slot(level + levels - dz, row + rows - dx), dx, dz)
            forward.start()
            forwards.append(forward)
    for dz in range(1, levels):
        z_copies[dz].wait_send()
    for move in x_moves.values():
        move.wait_send()
    for forward in forwards:
        forward.wait()


def gather_seq(block):
    levels = lax.axis_size("level")
    rows = lax.axis_size("row")
    spec = pl.BlockSpec(memory_space=pltpu.VMEM)
    return pl.pallas_call(
        functools.partial(gather_kernel, levels, rows),
        out_shape=jax.ShapeDtypeStruct((block.shape[0], 2 * levels * rows) + block.shape[1:], block.dtype),
        in_specs=[spec],
        out_specs=spec,
        scratch_shapes=[
            pltpu.SemaphoreType.DMA(()),
            pltpu.SemaphoreType.DMA((levels,)),
            pltpu.SemaphoreType.DMA((levels,)),
            pltpu.SemaphoreType.DMA((rows, levels)),
            pltpu.SemaphoreType.DMA((rows, levels)),
            pltpu.SemaphoreType.DMA((rows, levels)),
            pltpu.SemaphoreType.DMA((rows, levels)),
        ],
        compiler_params=pltpu.CompilerParams(collective_id=0, has_side_effects=True),
    )(block[:, None])


def reduce_seq(blocks):
    levels = lax.axis_size("level")
    split = blocks.reshape((blocks.shape[0], levels, -1) + blocks.shape[2:])
    by_ring = split.transpose(2, 1, 0, 3, 4)
    part = jnp.sum(exchange(by_ring, ("row", "core")).astype(jnp.float32), axis=0)
    return jnp.sum(exchange(part.astype(jnp.bfloat16), "level").astype(jnp.float32), axis=0)


def attend_block(
    queries, key_block, value_block, grad_block, query_pos, key_pos, query_seg, key_seg
):
    scores = jnp.einsum("bhge,lhe->hgbl", queries, key_block, preferred_element_type=jnp.float32)
    allowed = (
        (key_pos[None, :] <= query_pos[:, None])
        & (key_pos[None, :] > query_pos[:, None] - WINDOW)
        & (key_seg[None, :] == query_seg[:, None])
    )
    exp_scores = jnp.where(allowed[None, None], jnp.exp(scores), 0.0)
    probs = exp_scores / jnp.sum(exp_scores, axis=-1, keepdims=True)
    weights = probs.astype(jnp.bfloat16)
    attended = jnp.einsum(
        "hgbl,lhe->bhge", weights, value_block, preferred_element_type=jnp.float32
    ).astype(jnp.bfloat16)
    dprob = jnp.einsum(
        "bhge,lhe->hgbl", grad_block, value_block, preferred_element_type=jnp.float32
    )
    delta_row = jnp.sum(probs * dprob, axis=-1, keepdims=True)
    dscore = (probs * (dprob - delta_row)).astype(jnp.bfloat16)
    dquery = jnp.einsum("hgbl,lhe->bhge", dscore, key_block, preferred_element_type=jnp.float32)
    dkey = jnp.einsum("hgbl,bhge->lhe", dscore, queries, preferred_element_type=jnp.float32)
    dvalue = jnp.einsum("hgbl,bhge->lhe", weights, grad_block, preferred_element_type=jnp.float32)
    return (attended, dquery, dkey, dvalue)


def attention_kernel(q_ref, do_ref, k_ref, v_ref, qseg_ref, kseg_ref, out_ref, dq_ref, dkv_ref):
    rows = q_ref.shape[0]
    block = 256
    span = block + WINDOW
    dkv_ref[...] = jnp.zeros(dkv_ref.shape, jnp.float32)
    nt = (((1,), (1,)), ((), ()))
    tn = (((0,), (0,)), ((), ()))
    for b in range(rows // block):
        r0 = b * block
        k = k_ref[pl.ds(r0, span), :]
        v = v_ref[pl.ds(r0, span), :]
        row = lax.broadcasted_iota(jnp.int32, (block, span), 0)
        col = lax.broadcasted_iota(jnp.int32, (block, span), 1)
        allowed = (col <= row + WINDOW) & (col > row)
        allowed = allowed & (qseg_ref[pl.ds(r0, block), :] == kseg_ref[:, pl.ds(r0, span)])
        dk_acc = jnp.zeros((span, HD), jnp.float32)
        dv_acc = jnp.zeros((span, HD), jnp.float32)
        for g in range(2):
            q = q_ref[pl.ds(r0, block), pl.ds(g * HD, HD)]
            do = do_ref[pl.ds(r0, block), pl.ds(g * HD, HD)]
            scores = lax.dot_general(q, k, nt, preferred_element_type=jnp.float32)
            exp_scores = jnp.where(allowed, jnp.exp(scores), 0.0)
            probs = exp_scores / jnp.sum(exp_scores, axis=1, keepdims=True)
            weights = probs.astype(jnp.bfloat16)
            out_ref[pl.ds(r0, block), pl.ds(g * HD, HD)] = jnp.dot(
                weights, v, preferred_element_type=jnp.float32
            ).astype(out_ref.dtype)
            dprob = lax.dot_general(do, v, nt, preferred_element_type=jnp.float32)
            delta_row = jnp.sum(probs * dprob, axis=1, keepdims=True)
            dscore = (probs * (dprob - delta_row)).astype(jnp.bfloat16)
            dq_ref[pl.ds(r0, block), pl.ds(g * HD, HD)] = jnp.dot(
                dscore, k, preferred_element_type=jnp.float32
            )
            dk_acc = dk_acc + lax.dot_general(dscore, q, tn, preferred_element_type=jnp.float32)
            dv_acc = dv_acc + lax.dot_general(weights, do, tn, preferred_element_type=jnp.float32)
        dkv_ref[0, pl.ds(r0, span), :] += dk_acc
        dkv_ref[1, pl.ds(r0, span), :] += dv_acc


def attend(queries, grad_out, keys, values, query_seg, key_seg):
    rows = queries.shape[0]
    spec = pl.BlockSpec(memory_space=pltpu.VMEM)
    return pl.pallas_call(
        attention_kernel,
        out_shape=(
            jax.ShapeDtypeStruct((rows, 2 * HD), jnp.bfloat16),
            jax.ShapeDtypeStruct((rows, 2 * HD), jnp.float32),
            jax.ShapeDtypeStruct((2, keys.shape[0], HD), jnp.float32),
        ),
        in_specs=[spec] * 6,
        out_specs=(spec, spec, spec),
        cost_estimate=pl.CostEstimate(
            flops=12 * rows * (rows + WINDOW) * HD * 2, transcendentals=2 * rows * (rows + WINDOW),
            bytes_accessed=16 * rows * HD * 4,
        ),
    )(queries, grad_out, keys, values, query_seg, key_seg)


def body(normed, q_raw, key_weight, value_weight, q_gain, k_gain, segment_ids, grad_out):
    rows_here = normed.shape[0]
    feats = normed.shape[1]
    heads_here = q_raw.shape[1] // (2 * HD)
    n_seq = lax.axis_size(SEQ)
    n_uly = lax.axis_size("uly")
    col_block = key_weight.shape[1]
    seq_index = lax.axis_index(SEQ)
    base_row = seq_index * rows_here
    pair_t = jnp.stack([key_weight.T, value_weight.T])
    weight_t = gather_seq(pair_t).reshape(2, n_seq * col_block, feats)
    terms = lax.dot_general(
        normed, weight_t, (((1,), (2,)), ((), ())), preferred_element_type=jnp.float32
    ).astype(jnp.bfloat16)
    terms = terms.reshape(rows_here, 2, n_uly, heads_here * HD).transpose(2, 0, 1, 3)
    received = exchange(terms, "uly")
    raw_pair = jnp.sum(received.astype(jnp.float32), axis=0)
    key_raw = raw_pair[:, 0]
    value_raw = raw_pair[:, 1]
    key_in = key_raw.reshape(rows_here, heads_here, HD)
    keys_bf = normalize(key_in, k_gain, 1.0).astype(jnp.bfloat16)
    values_bf = value_raw.reshape(rows_here, heads_here, HD).astype(jnp.bfloat16)
    query_in = q_raw.astype(jnp.float32).reshape(rows_here, heads_here, 2, HD)
    queries = normalize(query_in, q_gain, query_scale).astype(jnp.bfloat16)
    grad_heads = grad_out.reshape(rows_here, heads_here, 2, HD)
    stacked = jnp.stack([keys_bf, values_bf])
    behind = from_behind(stacked, SEQ, 1)
    extended = jnp.concatenate([behind, stacked], axis=1).reshape(2, WINDOW + rows_here, HD)
    seg_pad = jnp.concatenate([jnp.full((WINDOW,), -1, jnp.int32), segment_ids])
    query_seg = lax.dynamic_slice_in_dim(segment_ids, base_row, rows_here, 0)
    key_seg = lax.dynamic_slice_in_dim(seg_pad, base_row, WINDOW + rows_here, 0)
    attention, dquery, grad_acc = attend(
        queries.reshape(rows_here, 2 * HD),
        grad_out,
        extended[0],
        extended[1],
        query_seg.reshape(rows_here, 1),
        key_seg.reshape(1, WINDOW + rows_here),
    )
    dquery = dquery.reshape(rows_here, heads_here, 2, HD)
    grad_acc = grad_acc.reshape(2, WINDOW + rows_here, heads_here, HD)
    own_grads = grad_acc[:, WINDOW:]
    offset_row = 0
    distance = 1
    first_row = max(0, distance * rows_here - WINDOW)
    piece_rows = rows_here - first_row
    outgoing = grad_acc[:, offset_row : offset_row + piece_rows]
    returned = from_behind(outgoing.astype(jnp.bfloat16), SEQ, -distance).astype(outgoing.dtype)
    own_grads = own_grads.at[:, first_row:].add(returned)
    _, pull_query = jax.vjp(lambda raw_vals: normalize(raw_vals, q_gain, query_scale), query_in)
    grad_q = pull_query(dquery)[0].astype(jnp.bfloat16).reshape(rows_here, 2 * heads_here * HD)
    _, pull_key = jax.vjp(lambda raw_vals: normalize(raw_vals, k_gain, 1.0), key_in)
    key_grad = pull_key(own_grads[0])[0].astype(jnp.bfloat16).reshape(rows_here, heads_here * HD)
    value_grad = own_grads[1].astype(jnp.bfloat16).reshape(rows_here, heads_here * HD)
    grads_all = gather_all(jnp.stack([key_grad, value_grad], axis=1), "uly")
    weight_heads = weight_t.reshape(2, n_uly, heads_here * HD, feats)
    grad_normed = jnp.einsum(
        "htkc,khcf->tf", grads_all, weight_heads, preferred_element_type=jnp.float32
    ).astype(jnp.bfloat16)
    weight_part = jnp.einsum(
        "htkc,tf->khcf", grads_all, normed, preferred_element_type=jnp.float32
    ).astype(jnp.bfloat16)
    summed = reduce_seq(weight_part.reshape(2, n_seq, col_block, feats))
    grad_key_weight = summed[0].T
    grad_value_weight = summed[1].T
    return (attention, grad_normed, grad_q, grad_key_weight, grad_value_weight)


def solution(mesh):
    n_seq, n_uly = mesh.shape["seq"], mesh.shape["uly"]
    rows = 4
    fine = jax.sharding.Mesh(
        mesh.devices.reshape(n_seq // (2 * rows), rows, 2, n_uly), ("level", "row", "core", "uly")
    )
    return jax.shard_map(
        body,
        mesh=fine,
        in_specs=(
            P(SEQ, "uly"),
            P(SEQ, "uly"),
            P("uly", SEQ),
            P("uly", SEQ),
            P(),
            P(),
            P(),
            P(SEQ, "uly"),
        ),
        out_specs=(
            P(SEQ, "uly"),
            P(SEQ, "uly"),
            P(SEQ, "uly"),
            P("uly", SEQ),
            P("uly", SEQ),
        ),
        check_vma=False,
    )
```

```python
import functools

import jax
import jax.numpy as jnp
from jax import lax
from jax.experimental import pallas as pl
from jax.experimental.pallas import tpu as pltpu
from jax.sharding import PartitionSpec as P

HD = 128
WINDOW = 1024


epsilon = 1e-06
query_scale = 168.0 ** (-0.5)


def from_behind(array, axis, by):
    devices = lax.axis_size(axis)
    pairs = [(i, i + by) for i in range(devices) if 0 <= i + by < devices]
    return lax.ppermute(array, axis, pairs)


def normalize(raw_vals, gain, factor):
    mean_sq = jnp.mean(raw_vals * raw_vals, axis=-1, keepdims=True)
    return raw_vals * lax.rsqrt(mean_sq + epsilon) * gain * factor


def exchange(blocks, axis):
    return lax.all_to_all(blocks, axis, 0, 0)


def gather_all(block, axis):
    count = lax.axis_size(axis)
    return exchange(jnp.broadcast_to(block[None], (count,) + block.shape), axis)


SEQ = ("level", "row", "core")
CHIP = ("level", "row")
SWAP = [(0, 1), (1, 0)]


def gather_kernel(levels, rows, x_ref, out_ref, local_sem, z_send, z_recv, x_send, x_recv, f_send, f_recv):
    level = lax.axis_index("level")
    row = lax.axis_index("row")
    core = lax.axis_index("core")
    uly = lax.axis_index("uly")
    other = 1 - core
    mesh_ids = pl.DeviceIdType.MESH

    def slot(at_level, at_row):
        return (lax.rem(at_level, levels) * rows + lax.rem(at_row, rows)) * 2 + core

    def window(index):
        return out_ref.at[:, pl.ds(index, 1)]

    def to_partner(index, dx, dz):
        return pltpu.make_async_remote_copy(
            src_ref=window(index),
            dst_ref=window(index),
            send_sem=f_send.at[dx, dz],
            recv_sem=f_recv.at[dx, dz],
            device_id=(level, row, other, uly),
            device_id_type=mesh_ids,
        )

    barrier = pltpu.get_barrier_semaphore()
    for dz in range(1, levels):
        peer = (lax.rem(level + dz, levels), row, core, uly)
        pl.semaphore_signal(barrier, 1, device_id=peer, device_id_type=mesh_ids)
    for dx in range(1, rows):
        peer = (level, lax.rem(row + dx, rows), core, uly)
        pl.semaphore_signal(barrier, 1, device_id=peer, device_id_type=mesh_ids)
    pl.semaphore_signal(barrier, 1, device_id=(level, row, other, uly), device_id_type=mesh_ids)
    pl.semaphore_wait(barrier, levels + rows - 1)
    mine = slot(level, row)
    local = pltpu.make_async_copy(x_ref, window(mine), local_sem)
    local.start()
    z_copies = {}
    for dz in range(1, levels):
        z_copies[dz] = pltpu.make_async_remote_copy(
            src_ref=x_ref,
            dst_ref=window(mine),
            send_sem=z_send.at[dz],
            recv_sem=z_recv.at[dz],
            device_id=(lax.rem(level + dz, levels), row, core, uly),
            device_id_type=mesh_ids,
        )
        z_copies[dz].start()
    local.wait()
    x_moves = {}
    forwards = []

    def spread(dz, index):
        for dx in range(1, rows):
            move = pltpu.make_async_remote_copy(
                src_ref=window(index),
                dst_ref=window(index),
                send_sem=x_send.at[dx, dz],
                recv_sem=x_recv.at[dx, dz],
                device_id=(level, lax.rem(row + dx, rows), core, uly),
                device_id_type=mesh_ids,
            )
            move.start()
            x_moves[dx, dz] = move
        forward = to_partner(index, 0, dz)
        forward.start()
        forwards.append(forward)

    spread(0, mine)
    for dz in range(1, levels):
        z_copies[dz].wait_recv()
        spread(dz, slot(level + levels - dz, row))
    for dx in range(1, rows):
        for dz in range(levels):
            x_moves[dx, dz].wait_recv()
            forward = to_partner(slot(level + levels - dz, row + rows - dx), dx, dz)
            forward.start()
            forwards.append(forward)
    for dz in range(1, levels):
        z_copies[dz].wait_send()
    for move in x_moves.values():
        move.wait_send()
    for forward in forwards:
        forward.wait()


def gather_seq(block):
    levels = lax.axis_size("level")
    rows = lax.axis_size("row")
    spec = pl.BlockSpec(memory_space=pltpu.VMEM)
    return pl.pallas_call(
        functools.partial(gather_kernel, levels, rows),
        out_shape=jax.ShapeDtypeStruct((block.shape[0], 2 * levels * rows) + block.shape[1:], block.dtype),
        in_specs=[spec],
        out_specs=spec,
        scratch_shapes=[
            pltpu.SemaphoreType.DMA(()),
            pltpu.SemaphoreType.DMA((levels,)),
            pltpu.SemaphoreType.DMA((levels,)),
            pltpu.SemaphoreType.DMA((rows, levels)),
            pltpu.SemaphoreType.DMA((rows, levels)),
            pltpu.SemaphoreType.DMA((rows, levels)),
            pltpu.SemaphoreType.DMA((rows, levels)),
        ],
        compiler_params=pltpu.CompilerParams(collective_id=0, has_side_effects=True),
    )(block[:, None])


def reduce_seq(blocks):
    chips = blocks.shape[1] // 2
    split = blocks.reshape((blocks.shape[0], chips, 2) + blocks.shape[2:])
    core = lax.axis_index("core")
    keep = jnp.take(split, core, axis=2)
    send = jnp.take(split, 1 - core, axis=2)
    pair = (keep.astype(jnp.float32) + lax.ppermute(send, "core", SWAP).astype(jnp.float32))
    pair = pair.astype(jnp.bfloat16).transpose(1, 0, 2, 3)
    levels = lax.axis_size("level")
    by_row = pair.reshape((levels, chips // levels) + pair.shape[1:]).transpose(1, 0, 2, 3, 4)
    part = jnp.sum(exchange(by_row, "row").astype(jnp.float32), axis=0)
    return jnp.sum(exchange(part.astype(jnp.bfloat16), "level").astype(jnp.float32), axis=0)


def attend_block(
    queries, key_block, value_block, grad_block, query_pos, key_pos, query_seg, key_seg
):
    scores = jnp.einsum("bhge,lhe->hgbl", queries, key_block, preferred_element_type=jnp.float32)
    allowed = (
        (key_pos[None, :] <= query_pos[:, None])
        & (key_pos[None, :] > query_pos[:, None] - WINDOW)
        & (key_seg[None, :] == query_seg[:, None])
    )
    exp_scores = jnp.where(allowed[None, None], jnp.exp(scores), 0.0)
    probs = exp_scores / jnp.sum(exp_scores, axis=-1, keepdims=True)
    weights = probs.astype(jnp.bfloat16)
    attended = jnp.einsum(
        "hgbl,lhe->bhge", weights, value_block, preferred_element_type=jnp.float32
    ).astype(jnp.bfloat16)
    dprob = jnp.einsum(
        "bhge,lhe->hgbl", grad_block, value_block, preferred_element_type=jnp.float32
    )
    delta_row = jnp.sum(probs * dprob, axis=-1, keepdims=True)
    dscore = (probs * (dprob - delta_row)).astype(jnp.bfloat16)
    dquery = jnp.einsum("hgbl,lhe->bhge", dscore, key_block, preferred_element_type=jnp.float32)
    dkey = jnp.einsum("hgbl,bhge->lhe", dscore, queries, preferred_element_type=jnp.float32)
    dvalue = jnp.einsum("hgbl,bhge->lhe", weights, grad_block, preferred_element_type=jnp.float32)
    return (attended, dquery, dkey, dvalue)


def attention_kernel(pos_ref, gain_ref, q_ref, do_ref, k_ref, v_ref, out_ref, dq_ref, dkv_ref):
    rows = q_ref.shape[0]
    block = 256
    span = block + WINDOW
    dkv_ref[...] = jnp.zeros(dkv_ref.shape, jnp.float32)
    nt = (((1,), (1,)), ((), ()))
    tn = (((0,), (0,)), ((), ()))
    for b in range(rows // block):
        r0 = b * block
        k = k_ref[pl.ds(r0, span), :]
        v = v_ref[pl.ds(r0, span), :]
        row = lax.broadcasted_iota(jnp.int32, (block, span), 0)
        col = lax.broadcasted_iota(jnp.int32, (block, span), 1)
        query_pos = pos_ref[0] + r0 + row
        key_pos = pos_ref[0] - WINDOW + r0 + col
        allowed = (col <= row + WINDOW) & (col > row) & (key_pos >= 0)
        allowed = allowed & ((key_pos < pos_ref[1]) == (query_pos < pos_ref[1]))
        dk_acc = jnp.zeros((span, HD), jnp.float32)
        dv_acc = jnp.zeros((span, HD), jnp.float32)
        for g in range(2):
            raw = q_ref[pl.ds(r0, block), pl.ds(g * HD, HD)].astype(jnp.float32)
            mean_sq = jnp.mean(raw * raw, axis=1, keepdims=True)
            q = (raw * lax.rsqrt(mean_sq + epsilon) * gain_ref[...] * query_scale).astype(jnp.bfloat16)
            do = do_ref[pl.ds(r0, block), pl.ds(g * HD, HD)]
            scores = lax.dot_general(q, k, nt, preferred_element_type=jnp.float32)
            exp_scores = jnp.where(allowed, jnp.exp(scores), 0.0)
            probs = exp_scores / jnp.sum(exp_scores, axis=1, keepdims=True)
            weights = probs.astype(jnp.bfloat16)
            out_ref[pl.ds(r0, block), pl.ds(g * HD, HD)] = jnp.dot(
                weights, v, preferred_element_type=jnp.float32
            ).astype(out_ref.dtype)
            dprob = lax.dot_general(do, v, nt, preferred_element_type=jnp.float32)
            delta_row = jnp.sum(probs * dprob, axis=1, keepdims=True)
            dscore = (probs * (dprob - delta_row)).astype(jnp.bfloat16)
            dq_ref[pl.ds(r0, block), pl.ds(g * HD, HD)] = jnp.dot(
                dscore, k, preferred_element_type=jnp.float32
            )
            dk_acc = dk_acc + lax.dot_general(dscore, q, tn, preferred_element_type=jnp.float32)
            dv_acc = dv_acc + lax.dot_general(weights, do, tn, preferred_element_type=jnp.float32)
        dkv_ref[0, pl.ds(r0, span), :] += dk_acc
        dkv_ref[1, pl.ds(r0, span), :] += dv_acc


def attend(positions, gain, q_raw, grad_out, keys, values):
    rows = q_raw.shape[0]
    spec = pl.BlockSpec(memory_space=pltpu.VMEM)
    return pl.pallas_call(
        attention_kernel,
        out_shape=(
            jax.ShapeDtypeStruct((rows, 2 * HD), jnp.bfloat16),
            jax.ShapeDtypeStruct((rows, 2 * HD), jnp.float32),
            jax.ShapeDtypeStruct((2, keys.shape[0], HD), jnp.float32),
        ),
        in_specs=[pl.BlockSpec(memory_space=pltpu.SMEM)] + [spec] * 5,
        out_specs=(spec, spec, spec),
        cost_estimate=pl.CostEstimate(
            flops=12 * rows * (rows + WINDOW) * HD * 2, transcendentals=2 * rows * (rows + WINDOW),
            bytes_accessed=16 * rows * HD * 4,
        ),
    )(positions, gain, q_raw, grad_out, keys, values)


def body(normed, q_raw, key_weight, value_weight, q_gain, k_gain, segment_ids, grad_out):
    rows_here = normed.shape[0]
    feats = normed.shape[1]
    heads_here = q_raw.shape[1] // (2 * HD)
    n_seq = lax.axis_size(SEQ)
    n_uly = lax.axis_size("uly")
    col_block = key_weight.shape[1]
    seq_index = lax.axis_index(SEQ)
    base_row = seq_index * rows_here
    pair_t = jnp.stack([key_weight.T, value_weight.T])
    weight_t = gather_seq(pair_t).reshape(2, n_seq * col_block, feats)
    terms = lax.dot_general(
        normed, weight_t, (((1,), (2,)), ((), ())), preferred_element_type=jnp.float32
    ).astype(jnp.bfloat16)
    terms = terms.reshape(rows_here, 2, n_uly, heads_here * HD).transpose(2, 0, 1, 3)
    received = exchange(terms, "uly")
    raw_pair = jnp.sum(received.astype(jnp.float32), axis=0)
    key_raw = raw_pair[:, 0]
    value_raw = raw_pair[:, 1]
    key_in = key_raw.reshape(rows_here, heads_here, HD)
    keys_bf = normalize(key_in, k_gain, 1.0).astype(jnp.bfloat16)
    values_bf = value_raw.reshape(rows_here, heads_here, HD).astype(jnp.bfloat16)
    query_in = q_raw.astype(jnp.float32).reshape(rows_here, heads_here, 2, HD)
    queries = normalize(query_in, q_gain, query_scale).astype(jnp.bfloat16)
    grad_heads = grad_out.reshape(rows_here, heads_here, 2, HD)
    stacked = jnp.stack([keys_bf, values_bf])
    behind = from_behind(stacked, SEQ, 1)
    extended = jnp.concatenate([behind, stacked], axis=1).reshape(2, WINDOW + rows_here, HD)
    boundary = jnp.sum((segment_ids == 0).astype(jnp.int32))
    positions = jnp.stack([base_row.astype(jnp.int32), boundary])
    attention, dquery, grad_acc = attend(
        positions,
        q_gain.reshape(1, HD),
        q_raw,
        grad_out,
        extended[0],
        extended[1],
    )
    dquery = dquery.reshape(rows_here, heads_here, 2, HD)
    grad_acc = grad_acc.reshape(2, WINDOW + rows_here, heads_here, HD)
    own_grads = grad_acc[:, WINDOW:]
    offset_row = 0
    distance = 1
    first_row = max(0, distance * rows_here - WINDOW)
    piece_rows = rows_here - first_row
    outgoing = grad_acc[:, offset_row : offset_row + piece_rows]
    returned = from_behind(outgoing.astype(jnp.bfloat16), SEQ, -distance).astype(outgoing.dtype)
    own_grads = own_grads.at[:, first_row:].add(returned)
    _, pull_query = jax.vjp(lambda raw_vals: normalize(raw_vals, q_gain, query_scale), query_in)
    grad_q = pull_query(dquery)[0].astype(jnp.bfloat16).reshape(rows_here, 2 * heads_here * HD)
    _, pull_key = jax.vjp(lambda raw_vals: normalize(raw_vals, k_gain, 1.0), key_in)
    key_grad = pull_key(own_grads[0])[0].astype(jnp.bfloat16).reshape(rows_here, heads_here * HD)
    value_grad = own_grads[1].astype(jnp.bfloat16).reshape(rows_here, heads_here * HD)
    grads_all = gather_all(jnp.stack([key_grad, value_grad], axis=1), "uly")
    weight_heads = weight_t.reshape(2, n_uly, heads_here * HD, feats)
    grad_normed = jnp.einsum(
        "htkc,khcf->tf", grads_all, weight_heads, preferred_element_type=jnp.float32
    ).astype(jnp.bfloat16)
    weight_part = jnp.einsum(
        "htkc,tf->khcf", grads_all, normed, preferred_element_type=jnp.float32
    ).astype(jnp.bfloat16)
    summed = reduce_seq(weight_part.reshape(2, n_seq, col_block, feats))
    grad_key_weight = summed[0].T
    grad_value_weight = summed[1].T
    return (attention, grad_normed, grad_q, grad_key_weight, grad_value_weight)


def solution(mesh):
    n_seq, n_uly = mesh.shape["seq"], mesh.shape["uly"]
    rows = 4
    fine = jax.sharding.Mesh(
        mesh.devices.reshape(n_seq // (2 * rows), rows, 2, n_uly), ("level", "row", "core", "uly")
    )
    return jax.shard_map(
        body,
        mesh=fine,
        in_specs=(
            P(SEQ, "uly"),
            P(SEQ, "uly"),
            P("uly", SEQ),
            P("uly", SEQ),
            P(),
            P(),
            P(),
            P(SEQ, "uly"),
        ),
        out_specs=(
            P(SEQ, "uly"),
            P(SEQ, "uly"),
            P(SEQ, "uly"),
            P("uly", SEQ),
            P("uly", SEQ),
        ),
        check_vma=False,
    )
```

```python
import functools

import jax
import jax.numpy as jnp
from jax import lax
from jax.experimental import pallas as pl
from jax.experimental.pallas import tpu as pltpu
from jax.sharding import PartitionSpec as P

HD = 128
WINDOW = 1024


epsilon = 1e-06
query_scale = 168.0 ** (-0.5)


def from_behind(array, axis, by):
    devices = lax.axis_size(axis)
    pairs = [(i, i + by) for i in range(devices) if 0 <= i + by < devices]
    return lax.ppermute(array, axis, pairs)


def normalize(raw_vals, gain, factor):
    mean_sq = jnp.mean(raw_vals * raw_vals, axis=-1, keepdims=True)
    return raw_vals * lax.rsqrt(mean_sq + epsilon) * gain * factor


def exchange(blocks, axis):
    return lax.all_to_all(blocks, axis, 0, 0)


def gather_all(block, axis):
    count = lax.axis_size(axis)
    return exchange(jnp.broadcast_to(block[None], (count,) + block.shape), axis)


SEQ = ("level", "row", "core")
CHIP = ("level", "row")
SWAP = [(0, 1), (1, 0)]


def gather_kernel(levels, rows, x_ref, out_ref, local_sem, z_send, z_recv, x_send, x_recv, f_send, f_recv):
    level = lax.axis_index("level")
    row = lax.axis_index("row")
    core = lax.axis_index("core")
    uly = lax.axis_index("uly")
    other = 1 - core
    mesh_ids = pl.DeviceIdType.MESH

    def slot(at_level, at_row):
        return (lax.rem(at_level, levels) * rows + lax.rem(at_row, rows)) * 2 + core

    def window(index):
        return out_ref.at[:, pl.ds(index, 1)]

    def to_partner(index, dx, dz):
        return pltpu.make_async_remote_copy(
            src_ref=window(index),
            dst_ref=window(index),
            send_sem=f_send.at[dx, dz],
            recv_sem=f_recv.at[dx, dz],
            device_id=(level, row, other, uly),
            device_id_type=mesh_ids,
        )

    barrier = pltpu.get_barrier_semaphore()
    for dz in range(1, levels):
        peer = (lax.rem(level + dz, levels), row, core, uly)
        pl.semaphore_signal(barrier, 1, device_id=peer, device_id_type=mesh_ids)
    for dx in range(1, rows):
        peer = (level, lax.rem(row + dx, rows), core, uly)
        pl.semaphore_signal(barrier, 1, device_id=peer, device_id_type=mesh_ids)
    pl.semaphore_signal(barrier, 1, device_id=(level, row, other, uly), device_id_type=mesh_ids)
    pl.semaphore_wait(barrier, levels + rows - 1)
    mine = slot(level, row)
    local = pltpu.make_async_copy(x_ref, window(mine), local_sem)
    local.start()
    z_copies = {}
    for dz in range(1, levels):
        z_copies[dz] = pltpu.make_async_remote_copy(
            src_ref=x_ref,
            dst_ref=window(mine),
            send_sem=z_send.at[dz],
            recv_sem=z_recv.at[dz],
            device_id=(lax.rem(level + dz, levels), row, core, uly),
            device_id_type=mesh_ids,
        )
        z_copies[dz].start()
    local.wait()
    x_moves = {}
    forwards = []

    def spread(dz, index):
        for dx in range(1, rows):
            move = pltpu.make_async_remote_copy(
                src_ref=window(index),
                dst_ref=window(index),
                send_sem=x_send.at[dx, dz],
                recv_sem=x_recv.at[dx, dz],
                device_id=(level, lax.rem(row + dx, rows), core, uly),
                device_id_type=mesh_ids,
            )
            move.start()
            x_moves[dx, dz] = move
        forward = to_partner(index, 0, dz)
        forward.start()
        forwards.append(forward)

    spread(0, mine)
    for dz in range(1, levels):
        z_copies[dz].wait_recv()
        spread(dz, slot(level + levels - dz, row))
    for dx in range(1, rows):
        for dz in range(levels):
            x_moves[dx, dz].wait_recv()
            forward = to_partner(slot(level + levels - dz, row + rows - dx), dx, dz)
            forward.start()
            forwards.append(forward)
    for dz in range(1, levels):
        z_copies[dz].wait_send()
    for move in x_moves.values():
        move.wait_send()
    for forward in forwards:
        forward.wait()


def gather_seq(block):
    levels = lax.axis_size("level")
    rows = lax.axis_size("row")
    spec = pl.BlockSpec(memory_space=pltpu.VMEM)
    return pl.pallas_call(
        functools.partial(gather_kernel, levels, rows),
        out_shape=jax.ShapeDtypeStruct((block.shape[0], 2 * levels * rows) + block.shape[1:], block.dtype),
        in_specs=[spec],
        out_specs=spec,
        scratch_shapes=[
            pltpu.SemaphoreType.DMA(()),
            pltpu.SemaphoreType.DMA((levels,)),
            pltpu.SemaphoreType.DMA((levels,)),
            pltpu.SemaphoreType.DMA((rows, levels)),
            pltpu.SemaphoreType.DMA((rows, levels)),
            pltpu.SemaphoreType.DMA((rows, levels)),
            pltpu.SemaphoreType.DMA((rows, levels)),
        ],
        compiler_params=pltpu.CompilerParams(collective_id=0, has_side_effects=True),
    )(block[:, None])


def reduce_seq(halves):
    core = lax.axis_index("core")
    keep = lax.dynamic_index_in_dim(halves, core, 0, keepdims=False)
    send = lax.dynamic_index_in_dim(halves, 1 - core, 0, keepdims=False)
    pair = (keep.astype(jnp.float32) + lax.ppermute(send, "core", SWAP).astype(jnp.float32))
    pair = pair.astype(jnp.bfloat16).transpose(1, 0, 2, 3)
    chips = pair.shape[0]
    levels = lax.axis_size("level")
    by_row = pair.reshape((levels, chips // levels) + pair.shape[1:]).transpose(1, 0, 2, 3, 4)
    part = jnp.sum(exchange(by_row, "row").astype(jnp.float32), axis=0)
    return jnp.sum(exchange(part.astype(jnp.bfloat16), "level").astype(jnp.float32), axis=0)


def attend_block(
    queries, key_block, value_block, grad_block, query_pos, key_pos, query_seg, key_seg
):
    scores = jnp.einsum("bhge,lhe->hgbl", queries, key_block, preferred_element_type=jnp.float32)
    allowed = (
        (key_pos[None, :] <= query_pos[:, None])
        & (key_pos[None, :] > query_pos[:, None] - WINDOW)
        & (key_seg[None, :] == query_seg[:, None])
    )
    exp_scores = jnp.where(allowed[None, None], jnp.exp(scores), 0.0)
    probs = exp_scores / jnp.sum(exp_scores, axis=-1, keepdims=True)
    weights = probs.astype(jnp.bfloat16)
    attended = jnp.einsum(
        "hgbl,lhe->bhge", weights, value_block, preferred_element_type=jnp.float32
    ).astype(jnp.bfloat16)
    dprob = jnp.einsum(
        "bhge,lhe->hgbl", grad_block, value_block, preferred_element_type=jnp.float32
    )
    delta_row = jnp.sum(probs * dprob, axis=-1, keepdims=True)
    dscore = (probs * (dprob - delta_row)).astype(jnp.bfloat16)
    dquery = jnp.einsum("hgbl,lhe->bhge", dscore, key_block, preferred_element_type=jnp.float32)
    dkey = jnp.einsum("hgbl,bhge->lhe", dscore, queries, preferred_element_type=jnp.float32)
    dvalue = jnp.einsum("hgbl,bhge->lhe", weights, grad_block, preferred_element_type=jnp.float32)
    return (attended, dquery, dkey, dvalue)


def attention_kernel(pos_ref, gain_ref, q_ref, do_ref, k_ref, v_ref, out_ref, dq_ref, dkv_ref):
    rows = q_ref.shape[0]
    block = 256
    span = block + WINDOW
    dkv_ref[...] = jnp.zeros(dkv_ref.shape, jnp.float32)
    nt = (((1,), (1,)), ((), ()))
    tn = (((0,), (0,)), ((), ()))
    for b in range(rows // block):
        r0 = b * block
        k = k_ref[pl.ds(r0, span), :]
        v = v_ref[pl.ds(r0, span), :]
        row = lax.broadcasted_iota(jnp.int32, (block, span), 0)
        col = lax.broadcasted_iota(jnp.int32, (block, span), 1)
        query_pos = pos_ref[0] + r0 + row
        key_pos = pos_ref[0] - WINDOW + r0 + col
        allowed = (col <= row + WINDOW) & (col > row) & (key_pos >= 0)
        allowed = allowed & ((key_pos < pos_ref[1]) == (query_pos < pos_ref[1]))
        dk_acc = jnp.zeros((span, HD), jnp.float32)
        dv_acc = jnp.zeros((span, HD), jnp.float32)
        for g in range(2):
            raw = q_ref[pl.ds(r0, block), pl.ds(g * HD, HD)].astype(jnp.float32)
            mean_sq = jnp.mean(raw * raw, axis=1, keepdims=True)
            q = (raw * lax.rsqrt(mean_sq + epsilon) * gain_ref[...] * query_scale).astype(jnp.bfloat16)
            do = do_ref[pl.ds(r0, block), pl.ds(g * HD, HD)]
            scores = lax.dot_general(q, k, nt, preferred_element_type=jnp.float32)
            exp_scores = jnp.where(allowed, jnp.exp(scores), 0.0)
            probs = exp_scores / jnp.sum(exp_scores, axis=1, keepdims=True)
            weights = probs.astype(jnp.bfloat16)
            out_ref[pl.ds(r0, block), pl.ds(g * HD, HD)] = jnp.dot(
                weights, v, preferred_element_type=jnp.float32
            ).astype(out_ref.dtype)
            dprob = lax.dot_general(do, v, nt, preferred_element_type=jnp.float32)
            delta_row = jnp.sum(probs * dprob, axis=1, keepdims=True)
            dscore = (probs * (dprob - delta_row)).astype(jnp.bfloat16)
            dq_ref[pl.ds(r0, block), pl.ds(g * HD, HD)] = jnp.dot(
                dscore, k, preferred_element_type=jnp.float32
            )
            dk_acc = dk_acc + lax.dot_general(dscore, q, tn, preferred_element_type=jnp.float32)
            dv_acc = dv_acc + lax.dot_general(weights, do, tn, preferred_element_type=jnp.float32)
        dkv_ref[0, pl.ds(r0, span), :] += dk_acc
        dkv_ref[1, pl.ds(r0, span), :] += dv_acc


def attend(positions, gain, q_raw, grad_out, keys, values):
    rows = q_raw.shape[0]
    spec = pl.BlockSpec(memory_space=pltpu.VMEM)
    return pl.pallas_call(
        attention_kernel,
        out_shape=(
            jax.ShapeDtypeStruct((rows, 2 * HD), jnp.bfloat16),
            jax.ShapeDtypeStruct((rows, 2 * HD), jnp.float32),
            jax.ShapeDtypeStruct((2, keys.shape[0], HD), jnp.float32),
        ),
        in_specs=[pl.BlockSpec(memory_space=pltpu.SMEM)] + [spec] * 5,
        out_specs=(spec, spec, spec),
        cost_estimate=pl.CostEstimate(
            flops=12 * rows * (rows + WINDOW) * HD * 2, transcendentals=2 * rows * (rows + WINDOW),
            bytes_accessed=16 * rows * HD * 4,
        ),
    )(positions, gain, q_raw, grad_out, keys, values)


def body(normed, q_raw, key_weight, value_weight, q_gain, k_gain, segment_ids, grad_out):
    rows_here = normed.shape[0]
    feats = normed.shape[1]
    heads_here = q_raw.shape[1] // (2 * HD)
    n_seq = lax.axis_size(SEQ)
    n_uly = lax.axis_size("uly")
    col_block = key_weight.shape[1]
    seq_index = lax.axis_index(SEQ)
    base_row = seq_index * rows_here
    pair_t = jnp.stack([key_weight.T, value_weight.T])
    weight_t = gather_seq(pair_t).reshape(2, n_seq * col_block, feats)
    terms = lax.dot_general(
        normed, weight_t, (((1,), (2,)), ((), ())), preferred_element_type=jnp.float32
    ).astype(jnp.bfloat16)
    terms = terms.reshape(rows_here, 2, n_uly, heads_here * HD).transpose(2, 0, 1, 3)
    received = exchange(terms, "uly")
    raw_pair = jnp.sum(received.astype(jnp.float32), axis=0)
    key_raw = raw_pair[:, 0]
    value_raw = raw_pair[:, 1]
    key_in = key_raw.reshape(rows_here, heads_here, HD)
    keys_bf = normalize(key_in, k_gain, 1.0).astype(jnp.bfloat16)
    values_bf = value_raw.reshape(rows_here, heads_here, HD).astype(jnp.bfloat16)
    query_in = q_raw.astype(jnp.float32).reshape(rows_here, heads_here, 2, HD)
    queries = normalize(query_in, q_gain, query_scale).astype(jnp.bfloat16)
    grad_heads = grad_out.reshape(rows_here, heads_here, 2, HD)
    stacked = jnp.stack([keys_bf, values_bf])
    behind = from_behind(stacked, SEQ, 1)
    extended = jnp.concatenate([behind, stacked], axis=1).reshape(2, WINDOW + rows_here, HD)
    boundary = jnp.sum((segment_ids == 0).astype(jnp.int32))
    positions = jnp.stack([base_row.astype(jnp.int32), boundary])
    attention, dquery, grad_acc = attend(
        positions,
        q_gain.reshape(1, HD),
        q_raw,
        grad_out,
        extended[0],
        extended[1],
    )
    dquery = dquery.reshape(rows_here, heads_here, 2, HD)
    grad_acc = grad_acc.reshape(2, WINDOW + rows_here, heads_here, HD)
    own_grads = grad_acc[:, WINDOW:]
    offset_row = 0
    distance = 1
    first_row = max(0, distance * rows_here - WINDOW)
    piece_rows = rows_here - first_row
    outgoing = grad_acc[:, offset_row : offset_row + piece_rows]
    returned = from_behind(outgoing.astype(jnp.bfloat16), SEQ, -distance).astype(outgoing.dtype)
    own_grads = own_grads.at[:, first_row:].add(returned)
    _, pull_query = jax.vjp(lambda raw_vals: normalize(raw_vals, q_gain, query_scale), query_in)
    grad_q = pull_query(dquery)[0].astype(jnp.bfloat16).reshape(rows_here, 2 * heads_here * HD)
    _, pull_key = jax.vjp(lambda raw_vals: normalize(raw_vals, k_gain, 1.0), key_in)
    key_grad = pull_key(own_grads[0])[0].astype(jnp.bfloat16).reshape(rows_here, heads_here * HD)
    value_grad = own_grads[1].astype(jnp.bfloat16).reshape(rows_here, heads_here * HD)
    grads_all = gather_all(jnp.stack([key_grad, value_grad], axis=1), "uly")
    weight_heads = weight_t.reshape(2, n_uly, heads_here * HD, feats)
    grad_normed = jnp.einsum(
        "htkc,khcf->tf", grads_all, weight_heads, preferred_element_type=jnp.float32
    ).astype(jnp.bfloat16)
    per_head = HD // col_block
    g6 = grads_all.reshape(n_uly, rows_here, 2, per_head // 2, 2, col_block)
    halves = jnp.einsum(
        "htkaoc,tf->okhacf", g6, normed, preferred_element_type=jnp.float32
    ).astype(jnp.bfloat16)
    summed = reduce_seq(halves.reshape(2, 2, n_seq // 2, col_block, feats))
    grad_key_weight = summed[0].T
    grad_value_weight = summed[1].T
    return (attention, grad_normed, grad_q, grad_key_weight, grad_value_weight)


def solution(mesh):
    n_seq, n_uly = mesh.shape["seq"], mesh.shape["uly"]
    rows = 4
    fine = jax.sharding.Mesh(
        mesh.devices.reshape(n_seq // (2 * rows), rows, 2, n_uly), ("level", "row", "core", "uly")
    )
    return jax.shard_map(
        body,
        mesh=fine,
        in_specs=(
            P(SEQ, "uly"),
            P(SEQ, "uly"),
            P("uly", SEQ),
            P("uly", SEQ),
            P(),
            P(),
            P(),
            P(SEQ, "uly"),
        ),
        out_specs=(
            P(SEQ, "uly"),
            P(SEQ, "uly"),
            P(SEQ, "uly"),
            P("uly", SEQ),
            P("uly", SEQ),
        ),
        check_vma=False,
    )
```

```python
import functools

import jax
import jax.numpy as jnp
from jax import lax
from jax.experimental import pallas as pl
from jax.experimental.pallas import tpu as pltpu
from jax.sharding import PartitionSpec as P

HD = 128
WINDOW = 1024


epsilon = 1e-06
query_scale = 168.0 ** (-0.5)


def from_behind(array, axis, by):
    devices = lax.axis_size(axis)
    pairs = [(i, i + by) for i in range(devices) if 0 <= i + by < devices]
    return lax.ppermute(array, axis, pairs)


def normalize(raw_vals, gain, factor):
    mean_sq = jnp.mean(raw_vals * raw_vals, axis=-1, keepdims=True)
    return raw_vals * lax.rsqrt(mean_sq + epsilon) * gain * factor


def exchange(blocks, axis):
    return lax.all_to_all(blocks, axis, 0, 0)


def gather_all(block, axis):
    count = lax.axis_size(axis)
    return exchange(jnp.broadcast_to(block[None], (count,) + block.shape), axis)


SEQ = ("level", "row", "core")
CHIP = ("level", "row")
SWAP = [(0, 1), (1, 0)]


def gather_kernel(levels, rows, x_ref, out_ref, local_sem, z_send, z_recv, x_send, x_recv, f_send, f_recv):
    level = lax.axis_index("level")
    row = lax.axis_index("row")
    core = lax.axis_index("core")
    uly = lax.axis_index("uly")
    other = 1 - core
    mesh_ids = pl.DeviceIdType.MESH

    def slot(at_level, at_row):
        return (lax.rem(at_level, levels) * rows + lax.rem(at_row, rows)) * 2 + core

    def window(index):
        return out_ref.at[:, pl.ds(index, 1)]

    def to_partner(index, dx, dz):
        return pltpu.make_async_remote_copy(
            src_ref=window(index),
            dst_ref=window(index),
            send_sem=f_send.at[dx, dz],
            recv_sem=f_recv.at[dx, dz],
            device_id=(level, row, other, uly),
            device_id_type=mesh_ids,
        )

    barrier = pltpu.get_barrier_semaphore()
    for dz in range(1, levels):
        peer = (lax.rem(level + dz, levels), row, core, uly)
        pl.semaphore_signal(barrier, 1, device_id=peer, device_id_type=mesh_ids)
    for dx in range(1, rows):
        peer = (level, lax.rem(row + dx, rows), core, uly)
        pl.semaphore_signal(barrier, 1, device_id=peer, device_id_type=mesh_ids)
    pl.semaphore_signal(barrier, 1, device_id=(level, row, other, uly), device_id_type=mesh_ids)
    pl.semaphore_wait(barrier, levels + rows - 1)
    mine = slot(level, row)
    local = pltpu.make_async_copy(x_ref, window(mine), local_sem)
    local.start()
    z_copies = {}
    for dz in range(1, levels):
        z_copies[dz] = pltpu.make_async_remote_copy(
            src_ref=x_ref,
            dst_ref=window(mine),
            send_sem=z_send.at[dz],
            recv_sem=z_recv.at[dz],
            device_id=(lax.rem(level + dz, levels), row, core, uly),
            device_id_type=mesh_ids,
        )
        z_copies[dz].start()
    local.wait()
    x_moves = {}
    forwards = []

    def spread(dz, index):
        for dx in range(1, rows):
            move = pltpu.make_async_remote_copy(
                src_ref=window(index),
                dst_ref=window(index),
                send_sem=x_send.at[dx, dz],
                recv_sem=x_recv.at[dx, dz],
                device_id=(level, lax.rem(row + dx, rows), core, uly),
                device_id_type=mesh_ids,
            )
            move.start()
            x_moves[dx, dz] = move
        forward = to_partner(index, 0, dz)
        forward.start()
        forwards.append(forward)

    spread(0, mine)
    for dz in range(1, levels):
        z_copies[dz].wait_recv()
        spread(dz, slot(level + levels - dz, row))
    for dx in range(1, rows):
        for dz in range(levels):
            x_moves[dx, dz].wait_recv()
            forward = to_partner(slot(level + levels - dz, row + rows - dx), dx, dz)
            forward.start()
            forwards.append(forward)
    for dz in range(1, levels):
        z_copies[dz].wait_send()
    for move in x_moves.values():
        move.wait_send()
    for forward in forwards:
        forward.wait()


def gather_seq(block):
    levels = lax.axis_size("level")
    rows = lax.axis_size("row")
    spec = pl.BlockSpec(memory_space=pltpu.VMEM)
    return pl.pallas_call(
        functools.partial(gather_kernel, levels, rows),
        out_shape=jax.ShapeDtypeStruct((block.shape[0], 2 * levels * rows) + block.shape[1:], block.dtype),
        in_specs=[spec],
        out_specs=spec,
        scratch_shapes=[
            pltpu.SemaphoreType.DMA(()),
            pltpu.SemaphoreType.DMA((levels,)),
            pltpu.SemaphoreType.DMA((levels,)),
            pltpu.SemaphoreType.DMA((rows, levels)),
            pltpu.SemaphoreType.DMA((rows, levels)),
            pltpu.SemaphoreType.DMA((rows, levels)),
            pltpu.SemaphoreType.DMA((rows, levels)),
        ],
        compiler_params=pltpu.CompilerParams(collective_id=0, has_side_effects=True),
    )(block[:, None])


def reduce_seq(blocks):
    chips = blocks.shape[1] // 2
    split = blocks.reshape((blocks.shape[0], chips, 2) + blocks.shape[2:])
    core = lax.axis_index("core")
    keep = jnp.take(split, core, axis=2)
    send = jnp.take(split, 1 - core, axis=2)
    pair = (keep.astype(jnp.float32) + lax.ppermute(send, "core", SWAP).astype(jnp.float32))
    pair = pair.astype(jnp.bfloat16).transpose(1, 0, 2, 3)
    levels = lax.axis_size("level")
    by_row = pair.reshape((levels, chips // levels) + pair.shape[1:]).transpose(1, 0, 2, 3, 4)
    part = jnp.sum(exchange(by_row, "row").astype(jnp.float32), axis=0)
    return jnp.sum(exchange(part.astype(jnp.bfloat16), "level").astype(jnp.float32), axis=0)


def attend_block(
    queries, key_block, value_block, grad_block, query_pos, key_pos, query_seg, key_seg
):
    scores = jnp.einsum("bhge,lhe->hgbl", queries, key_block, preferred_element_type=jnp.float32)
    allowed = (
        (key_pos[None, :] <= query_pos[:, None])
        & (key_pos[None, :] > query_pos[:, None] - WINDOW)
        & (key_seg[None, :] == query_seg[:, None])
    )
    exp_scores = jnp.where(allowed[None, None], jnp.exp(scores), 0.0)
    probs = exp_scores / jnp.sum(exp_scores, axis=-1, keepdims=True)
    weights = probs.astype(jnp.bfloat16)
    attended = jnp.einsum(
        "hgbl,lhe->bhge", weights, value_block, preferred_element_type=jnp.float32
    ).astype(jnp.bfloat16)
    dprob = jnp.einsum(
        "bhge,lhe->hgbl", grad_block, value_block, preferred_element_type=jnp.float32
    )
    delta_row = jnp.sum(probs * dprob, axis=-1, keepdims=True)
    dscore = (probs * (dprob - delta_row)).astype(jnp.bfloat16)
    dquery = jnp.einsum("hgbl,lhe->bhge", dscore, key_block, preferred_element_type=jnp.float32)
    dkey = jnp.einsum("hgbl,bhge->lhe", dscore, queries, preferred_element_type=jnp.float32)
    dvalue = jnp.einsum("hgbl,bhge->lhe", weights, grad_block, preferred_element_type=jnp.float32)
    return (attended, dquery, dkey, dvalue)


def attention_kernel(pos_ref, gain_ref, q_ref, do_ref, k_ref, v_ref, out_ref, dq_ref, dkv_ref):
    rows = q_ref.shape[0]
    block = 128
    span = block + WINDOW
    dkv_ref[...] = jnp.zeros(dkv_ref.shape, jnp.float32)
    nt = (((1,), (1,)), ((), ()))
    tn = (((0,), (0,)), ((), ()))
    for b in range(rows // block):
        r0 = b * block
        k = k_ref[pl.ds(r0, span), :]
        v = v_ref[pl.ds(r0, span), :]
        row = lax.broadcasted_iota(jnp.int32, (block, span), 0)
        col = lax.broadcasted_iota(jnp.int32, (block, span), 1)
        query_pos = pos_ref[0] + r0 + row
        key_pos = pos_ref[0] - WINDOW + r0 + col
        allowed = (col <= row + WINDOW) & (col > row) & (key_pos >= 0)
        allowed = allowed & ((key_pos < pos_ref[1]) == (query_pos < pos_ref[1]))
        dk_acc = jnp.zeros((span, HD), jnp.float32)
        dv_acc = jnp.zeros((span, HD), jnp.float32)
        for g in range(2):
            raw = q_ref[pl.ds(r0, block), pl.ds(g * HD, HD)].astype(jnp.float32)
            mean_sq = jnp.mean(raw * raw, axis=1, keepdims=True)
            q = (raw * lax.rsqrt(mean_sq + epsilon) * gain_ref[...] * query_scale).astype(jnp.bfloat16)
            do = do_ref[pl.ds(r0, block), pl.ds(g * HD, HD)]
            scores = lax.dot_general(q, k, nt, preferred_element_type=jnp.float32)
            exp_scores = jnp.where(allowed, jnp.exp(scores), 0.0)
            probs = exp_scores / jnp.sum(exp_scores, axis=1, keepdims=True)
            weights = probs.astype(jnp.bfloat16)
            out_ref[pl.ds(r0, block), pl.ds(g * HD, HD)] = jnp.dot(
                weights, v, preferred_element_type=jnp.float32
            ).astype(out_ref.dtype)
            dprob = lax.dot_general(do, v, nt, preferred_element_type=jnp.float32)
            delta_row = jnp.sum(probs * dprob, axis=1, keepdims=True)
            dscore = (probs * (dprob - delta_row)).astype(jnp.bfloat16)
            dq_ref[pl.ds(r0, block), pl.ds(g * HD, HD)] = jnp.dot(
                dscore, k, preferred_element_type=jnp.float32
            )
            dk_acc = dk_acc + lax.dot_general(dscore, q, tn, preferred_element_type=jnp.float32)
            dv_acc = dv_acc + lax.dot_general(weights, do, tn, preferred_element_type=jnp.float32)
        dkv_ref[0, pl.ds(r0, span), :] += dk_acc
        dkv_ref[1, pl.ds(r0, span), :] += dv_acc


def attend(positions, gain, q_raw, grad_out, keys, values):
    rows = q_raw.shape[0]
    spec = pl.BlockSpec(memory_space=pltpu.VMEM)
    return pl.pallas_call(
        attention_kernel,
        out_shape=(
            jax.ShapeDtypeStruct((rows, 2 * HD), jnp.bfloat16),
            jax.ShapeDtypeStruct((rows, 2 * HD), jnp.float32),
            jax.ShapeDtypeStruct((2, keys.shape[0], HD), jnp.float32),
        ),
        in_specs=[pl.BlockSpec(memory_space=pltpu.SMEM)] + [spec] * 5,
        out_specs=(spec, spec, spec),
        cost_estimate=pl.CostEstimate(
            flops=12 * rows * (rows + WINDOW) * HD * 2, transcendentals=2 * rows * (rows + WINDOW),
            bytes_accessed=16 * rows * HD * 4,
        ),
    )(positions, gain, q_raw, grad_out, keys, values)


def body(normed, q_raw, key_weight, value_weight, q_gain, k_gain, segment_ids, grad_out):
    rows_here = normed.shape[0]
    feats = normed.shape[1]
    heads_here = q_raw.shape[1] // (2 * HD)
    n_seq = lax.axis_size(SEQ)
    n_uly = lax.axis_size("uly")
    col_block = key_weight.shape[1]
    seq_index = lax.axis_index(SEQ)
    base_row = seq_index * rows_here
    pair_t = jnp.stack([key_weight.T, value_weight.T])
    weight_t = gather_seq(pair_t).reshape(2, n_seq * col_block, feats)
    terms = lax.dot_general(
        normed, weight_t, (((1,), (2,)), ((), ())), preferred_element_type=jnp.float32
    ).astype(jnp.bfloat16)
    terms = terms.reshape(rows_here, 2, n_uly, heads_here * HD).transpose(2, 0, 1, 3)
    received = exchange(terms, "uly")
    raw_pair = jnp.sum(received.astype(jnp.float32), axis=0)
    key_raw = raw_pair[:, 0]
    value_raw = raw_pair[:, 1]
    key_in = key_raw.reshape(rows_here, heads_here, HD)
    keys_bf = normalize(key_in, k_gain, 1.0).astype(jnp.bfloat16)
    values_bf = value_raw.reshape(rows_here, heads_here, HD).astype(jnp.bfloat16)
    query_in = q_raw.astype(jnp.float32).reshape(rows_here, heads_here, 2, HD)
    queries = normalize(query_in, q_gain, query_scale).astype(jnp.bfloat16)
    grad_heads = grad_out.reshape(rows_here, heads_here, 2, HD)
    stacked = jnp.stack([keys_bf, values_bf])
    behind = from_behind(stacked, SEQ, 1)
    extended = jnp.concatenate([behind, stacked], axis=1).reshape(2, WINDOW + rows_here, HD)
    boundary = jnp.sum((segment_ids == 0).astype(jnp.int32))
    positions = jnp.stack([base_row.astype(jnp.int32), boundary])
    attention, dquery, grad_acc = attend(
        positions,
        q_gain.reshape(1, HD),
        q_raw,
        grad_out,
        extended[0],
        extended[1],
    )
    dquery = dquery.reshape(rows_here, heads_here, 2, HD)
    grad_acc = grad_acc.reshape(2, WINDOW + rows_here, heads_here, HD)
    own_grads = grad_acc[:, WINDOW:]
    offset_row = 0
    distance = 1
    first_row = max(0, distance * rows_here - WINDOW)
    piece_rows = rows_here - first_row
    outgoing = grad_acc[:, offset_row : offset_row + piece_rows]
    returned = from_behind(outgoing.astype(jnp.bfloat16), SEQ, -distance).astype(outgoing.dtype)
    own_grads = own_grads.at[:, first_row:].add(returned)
    _, pull_query = jax.vjp(lambda raw_vals: normalize(raw_vals, q_gain, query_scale), query_in)
    grad_q = pull_query(dquery)[0].astype(jnp.bfloat16).reshape(rows_here, 2 * heads_here * HD)
    _, pull_key = jax.vjp(lambda raw_vals: normalize(raw_vals, k_gain, 1.0), key_in)
    key_grad = pull_key(own_grads[0])[0].astype(jnp.bfloat16).reshape(rows_here, heads_here * HD)
    value_grad = own_grads[1].astype(jnp.bfloat16).reshape(rows_here, heads_here * HD)
    grads_all = gather_all(jnp.stack([key_grad, value_grad], axis=1), "uly")
    weight_heads = weight_t.reshape(2, n_uly, heads_here * HD, feats)
    grad_normed = jnp.einsum(
        "htkc,khcf->tf", grads_all, weight_heads, preferred_element_type=jnp.float32
    ).astype(jnp.bfloat16)
    weight_part = jnp.einsum(
        "htkc,tf->khcf", grads_all, normed, preferred_element_type=jnp.float32
    ).astype(jnp.bfloat16)
    summed = reduce_seq(weight_part.reshape(2, n_seq, col_block, feats))
    grad_key_weight = summed[0].T
    grad_value_weight = summed[1].T
    return (attention, grad_normed, grad_q, grad_key_weight, grad_value_weight)


def solution(mesh):
    n_seq, n_uly = mesh.shape["seq"], mesh.shape["uly"]
    rows = 4
    fine = jax.sharding.Mesh(
        mesh.devices.reshape(n_seq // (2 * rows), rows, 2, n_uly), ("level", "row", "core", "uly")
    )
    return jax.shard_map(
        body,
        mesh=fine,
        in_specs=(
            P(SEQ, "uly"),
            P(SEQ, "uly"),
            P("uly", SEQ),
            P("uly", SEQ),
            P(),
            P(),
            P(),
            P(SEQ, "uly"),
        ),
        out_specs=(
            P(SEQ, "uly"),
            P(SEQ, "uly"),
            P(SEQ, "uly"),
            P("uly", SEQ),
            P("uly", SEQ),
        ),
        check_vma=False,
    )
```

```python
import functools

import jax
import jax.numpy as jnp
from jax import lax
from jax.experimental import pallas as pl
from jax.experimental.pallas import tpu as pltpu
from jax.sharding import PartitionSpec as P

HD = 128
WINDOW = 1024


epsilon = 1e-06
query_scale = 168.0 ** (-0.5)


def from_behind(array, axis, by):
    devices = lax.axis_size(axis)
    pairs = [(i, i + by) for i in range(devices) if 0 <= i + by < devices]
    return lax.ppermute(array, axis, pairs)


def normalize(raw_vals, gain, factor):
    mean_sq = jnp.mean(raw_vals * raw_vals, axis=-1, keepdims=True)
    return raw_vals * lax.rsqrt(mean_sq + epsilon) * gain * factor


def exchange(blocks, axis):
    return lax.all_to_all(blocks, axis, 0, 0)


def gather_all(block, axis):
    count = lax.axis_size(axis)
    return exchange(jnp.broadcast_to(block[None], (count,) + block.shape), axis)


SEQ = ("level", "row", "core")
CHIP = ("level", "row")
SWAP = [(0, 1), (1, 0)]


def gather_kernel(levels, rows, x_ref, out_ref, local_sem, z_send, z_recv, x_send, x_recv, f_send, f_recv):
    level = lax.axis_index("level")
    row = lax.axis_index("row")
    core = lax.axis_index("core")
    uly = lax.axis_index("uly")
    other = 1 - core
    mesh_ids = pl.DeviceIdType.MESH

    def slot(at_level, at_row):
        return (lax.rem(at_level, levels) * rows + lax.rem(at_row, rows)) * 2 + core

    def window(index):
        return out_ref.at[:, pl.ds(index, 1)]

    def to_partner(index, dx, dz):
        return pltpu.make_async_remote_copy(
            src_ref=window(index),
            dst_ref=window(index),
            send_sem=f_send.at[dx, dz],
            recv_sem=f_recv.at[dx, dz],
            device_id=(level, row, other, uly),
            device_id_type=mesh_ids,
        )

    barrier = pltpu.get_barrier_semaphore()
    for dz in range(1, levels):
        peer = (lax.rem(level + dz, levels), row, core, uly)
        pl.semaphore_signal(barrier, 1, device_id=peer, device_id_type=mesh_ids)
    for dx in range(1, rows):
        peer = (level, lax.rem(row + dx, rows), core, uly)
        pl.semaphore_signal(barrier, 1, device_id=peer, device_id_type=mesh_ids)
    pl.semaphore_signal(barrier, 1, device_id=(level, row, other, uly), device_id_type=mesh_ids)
    pl.semaphore_wait(barrier, levels + rows - 1)
    mine = slot(level, row)
    local = pltpu.make_async_copy(x_ref, window(mine), local_sem)
    local.start()
    z_copies = {}
    for dz in range(1, levels):
        z_copies[dz] = pltpu.make_async_remote_copy(
            src_ref=x_ref,
            dst_ref=window(mine),
            send_sem=z_send.at[dz],
            recv_sem=z_recv.at[dz],
            device_id=(lax.rem(level + dz, levels), row, core, uly),
            device_id_type=mesh_ids,
        )
        z_copies[dz].start()
    local.wait()
    x_moves = {}
    forwards = []

    def spread(dz, index):
        for dx in range(1, rows):
            move = pltpu.make_async_remote_copy(
                src_ref=window(index),
                dst_ref=window(index),
                send_sem=x_send.at[dx, dz],
                recv_sem=x_recv.at[dx, dz],
                device_id=(level, lax.rem(row + dx, rows), core, uly),
                device_id_type=mesh_ids,
            )
            move.start()
            x_moves[dx, dz] = move
        forward = to_partner(index, 0, dz)
        forward.start()
        forwards.append(forward)

    spread(0, mine)
    for dz in range(1, levels):
        z_copies[dz].wait_recv()
        spread(dz, slot(level + levels - dz, row))
    for dx in range(1, rows):
        for dz in range(levels):
            x_moves[dx, dz].wait_recv()
            forward = to_partner(slot(level + levels - dz, row + rows - dx), dx, dz)
            forward.start()
            forwards.append(forward)
    for dz in range(1, levels):
        z_copies[dz].wait_send()
    for move in x_moves.values():
        move.wait_send()
    for forward in forwards:
        forward.wait()


def gather_seq(block):
    levels = lax.axis_size("level")
    rows = lax.axis_size("row")
    spec = pl.BlockSpec(memory_space=pltpu.VMEM)
    return pl.pallas_call(
        functools.partial(gather_kernel, levels, rows),
        out_shape=jax.ShapeDtypeStruct((block.shape[0], 2 * levels * rows) + block.shape[1:], block.dtype),
        in_specs=[spec],
        out_specs=spec,
        scratch_shapes=[
            pltpu.SemaphoreType.DMA(()),
            pltpu.SemaphoreType.DMA((levels,)),
            pltpu.SemaphoreType.DMA((levels,)),
            pltpu.SemaphoreType.DMA((rows, levels)),
            pltpu.SemaphoreType.DMA((rows, levels)),
            pltpu.SemaphoreType.DMA((rows, levels)),
            pltpu.SemaphoreType.DMA((rows, levels)),
        ],
        compiler_params=pltpu.CompilerParams(collective_id=0, has_side_effects=True),
    )(block[:, None])


def reduce_seq(blocks):
    chips = blocks.shape[1] // 2
    split = blocks.reshape((blocks.shape[0], chips, 2) + blocks.shape[2:])
    core = lax.axis_index("core")
    keep = jnp.take(split, core, axis=2)
    send = jnp.take(split, 1 - core, axis=2)
    pair = (keep.astype(jnp.float32) + lax.ppermute(send, "core", SWAP).astype(jnp.float32))
    pair = pair.astype(jnp.bfloat16).transpose(1, 0, 2, 3)
    levels = lax.axis_size("level")
    by_row = pair.reshape((levels, chips // levels) + pair.shape[1:]).transpose(1, 0, 2, 3, 4)
    part = jnp.sum(exchange(by_row, "row").astype(jnp.float32), axis=0)
    return jnp.sum(exchange(part.astype(jnp.bfloat16), "level").astype(jnp.float32), axis=0)


def attend_block(
    queries, key_block, value_block, grad_block, query_pos, key_pos, query_seg, key_seg
):
    scores = jnp.einsum("bhge,lhe->hgbl", queries, key_block, preferred_element_type=jnp.float32)
    allowed = (
        (key_pos[None, :] <= query_pos[:, None])
        & (key_pos[None, :] > query_pos[:, None] - WINDOW)
        & (key_seg[None, :] == query_seg[:, None])
    )
    exp_scores = jnp.where(allowed[None, None], jnp.exp(scores), 0.0)
    probs = exp_scores / jnp.sum(exp_scores, axis=-1, keepdims=True)
    weights = probs.astype(jnp.bfloat16)
    attended = jnp.einsum(
        "hgbl,lhe->bhge", weights, value_block, preferred_element_type=jnp.float32
    ).astype(jnp.bfloat16)
    dprob = jnp.einsum(
        "bhge,lhe->hgbl", grad_block, value_block, preferred_element_type=jnp.float32
    )
    delta_row = jnp.sum(probs * dprob, axis=-1, keepdims=True)
    dscore = (probs * (dprob - delta_row)).astype(jnp.bfloat16)
    dquery = jnp.einsum("hgbl,lhe->bhge", dscore, key_block, preferred_element_type=jnp.float32)
    dkey = jnp.einsum("hgbl,bhge->lhe", dscore, queries, preferred_element_type=jnp.float32)
    dvalue = jnp.einsum("hgbl,bhge->lhe", weights, grad_block, preferred_element_type=jnp.float32)
    return (attended, dquery, dkey, dvalue)


def attention_kernel(pos_ref, gain_ref, q_ref, do_ref, k_ref, v_ref, out_ref, dq_ref, dkv_ref):
    rows = q_ref.shape[0]
    block = 512
    span = block + WINDOW
    dkv_ref[...] = jnp.zeros(dkv_ref.shape, jnp.float32)
    nt = (((1,), (1,)), ((), ()))
    tn = (((0,), (0,)), ((), ()))
    for b in range(rows // block):
        r0 = b * block
        k = k_ref[pl.ds(r0, span), :]
        v = v_ref[pl.ds(r0, span), :]
        row = lax.broadcasted_iota(jnp.int32, (block, span), 0)
        col = lax.broadcasted_iota(jnp.int32, (block, span), 1)
        query_pos = pos_ref[0] + r0 + row
        key_pos = pos_ref[0] - WINDOW + r0 + col
        allowed = (col <= row + WINDOW) & (col > row) & (key_pos >= 0)
        allowed = allowed & ((key_pos < pos_ref[1]) == (query_pos < pos_ref[1]))
        dk_acc = jnp.zeros((span, HD), jnp.float32)
        dv_acc = jnp.zeros((span, HD), jnp.float32)
        for g in range(2):
            raw = q_ref[pl.ds(r0, block), pl.ds(g * HD, HD)].astype(jnp.float32)
            mean_sq = jnp.mean(raw * raw, axis=1, keepdims=True)
            q = (raw * lax.rsqrt(mean_sq + epsilon) * gain_ref[...] * query_scale).astype(jnp.bfloat16)
            do = do_ref[pl.ds(r0, block), pl.ds(g * HD, HD)]
            scores = lax.dot_general(q, k, nt, preferred_element_type=jnp.float32)
            exp_scores = jnp.where(allowed, jnp.exp(scores), 0.0)
            probs = exp_scores / jnp.sum(exp_scores, axis=1, keepdims=True)
            weights = probs.astype(jnp.bfloat16)
            out_ref[pl.ds(r0, block), pl.ds(g * HD, HD)] = jnp.dot(
                weights, v, preferred_element_type=jnp.float32
            ).astype(out_ref.dtype)
            dprob = lax.dot_general(do, v, nt, preferred_element_type=jnp.float32)
            delta_row = jnp.sum(probs * dprob, axis=1, keepdims=True)
            dscore = (probs * (dprob - delta_row)).astype(jnp.bfloat16)
            dq_ref[pl.ds(r0, block), pl.ds(g * HD, HD)] = jnp.dot(
                dscore, k, preferred_element_type=jnp.float32
            )
            dk_acc = dk_acc + lax.dot_general(dscore, q, tn, preferred_element_type=jnp.float32)
            dv_acc = dv_acc + lax.dot_general(weights, do, tn, preferred_element_type=jnp.float32)
        dkv_ref[0, pl.ds(r0, span), :] += dk_acc
        dkv_ref[1, pl.ds(r0, span), :] += dv_acc


def attend(positions, gain, q_raw, grad_out, keys, values):
    rows = q_raw.shape[0]
    spec = pl.BlockSpec(memory_space=pltpu.VMEM)
    return pl.pallas_call(
        attention_kernel,
        out_shape=(
            jax.ShapeDtypeStruct((rows, 2 * HD), jnp.bfloat16),
            jax.ShapeDtypeStruct((rows, 2 * HD), jnp.float32),
            jax.ShapeDtypeStruct((2, keys.shape[0], HD), jnp.float32),
        ),
        in_specs=[pl.BlockSpec(memory_space=pltpu.SMEM)] + [spec] * 5,
        out_specs=(spec, spec, spec),
        cost_estimate=pl.CostEstimate(
            flops=12 * rows * (rows + WINDOW) * HD * 2, transcendentals=2 * rows * (rows + WINDOW),
            bytes_accessed=16 * rows * HD * 4,
        ),
    )(positions, gain, q_raw, grad_out, keys, values)


def body(normed, q_raw, key_weight, value_weight, q_gain, k_gain, segment_ids, grad_out):
    rows_here = normed.shape[0]
    feats = normed.shape[1]
    heads_here = q_raw.shape[1] // (2 * HD)
    n_seq = lax.axis_size(SEQ)
    n_uly = lax.axis_size("uly")
    col_block = key_weight.shape[1]
    seq_index = lax.axis_index(SEQ)
    base_row = seq_index * rows_here
    pair_t = jnp.stack([key_weight.T, value_weight.T])
    weight_t = gather_seq(pair_t).reshape(2, n_seq * col_block, feats)
    terms = lax.dot_general(
        normed, weight_t, (((1,), (2,)), ((), ())), preferred_element_type=jnp.float32
    ).astype(jnp.bfloat16)
    terms = terms.reshape(rows_here, 2, n_uly, heads_here * HD).transpose(2, 0, 1, 3)
    received = exchange(terms, "uly")
    raw_pair = jnp.sum(received.astype(jnp.float32), axis=0)
    key_raw = raw_pair[:, 0]
    value_raw = raw_pair[:, 1]
    key_in = key_raw.reshape(rows_here, heads_here, HD)
    keys_bf = normalize(key_in, k_gain, 1.0).astype(jnp.bfloat16)
    values_bf = value_raw.reshape(rows_here, heads_here, HD).astype(jnp.bfloat16)
    query_in = q_raw.astype(jnp.float32).reshape(rows_here, heads_here, 2, HD)
    queries = normalize(query_in, q_gain, query_scale).astype(jnp.bfloat16)
    grad_heads = grad_out.reshape(rows_here, heads_here, 2, HD)
    stacked = jnp.stack([keys_bf, values_bf])
    behind = from_behind(stacked, SEQ, 1)
    extended = jnp.concatenate([behind, stacked], axis=1).reshape(2, WINDOW + rows_here, HD)
    boundary = jnp.sum((segment_ids == 0).astype(jnp.int32))
    positions = jnp.stack([base_row.astype(jnp.int32), boundary])
    attention, dquery, grad_acc = attend(
        positions,
        q_gain.reshape(1, HD),
        q_raw,
        grad_out,
        extended[0],
        extended[1],
    )
    dquery = dquery.reshape(rows_here, heads_here, 2, HD)
    grad_acc = grad_acc.reshape(2, WINDOW + rows_here, heads_here, HD)
    own_grads = grad_acc[:, WINDOW:]
    offset_row = 0
    distance = 1
    first_row = max(0, distance * rows_here - WINDOW)
    piece_rows = rows_here - first_row
    outgoing = grad_acc[:, offset_row : offset_row + piece_rows]
    returned = from_behind(outgoing.astype(jnp.bfloat16), SEQ, -distance).astype(outgoing.dtype)
    own_grads = own_grads.at[:, first_row:].add(returned)
    _, pull_query = jax.vjp(lambda raw_vals: normalize(raw_vals, q_gain, query_scale), query_in)
    grad_q = pull_query(dquery)[0].astype(jnp.bfloat16).reshape(rows_here, 2 * heads_here * HD)
    _, pull_key = jax.vjp(lambda raw_vals: normalize(raw_vals, k_gain, 1.0), key_in)
    key_grad = pull_key(own_grads[0])[0].astype(jnp.bfloat16).reshape(rows_here, heads_here * HD)
    value_grad = own_grads[1].astype(jnp.bfloat16).reshape(rows_here, heads_here * HD)
    grads_all = gather_all(jnp.stack([key_grad, value_grad], axis=1), "uly")
    weight_heads = weight_t.reshape(2, n_uly, heads_here * HD, feats)
    grad_normed = jnp.einsum(
        "htkc,khcf->tf", grads_all, weight_heads, preferred_element_type=jnp.float32
    ).astype(jnp.bfloat16)
    weight_part = jnp.einsum(
        "htkc,tf->khcf", grads_all, normed, preferred_element_type=jnp.float32
    ).astype(jnp.bfloat16)
    summed = reduce_seq(weight_part.reshape(2, n_seq, col_block, feats))
    grad_key_weight = summed[0].T
    grad_value_weight = summed[1].T
    return (attention, grad_normed, grad_q, grad_key_weight, grad_value_weight)


def solution(mesh):
    n_seq, n_uly = mesh.shape["seq"], mesh.shape["uly"]
    rows = 4
    fine = jax.sharding.Mesh(
        mesh.devices.reshape(n_seq // (2 * rows), rows, 2, n_uly), ("level", "row", "core", "uly")
    )
    return jax.shard_map(
        body,
        mesh=fine,
        in_specs=(
            P(SEQ, "uly"),
            P(SEQ, "uly"),
            P("uly", SEQ),
            P("uly", SEQ),
            P(),
            P(),
            P(),
            P(SEQ, "uly"),
        ),
        out_specs=(
            P(SEQ, "uly"),
            P(SEQ, "uly"),
            P(SEQ, "uly"),
            P("uly", SEQ),
            P("uly", SEQ),
        ),
        check_vma=False,
    )
```
